32 devices in a mesh: dp: 8 (over y, x, core), tensor: 4 (over z).
Axes of the slice: x: 2, y: 2, z: 4, core: 2. Of those that a mesh axis runs over, the one named last changes fastest.
Arguments:
- tokens: bfloat16 [37888, 768], P(('dp', 'tensor')), may hold values from -6 to 6
- lengths: int32 [64], P('dp'), may hold values from 297 to 592, as said below
- cotangent: bfloat16 [37888, 768], P(('dp', 'tensor')), may hold values from -6 to 6
- ln1_gain: float32 [768], replicated, may hold values from 0.5 to 1.5
- ln1_bias: float32 [768], replicated, may hold values from -2 to 2
- w_qkv: bfloat16 [3, 768, 768], P(None, None, 'tensor'), may hold values from -0.21875 to 0.21875
- b_qv: float32 [2, 768], P(None, 'tensor'), may hold values from -3 to 3
- w_out: bfloat16 [768, 768], P('tensor'), may hold values from -0.875 to 0.875
- b_out: float32 [768], replicated, may hold values from -2 to 2
- ln2_gain: float32 [768], replicated, may hold values from 0.5 to 1.5
- ln2_bias: float32 [768], replicated, may hold values from -2 to 2
- w_up: bfloat16 [768, 3072], P(None, 'tensor'), may hold values from -0.21875 to 0.21875
- b_up: float32 [3072], P('tensor'), may hold values from -3 to 3
- w_down: bfloat16 [3072, 768], P('tensor'), may hold values from -0.109375 to 0.109375
- b_down: float32 [768], replicated, may hold values from -2 to 2
Outputs:
- block_output: bfloat16 [37888, 768], P(('dp', 'tensor'))
- input_grad: bfloat16 [37888, 768], P(('dp', 'tensor'))
- grad_ln1_gain: float32 [768], P(('dp', 'tensor'))
- grad_ln1_bias: float32 [768], P(('dp', 'tensor'))
- grad_w_qkv: float32 [3, 768, 768], P(None, 'dp', 'tensor')
- grad_b_qv: float32 [2, 768], P(None, ('tensor', 'dp'))
- grad_w_out: float32 [768, 768], P('tensor', 'dp')
- grad_b_out: float32 [768], P(('dp', 'tensor'))
- grad_ln2_gain: float32 [768], P(('dp', 'tensor'))
- grad_ln2_bias: float32 [768], P(('dp', 'tensor'))
- grad_w_up: float32 [768, 3072], P('dp', 'tensor')
- grad_b_up: float32 [3072], P(('tensor', 'dp'))
- grad_w_down: float32 [3072, 768], P('tensor', 'dp')
- grad_b_down: float32 [768], P(('dp', 'tensor'))
The draws below stay inside these ranges and needn't reach their ends.
Inputs may be any that keep to these rules, and one draw needn't show every extreme that they name: `lengths`: one length a sequence, in sequence order; the first sequence has length 592.
All inputs are finite; a program needn't handle non-finite values.
Results may differ from the reference program's by a relative error of at most 0.022.
Values may be sent and summed in bfloat16 or wider, within the bound.
No kernel may reach another device: no remote copies, remote signals or barrier semaphores. Data moves between devices by JAX's collectives and lax.ppermute only.
A program may use at most 192 MiB of HBM per device.

```python
import jax
import jax.numpy as jnp
from jax import lax

D = 768
HEADS = 12
HD = 64
FF = 3072
SEQ_LEN = 592
SEQS = 64
TOKENS = 37888


def draw_lengths(key, part):
    camera = jax.random.randint(jax.random.fold_in(key, 11), (SEQS,), 0, 2)
    short_len = SEQ_LEN * 9 // 16 - jax.random.randint(jax.random.fold_in(key, 12), (SEQS,), 0, SEQ_LEN // 16)
    long_len = SEQ_LEN - jax.random.randint(jax.random.fold_in(key, 13), (SEQS,), 0, SEQ_LEN // 32 + 1)
    result = jnp.where(camera == 1, long_len, short_len)
    result = result.at[0].set(SEQ_LEN)
    return result.astype(jnp.int32)


def with_spikes(drawn, rng, source, target, parts, factor):
    def block_of(position):
        return (jnp.arange(drawn.shape[position]) // (drawn.shape[position] // parts)).reshape((-1,) + (1,) * (drawn.ndim - 1 - position))

    first = jax.random.permutation(rng, parts)[block_of(target)]
    far = (block_of(target) + parts // 2) % parts
    return jnp.where((block_of(source) == first) | (block_of(source) == far), factor * drawn, drawn)


def block_levels(own_key, extent, cuts, least, high):
    def one(position, parts):
        heights = jax.random.uniform(jax.random.fold_in(jax.random.fold_in(own_key, 6), position), (parts,), jnp.float32, least / len(cuts), high / len(cuts))
        return jnp.repeat(jnp.exp(heights), extent[position] // parts).reshape((-1,) + (1,) * (len(extent) - position - 1))

    level = one(*cuts[0])
    for cut in cuts[1:]:
        level = level * one(*cut)
    return level


def gaussian(rng, shape, scale, most, cuts=(), held_as=jnp.bfloat16):
    entries = jax.random.normal(rng, shape, jnp.float32) * scale
    if len(cuts) > 0:
        entries = block_levels(rng, shape, cuts, -0.22, 0.18) * entries
    return jnp.clip(entries, min=-most, max=most).astype(held_as)


def gaussian_with(rng, dims, spread, reach, shards, heavy, kind=jnp.bfloat16):
    drawn = spread * jax.random.normal(rng, dims, jnp.float32)
    if shards:
        drawn = drawn * block_levels(rng, dims, shards, -0.22, 0.18)
    return jnp.clip(with_spikes(drawn, jax.random.fold_in(rng, 3), *heavy), -reach, reach).astype(kind)


def setup_inputs(seed: int = 0) -> dict:
    splits = jax.random.split(jax.random.key(seed), 16)
    return {
        "tokens": gaussian(splits[0], (TOKENS, D), 1.0, 6.0, ((0, 32),)),
        "lengths": draw_lengths(jax.random.fold_in(splits[15], 71), 0),
        "cotangent": gaussian_with(splits[2], (TOKENS, D), 1.0, 6.0, ((0, 32),), (0, 1, 32, 2.75)),
        "ln1_gain": jnp.clip(1.0 + 0.1 * jax.random.normal(splits[3], (D,), jnp.float32), 0.5, 1.5),
        "ln1_bias": gaussian(splits[4], (D,), 0.3, 2.0, (), jnp.float32),
        "w_qkv": gaussian(splits[5], (3, D, D), D ** -0.5, 0.21875, ((2, 4),)),
        "b_qv": gaussian(splits[6], (2, D), 0.5, 3.0, ((1, 4),), jnp.float32),
        "w_out": gaussian(splits[7], (D, D), (D // 16) ** -0.5, 0.875, ((0, 4),)),
        "b_out": gaussian(splits[8], (D,), 0.3, 2.0, (), jnp.float32),
        "ln2_gain": jnp.clip(1.0 + 0.1 * jax.random.normal(splits[9], (D,), jnp.float32), 0.5, 1.5),
        "ln2_bias": gaussian(splits[10], (D,), 0.3, 2.0, (), jnp.float32),
        "w_up": gaussian(splits[11], (D, FF), D ** -0.5, 0.21875, ((1, 4),)),
        "b_up": gaussian(splits[12], (FF,), 0.5, 3.0, ((0, 4),), jnp.float32),
        "w_down": gaussian(splits[13], (FF, D), FF ** -0.5, 0.109375, ((0, 4),)),
        "b_down": gaussian(splits[14], (D,), 0.3, 2.0, (), jnp.float32),
    }


HIGH = lax.Precision.HIGHEST

@jax.custom_vjp
def low(v):
    return lax.optimization_barrier(v.astype(jnp.bfloat16)).astype(jnp.float32)

@jax.custom_vjp
def low_back(v):
    return v

def low_keep(v):
    return (low(v), None)

def low_pass(kept, grad):
    return (grad,)

def back_keep(v):
    return (v, None)

def back_low(kept, grad):
    return (low(grad),)
low.defvjp(low_keep, low_pass)
low_back.defvjp(back_keep, back_low)

def layer_norm(values, gain, shift):
    center = values - lax.optimization_barrier(jnp.mean(values, axis=-1, keepdims=True))
    inverse = lax.rsqrt(lax.optimization_barrier(jnp.mean(center * center, axis=-1, keepdims=True)) + 1e-06)
    return center * inverse * gain + shift

def attend(pieces):
    query, keys, values, length = pieces
    scores = low_back(jnp.einsum('qhd,khd->hqk', query, keys, precision=HIGH) * HD ** (-0.5))
    live = jnp.arange(keys.shape[0], dtype=jnp.int32) < length
    scores = jnp.where(live[None, None, :], scores, -1e+30)
    probs = low(jax.nn.softmax(scores, axis=-1))
    return jnp.einsum('hqk,khd->qhd', probs, values, precision=HIGH)

def block(tokens_in, ln1_gain, ln1_bias, w_qkv, b_qv, w_out, b_out, ln2_gain, ln2_bias, w_up, b_up, w_down, b_down, seq_lengths):
    row_count = tokens_in.shape[0]
    group = row_count // SEQ_LEN
    normed1 = low(layer_norm(tokens_in, ln1_gain, ln1_bias))
    query = low(low_back(jnp.dot(normed1, w_qkv[0], precision=HIGH) + b_qv[0]))
    keys = low(low_back(jnp.dot(normed1, w_qkv[1], precision=HIGH)))
    values = low(low_back(jnp.dot(normed1, w_qkv[2], precision=HIGH) + b_qv[1]))

    def split(matrix):
        return matrix.reshape(group, SEQ_LEN, HEADS, HD)
    mixed = lax.map(jax.checkpoint(attend), (split(query), split(keys), split(values), seq_lengths))
    mixed = low(low_back(mixed.reshape(row_count, D)))
    middle = tokens_in + low_back(jnp.dot(mixed, w_out, precision=HIGH)) + b_out
    normed2 = low(layer_norm(middle, ln2_gain, ln2_bias))
    preact = low_back(jnp.dot(normed2, w_up, precision=HIGH) + b_up)
    hidden = low(jax.nn.gelu(preact, approximate=True))
    return middle + low_back(jnp.dot(hidden, w_down, precision=HIGH)) + b_down

def reference(tokens, lengths, cotangent, ln1_gain, ln1_bias, w_qkv, b_qv, w_out, b_out, ln2_gain, ln2_bias, w_up, b_up, w_down, b_down):
    params = tuple((p.astype(jnp.float32) for p in (ln1_gain, ln1_bias, w_qkv, b_qv, w_out, b_out, ln2_gain, ln2_bias, w_up, b_up, w_down, b_down)))
    group = 4
    count = SEQS // group
    inputs = tokens.astype(jnp.float32).reshape(count, group * SEQ_LEN, D)
    grads_in = cotangent.astype(jnp.float32).reshape(count, group * SEQ_LEN, D)
    seq_lengths = lengths.reshape(count, group)

    def step(totals, pieces):
        rows_in, grad_rows, lens_here = pieces

        def forward(values, *weights):
            return block(values, *weights, lens_here)
        result, pull = jax.vjp(forward, rows_in, *params)
        grads = pull(grad_rows)
        totals = tuple((a + b for a, b in zip(totals, grads[1:])))
        return (totals, (result.astype(jnp.bfloat16), grads[0].astype(jnp.bfloat16)))
    start = tuple((jnp.zeros_like(p) for p in params))
    totals, (outputs, input_grads) = lax.scan(step, start, (inputs, grads_in, seq_lengths))
    return (outputs.reshape(TOKENS, D), input_grads.reshape(TOKENS, D), totals[0], totals[1], totals[2], totals[3], totals[4], totals[5], totals[6], totals[7], totals[8], totals[9], totals[10], totals[11])
```

```python
import functools

import jax
import jax.numpy as jnp
from jax import lax
from jax.experimental import pallas as pl
from jax.experimental.pallas import tpu as pltpu
from jax.sharding import PartitionSpec as P

HD = 64
SEQ_LEN = 592
SCALE = HD**-0.5
EPSILON = 1e-06
MASKED = -1e30
LOW = jnp.bfloat16
WIDE = jnp.float32
VMEM_BYTES = 60 << 20
NT = (((1,), (1,)), ((), ()))
TN = (((0,), (0,)), ((), ()))


def product(left, right, dims=(((1,), (0,)), ((), ()))):
    return lax.dot_general(left, right, dims, preferred_element_type=WIDE)


def head_slots(heads):
    return [(128 * (h // 2), h % 2) for h in range(heads)]


def tile_of(ref, first):
    width = ref.shape[1]
    if first + 128 <= width:
        return ref[:, first : first + 128]
    part = ref[:, first:width]
    return jnp.concatenate([part, jnp.zeros((part.shape[0], 128 - part.shape[1]), part.dtype)], axis=1)


def three_parts(value):
    first = value.astype(LOW).astype(WIDE)
    rest = value - first
    second = rest.astype(LOW).astype(WIDE)
    return first, second, rest - second


def attend_kernel(heads, length_ref, q_ref, k_ref, v_ref, mixed_ref, log_ref):
    live = length_ref[pl.program_id(1)]
    lane = lax.broadcasted_iota(jnp.int32, (1, 128), 1)
    row = lax.broadcasted_iota(jnp.int32, (SEQ_LEN, 1), 0)
    side = lax.broadcasted_iota(jnp.int32, (128, 1), 0)
    bias = jnp.where(row < live, 0.0, MASKED).astype(LOW)
    width = q_ref.shape[1]
    results = {}
    for head, (first, upper) in enumerate(head_slots(heads)):
        own = (lane >= 64) if upper else (lane < 64)
        spare = 0 if upper else 64
        query = tile_of(q_ref, first) * jnp.asarray(SCALE, LOW)
        keys, values = tile_of(k_ref, first), tile_of(v_ref, first)
        zero, one = jnp.zeros_like(query), jnp.ones_like(query)
        query = jnp.where(own, query, jnp.where(lane == spare, one, zero))
        keys = jnp.where(own, keys, jnp.where(lane == spare, bias, zero))
        values = jnp.where(own, values, jnp.where(lane == spare, one, zero))
        scores = product(keys, query, NT)
        highest = jnp.max(scores, axis=0, keepdims=True)
        weights = jnp.exp(scores - highest).astype(LOW)
        summed = product(values, weights, TN)
        total = summed[spare : spare + 1, :]
        log_ref[head : head + 1, :] = highest + jnp.log(total)
        results.setdefault(first, []).append(summed * (1.0 / total))
    for first, pair in results.items():
        both = jnp.where(side < 64, pair[0], pair[1]) if len(pair) == 2 else pair[0]
        stored = both.astype(LOW).T
        upto = min(128, width - first)
        mixed_ref[:, first : first + upto] = stored[:, :upto]


def attend_back_kernel(heads, length_ref, q_ref, k_ref, v_ref, mixed_ref, gm_ref, log_ref, gq_ref, gk_ref, gv_ref):
    live = length_ref[pl.program_id(1)]
    lane = lax.broadcasted_iota(jnp.int32, (1, 128), 1)
    row = lax.broadcasted_iota(jnp.int32, (SEQ_LEN, 1), 0)
    bias = jnp.where(row < live, 0.0, MASKED).astype(LOW)
    width = q_ref.shape[1]
    totals = {}
    for head, (first, upper) in enumerate(head_slots(heads)):
        own = (lane >= 64) if upper else (lane < 64)
        spare = 0 if upper else 64
        query = tile_of(q_ref, first) * jnp.asarray(SCALE, LOW)
        keys, values = tile_of(k_ref, first), tile_of(v_ref, first)
        grad = tile_of(gm_ref, first)
        zero, one = jnp.zeros_like(query), jnp.ones_like(query)
        grad = jnp.where(own, grad, zero)
        wide_grad = grad.astype(WIDE)
        inner = jnp.sum(wide_grad * tile_of(mixed_ref, first).astype(WIDE), axis=-1, keepdims=True)
        parts = three_parts(-inner)
        shifted = wide_grad
        for place in range(3):
            shifted = jnp.where(lane == spare + place, parts[place], shifted)
        masked_query = jnp.where(own, query, jnp.where(lane == spare, one, zero))
        masked_keys = jnp.where(own, keys, jnp.where(lane == spare, bias, zero))
        spread_values = jnp.where(own, values, jnp.where((lane >= spare) & (lane < spare + 3), one, zero))
        probs = jnp.exp(product(masked_keys, masked_query, NT) - log_ref[head : head + 1, :])
        centred = product(spread_values, shifted.astype(LOW), NT)
        grad_scores = (probs * centred).astype(LOW)
        parts = (
            product(jnp.where(own, keys, zero), grad_scores, TN),
            product(grad_scores, jnp.where(own, query, zero)),
            product(probs.astype(LOW), grad),
        )
        held = totals.get(first)
        totals[first] = parts if held is None else tuple(a + b for a, b in zip(held, parts))
    for first, (gq, gk, gv) in totals.items():
        upto = min(128, width - first)
        gq_ref[:, first : first + upto] = (gq * SCALE).astype(LOW).T[:, :upto]
        gk_ref[:, first : first + upto] = gk.astype(LOW)[:, :upto]
        gv_ref[:, first : first + upto] = gv.astype(LOW)[:, :upto]


def attention_specs(width, heads):
    rows = pl.BlockSpec((None, SEQ_LEN, width), lambda s, i, _: (s, i, 0))
    logs = pl.BlockSpec((None, None, heads, SEQ_LEN), lambda s, i, _: (s, i, 0, 0))
    return rows, logs


def attend(lengths, query, keys, values):
    shards, count, width = query.shape
    seqs, heads = count // SEQ_LEN, width // HD
    rows, logs = attention_specs(width, heads)
    pairs = shards * seqs * heads
    return pl.pallas_call(
        functools.partial(attend_kernel, heads),
        out_shape=(
            jax.ShapeDtypeStruct(query.shape, LOW),
            jax.ShapeDtypeStruct((shards, seqs, heads, SEQ_LEN), WIDE),
        ),
        grid_spec=pltpu.PrefetchScalarGridSpec(
            num_scalar_prefetch=1, grid=(shards, seqs), in_specs=[rows] * 3, out_specs=(rows, logs)
        ),
        compiler_params=pltpu.CompilerParams(vmem_limit_bytes=VMEM_BYTES),
        cost_estimate=pl.CostEstimate(
            flops=pairs * 16 * SEQ_LEN * SEQ_LEN * HD,
            bytes_accessed=4 * query.size * 2,
            transcendentals=pairs * SEQ_LEN * SEQ_LEN,
        ),
        name="attend",
    )(lengths, query, keys, values)


def attend_back(lengths, query, keys, values, mixed, grad_mixed, logs_in):
    shards, count, width = query.shape
    seqs, heads = count // SEQ_LEN, width // HD
    rows, logs = attention_specs(width, heads)
    pairs = shards * seqs * heads
    return pl.pallas_call(
        functools.partial(attend_back_kernel, heads),
        out_shape=(jax.ShapeDtypeStruct(query.shape, LOW),) * 3,
        grid_spec=pltpu.PrefetchScalarGridSpec(
            num_scalar_prefetch=1,
            grid=(shards, seqs),
            in_specs=[rows] * 5 + [logs],
            out_specs=(rows,) * 3,
        ),
        compiler_params=pltpu.CompilerParams(vmem_limit_bytes=VMEM_BYTES),
        cost_estimate=pl.CostEstimate(
            flops=pairs * 40 * SEQ_LEN * SEQ_LEN * HD,
            bytes_accessed=8 * query.size * 2,
            transcendentals=pairs * SEQ_LEN * SEQ_LEN,
        ),
        name="attend_back",
    )(lengths, query, keys, values, mixed, grad_mixed, logs_in)


def norm_parts(values):
    center = values - jnp.mean(values, axis=-1, keepdims=True)
    inverse = lax.rsqrt(jnp.mean(center * center, axis=-1, keepdims=True) + EPSILON)
    return (center * inverse, inverse)


def norm_back(grad_out, normed, inverse, gain):
    scaled = grad_out * gain
    return inverse * (
        scaled
        - jnp.mean(scaled, axis=-1, keepdims=True)
        - normed * jnp.mean(scaled * normed, axis=-1, keepdims=True)
    )


def gather_shards(shard, dp_size):
    rows, columns = shard.shape
    part = rows // dp_size
    own = lax.dynamic_slice_in_dim(shard, lax.axis_index("dp") * part, part, 0)
    parts = lax.all_gather(own, ("dp", "tensor"), axis=0)
    parts = parts.reshape(dp_size, -1, part, columns).transpose(1, 0, 2, 3)
    return parts.reshape(-1, rows, columns)


def reduce_shards(partial, dp_size):
    shards, rows, columns = partial.shape
    parts = partial.astype(LOW).reshape(shards, dp_size, rows // dp_size, columns).transpose(1, 0, 2, 3)
    parts = lax.psum_scatter(parts, "dp", scatter_dimension=0, tiled=True)[0]
    return lax.psum_scatter(parts, "tensor", scatter_dimension=0, tiled=True)[0].astype(WIDE)


def per_device(dp_size, tensor_size, tokens, lengths, cotangent, ln1_gain, ln1_bias, w_qkv, b_qv, w_out, b_out, ln2_gain, ln2_bias, w_up, b_up, w_down, b_down):
    count, depth = tokens.shape
    width = w_qkv.shape[2]
    seqs = count // SEQ_LEN
    own_lengths = lax.dynamic_slice_in_dim(lengths, lax.axis_index("tensor") * seqs, seqs, 0)
    attn_shard = jnp.concatenate([w_qkv.transpose(0, 2, 1).reshape(3 * width, depth), w_out], axis=0)
    attn = gather_shards(attn_shard, dp_size)
    up = gather_shards(w_up, dp_size)
    down = gather_shards(w_down, dp_size)
    qv_biases = lax.all_gather(b_qv, "tensor", axis=0)
    up_biases = lax.all_gather(b_up, "tensor", axis=0)

    tokens_in = tokens.astype(WIDE)
    normed1, inverse1 = norm_parts(tokens_in)
    h1 = (normed1 * ln1_gain + ln1_bias).astype(LOW)
    projected = jnp.einsum("rd,tcd->trc", h1, attn[:, : 3 * width], preferred_element_type=WIDE)
    query = (projected[:, :, :width] + qv_biases[:, None, 0]).astype(LOW)
    keys = projected[:, :, width : 2 * width].astype(LOW)
    values = (projected[:, :, 2 * width :] + qv_biases[:, None, 1]).astype(LOW)
    mixed, logs = attend(own_lengths, query, keys, values)
    out_weights = attn[:, 3 * width :]
    middle = tokens_in + jnp.einsum("trc,tcd->rd", mixed, out_weights, preferred_element_type=WIDE) + b_out
    normed2, inverse2 = norm_parts(middle)
    h2 = (normed2 * ln2_gain + ln2_bias).astype(LOW)
    preact = jnp.einsum("rd,tdf->trf", h2, up, preferred_element_type=WIDE) + up_biases[:, None]
    hidden, gelu_pull = jax.vjp(lambda u: jax.nn.gelu(u, approximate=True), preact)
    hidden = hidden.astype(LOW)
    block_output = (
        middle + jnp.einsum("trf,tfd->rd", hidden, down, preferred_element_type=WIDE) + b_down
    ).astype(LOW)

    grad_out = cotangent.astype(WIDE)
    grad_down = jnp.einsum("rd,trf->tdf", cotangent, hidden, preferred_element_type=WIDE)
    grad_hidden = jnp.einsum("rd,tfd->trf", cotangent, down, preferred_element_type=WIDE)
    grad_preact = gelu_pull(grad_hidden)[0].astype(LOW)
    grad_up = jnp.einsum("rd,trf->tdf", h2, grad_preact, preferred_element_type=WIDE)
    grad_up_bias = jnp.sum(grad_preact.astype(WIDE), axis=1)
    grad_down = reduce_shards(grad_down, dp_size)
    grad_up = reduce_shards(grad_up, dp_size)
    grad_h2 = jnp.einsum("trf,tdf->rd", grad_preact, up, preferred_element_type=WIDE)
    grad_middle = grad_out + norm_back(grad_h2, normed2, inverse2, ln2_gain)
    branch = grad_middle.astype(LOW)
    grad_out_proj = jnp.einsum("rd,trc->tdc", branch, mixed, preferred_element_type=WIDE)
    grad_mixed = jnp.einsum("rd,tcd->trc", branch, out_weights, preferred_element_type=WIDE).astype(LOW)
    grad_stack = jnp.concatenate(
        attend_back(own_lengths, query, keys, values, mixed, grad_mixed, logs), axis=2
    )
    grad_qkv = jnp.einsum("rd,trc->tdc", h1, grad_stack, preferred_element_type=WIDE)
    grad_attn = reduce_shards(jnp.concatenate([grad_qkv, grad_out_proj], axis=2), dp_size)
    grad_qv_bias = jnp.sum(grad_stack.astype(WIDE), axis=1)
    grad_h1 = jnp.einsum("trc,tcd->rd", grad_stack, attn[:, : 3 * width], preferred_element_type=WIDE)
    input_grad = (grad_middle + norm_back(grad_h1, normed1, inverse1, ln1_gain)).astype(LOW)

    vectors = jnp.stack(
        [
            jnp.sum(grad_h1 * normed1, axis=0),
            jnp.sum(grad_h1, axis=0),
            jnp.sum(grad_middle, axis=0),
            jnp.sum(grad_h2 * normed2, axis=0),
            jnp.sum(grad_h2, axis=0),
            jnp.sum(grad_out, axis=0),
        ]
    )
    vectors = lax.psum_scatter(vectors, ("dp", "tensor"), scatter_dimension=1, tiled=True)
    biases = jnp.concatenate([grad_qv_bias[:, :width], grad_qv_bias[:, 2 * width :], grad_up_bias], axis=1)
    biases = lax.psum_scatter(biases, "tensor", scatter_dimension=0, tiled=True)[0]
    biases = [
        lax.psum_scatter(biases[a:b], "dp", scatter_dimension=0, tiled=True)
        for a, b in ((0, width), (width, 2 * width), (2 * width, biases.shape[0]))
    ]
    part = depth // dp_size
    return (
        block_output,
        input_grad,
        vectors[0],
        vectors[1],
        grad_attn[:, : 3 * width].reshape(part, 3, width).transpose(1, 0, 2),
        jnp.stack(biases[:2]),
        grad_attn[:, 3 * width :].T,
        vectors[2],
        vectors[3],
        vectors[4],
        grad_up,
        biases[2],
        grad_down.T,
        vectors[5],
    )


def solution(mesh):
    in_specs = (
        P(("dp", "tensor"), None),
        P("dp"),
        P(("dp", "tensor"), None),
        P(),
        P(),
        P(None, None, "tensor"),
        P(None, "tensor"),
        P("tensor", None),
        P(),
        P(),
        P(),
        P(None, "tensor"),
        P("tensor"),
        P("tensor", None),
        P(),
    )
    out_specs = (
        P(("dp", "tensor"), None),
        P(("dp", "tensor"), None),
        P(("dp", "tensor")),
        P(("dp", "tensor")),
        P(None, "dp", "tensor"),
        P(None, ("tensor", "dp")),
        P("tensor", "dp"),
        P(("dp", "tensor")),
        P(("dp", "tensor")),
        P(("dp", "tensor")),
        P("dp", "tensor"),
        P(("tensor", "dp")),
        P("tensor", "dp"),
        P(("dp", "tensor")),
    )
    return jax.shard_map(
        functools.partial(per_device, mesh.shape["dp"], mesh.shape["tensor"]), mesh=mesh, in_specs=in_specs, out_specs=out_specs, check_vma=False
    )
```

```python
import functools

import jax
import jax.numpy as jnp
from jax import lax
from jax.experimental import pallas as pl
from jax.experimental.pallas import tpu as pltpu
from jax.sharding import PartitionSpec as P

HD = 64
SEQ_LEN = 592
SCALE = HD**-0.5
EPSILON = 1e-06
MASKED = -1e30
LOW = jnp.bfloat16
WIDE = jnp.float32
VMEM_BYTES = 60 << 20
HEADS = 3
NN = (((1,), (0,)), ((), ()))
NT = (((1,), (1,)), ((), ()))
TN = (((0,), (0,)), ((), ()))
PI_ROOT = (2.0 / 3.141592653589793) ** 0.5


def product(left, right, dims=NN):
    return lax.dot_general(left, right, dims, preferred_element_type=WIDE)


def three_parts(value):
    first = value.astype(LOW).astype(WIDE)
    rest = value - first
    second = rest.astype(LOW).astype(WIDE)
    return first, second, rest - second


def norm_parts(values):
    center = values - jnp.mean(values, axis=-1, keepdims=True)
    inverse = lax.rsqrt(jnp.mean(center * center, axis=-1, keepdims=True) + EPSILON)
    return center * inverse, inverse


def norm_back(grad, normed, inverse, gain):
    scaled = grad * gain
    return inverse * (
        scaled
        - jnp.mean(scaled, axis=-1, keepdims=True)
        - normed * jnp.mean(scaled * normed, axis=-1, keepdims=True)
    )


def call(kernel, name, outs, grid, in_specs, out_specs, scratch=(), scalars=0, flops=0, moved=0, aliases=None):
    return pl.pallas_call(
        kernel,
        out_shape=outs,
        grid_spec=pltpu.PrefetchScalarGridSpec(
            num_scalar_prefetch=scalars,
            grid=grid,
            in_specs=in_specs,
            out_specs=out_specs,
            scratch_shapes=list(scratch),
        ),
        compiler_params=pltpu.CompilerParams(vmem_limit_bytes=VMEM_BYTES),
        cost_estimate=pl.CostEstimate(flops=flops, bytes_accessed=moved, transcendentals=0),
        input_output_aliases=aliases or {},
        name=name,
    )


def whole(shape):
    zeros = (0,) * len(shape)
    return pl.BlockSpec(shape, lambda *_: zeros)


def kept(shape, dtype=LOW):
    return jax.ShapeDtypeStruct(shape, dtype)


ANYWHERE = pl.BlockSpec(memory_space=pl.ANY)


def pack_attention(w_qkv, w_out):
    depth = w_out.shape[1]
    width = w_qkv.shape[2]
    rows = w_qkv.transpose(0, 2, 1)
    return jnp.concatenate(
        [
            rows[:, :128].reshape(384, depth),
            rows[0, 128:],
            rows[1, 128:],
            rows[2, 128:],
            w_out[128:],
            w_out[:128],
        ],
        axis=0,
    )


def unpack_attention(grads):
    q01, k01, v01, q2, k2, v2, o2, o01 = (
        grads[:, a:b]
        for a, b in ((0, 128), (128, 256), (256, 384), (384, 448), (448, 512), (512, 576), (576, 640), (640, 768))
    )
    stacked = [jnp.concatenate(pair, axis=1) for pair in ((q01, q2), (k01, k2), (v01, v2), (o01, o2))]
    return jnp.stack(stacked[:3]), stacked[3].T


def load_pieces(place_ref, pieces, target, sems, part):
    copies = []
    for ref, offsets in pieces:
        for number, offset in enumerate(offsets):
            start = pl.multiple_of((place_ref[0] ^ offset) * part, part)
            source = ref.at[pl.ds(number * part, part), :]
            copies.append(
                pltpu.make_async_copy(source, target.at[pl.ds(start, part), :], sems.at[len(copies)])
            )
    return copies


def gelu_both(u):
    square = u * u
    t = jnp.tanh(PI_ROOT * u * (1.0 + 0.044715 * square))
    half = 0.5 * (1.0 + t)
    slope = half + (0.5 * PI_ROOT) * u * (1.0 - t * t) * (1.0 + (3 * 0.044715) * square)
    return u * half, slope


def prepare_kernel(x_ref, g_ref, gain_ref, bias_ref, out_bias_ref, h_ref, ht_ref, gt_ref, sum_ref, gsum_ref):
    x = x_ref[...].astype(WIDE)
    normed, _ = norm_parts(x)
    h = (normed * gain_ref[...] + bias_ref[...]).astype(LOW)
    h_ref[...] = h
    ht_ref[...] = h.T
    grad = g_ref[...]
    gt_ref[...] = grad.T
    gsum_ref[...] = jnp.sum(grad.astype(WIDE), axis=0, keepdims=True)
    sum_ref[...] = x + out_bias_ref[...]


def prepare(tokens, cotangent, gain, bias, out_bias):
    count, depth = tokens.shape
    outs = (
        kept((count, depth)),
        kept((depth, count)),
        kept((depth, count)),
        kept((count, depth), WIDE),
        kept((1, depth), WIDE),
    )
    return call(
        prepare_kernel,
        "prepare",
        outs,
        (1,),
        [whole((count, depth))] * 2 + [whole((1, depth))] * 3,
        [whole(o.shape) for o in outs],
        moved=count * depth * 14,
    )(tokens, cotangent, gain, bias, out_bias)


def middle_kernel(sum_ref, gain_ref, bias_ref, down_bias_ref, h_ref, ht_ref, out_ref):
    middle = sum_ref[...]
    normed, _ = norm_parts(middle)
    h = (normed * gain_ref[...] + bias_ref[...]).astype(LOW)
    h_ref[...] = h
    ht_ref[...] = h.T
    out_ref[...] = middle + down_bias_ref[...]


def middle_norm(total, gain, bias, down_bias):
    count, depth = total.shape
    outs = (kept((count, depth)), kept((depth, count)), kept((count, depth), WIDE))
    return call(
        middle_kernel,
        "middle_norm",
        outs,
        (1,),
        [whole((count, depth))] + [whole((1, depth))] * 3,
        [whole(o.shape) for o in outs],
        moved=count * depth * 12,
    )(total, gain, bias, down_bias)


def turn_kernel(e_ref, middle_ref, g_ref, gain_ref, grad_ref, branch_ref, branch_t_ref, sums_ref):
    grad_h = e_ref[...]
    normed, inverse = norm_parts(middle_ref[...])
    grad = g_ref[...].astype(WIDE) + norm_back(grad_h, normed, inverse, gain_ref[...])
    grad_ref[...] = grad
    branch = grad.astype(LOW)
    branch_ref[...] = branch
    branch_t_ref[...] = branch.T
    sums_ref[0:1, :] = jnp.sum(grad_h * normed, axis=0, keepdims=True)
    sums_ref[1:2, :] = jnp.sum(grad_h, axis=0, keepdims=True)
    sums_ref[2:3, :] = jnp.sum(grad, axis=0, keepdims=True)


def turn(grad_h2, middle, cotangent, gain):
    count, depth = middle.shape
    outs = (
        kept((count, depth), WIDE),
        kept((count, depth)),
        kept((depth, count)),
        kept((3, depth), WIDE),
    )
    return call(
        turn_kernel,
        "turn",
        outs,
        (1,),
        [whole((count, depth))] * 3 + [whole((1, depth))],
        [whole(o.shape) for o in outs],
        moved=count * depth * 18,
    )(grad_h2, middle, cotangent, gain)


def finish_kernel(e_ref, x_ref, grad_ref, gain_ref, out_ref, sums_ref):
    grad_h = e_ref[...]
    normed, inverse = norm_parts(x_ref[...].astype(WIDE))
    out_ref[...] = (grad_ref[...] + norm_back(grad_h, normed, inverse, gain_ref[...])).astype(LOW)
    first = jnp.sum(grad_h * normed, axis=0, keepdims=True)
    second = jnp.sum(grad_h, axis=0, keepdims=True)

    @pl.when(pl.program_id(0) == 0)
    def _():
        sums_ref[0:1, :] = first
        sums_ref[1:2, :] = second

    @pl.when(pl.program_id(0) > 0)
    def _():
        sums_ref[0:1, :] += first
        sums_ref[1:2, :] += second


def finish(grad_h1, tokens, grad_middle, gain):
    count, depth = tokens.shape
    rows = pl.BlockSpec((SEQ_LEN, depth), lambda i: (i, 0))
    return call(
        finish_kernel,
        "finish",
        (kept((count, depth)), kept((2, depth), WIDE)),
        (count // SEQ_LEN,),
        [rows] * 3 + [whole((1, depth))],
        [rows, whole((2, depth))],
        moved=count * depth * 12,
    )(grad_h1, tokens, grad_middle, gain)


def spare_lane(upper):
    return 0 if upper else 64


def attend_kernel(loaded, place_ref, live_ref, h_ref, total_ref, bias_ref, *refs):
    if loaded:
        near_ref, far_ref, proj_ref, mixed_ref, log_ref, out_ref, weights_ref, sems = refs

        @pl.when(pl.program_id(0) == 0)
        def _():
            pieces = ((near_ref, (0, 2, 4, 6)), (far_ref, (1, 3, 5, 7)))
            copies = load_pieces(place_ref, pieces, weights_ref, sems, weights_ref.shape[0] // 8)
            for copy in copies:
                copy.start()
            for copy in copies:
                copy.wait()
    else:
        weights_ref, proj_ref, mixed_ref, log_ref, out_ref = refs
    live = live_ref[pl.program_id(0)]
    h = h_ref[...]
    proj = (product(h, weights_ref[0:576, :], NT) + bias_ref[...]).astype(LOW)
    proj = jnp.concatenate([proj, jnp.zeros((SEQ_LEN, 64), LOW)], axis=1)
    proj_ref[...] = proj
    lane = lax.broadcasted_iota(jnp.int32, (1, 128), 1)
    row = lax.broadcasted_iota(jnp.int32, (SEQ_LEN, 1), 0)
    side = lax.broadcasted_iota(jnp.int32, (128, 1), 0)
    mask = jnp.where(row < live, 0.0, MASKED).astype(LOW)
    mixed = []
    for head in range(HEADS):
        upper = head == 1
        own = (lane >= 64) if upper else (lane < 64)
        spare = spare_lane(upper)
        query, keys, values = head_tiles(proj, head)
        query = query * jnp.asarray(SCALE, LOW)
        zero, one = jnp.zeros_like(query), jnp.ones_like(query)
        query = jnp.where(own, query, jnp.where(lane == spare, one, zero))
        keys = jnp.where(own, keys, jnp.where(lane == spare, mask, zero))
        values = jnp.where(own, values, jnp.where(lane == spare, one, zero))
        scores = product(keys, query, NT)
        highest = jnp.max(scores, axis=0, keepdims=True)
        weights = jnp.exp(scores - highest).astype(LOW)
        summed = product(values, weights, TN)
        spent = summed[spare : spare + 1, :]
        log_ref[head : head + 1, :] = highest + jnp.log(spent)
        mixed.append(summed * (1.0 / spent))
    first = jnp.where(side < 64, mixed[0], mixed[1]).astype(LOW).T
    third = jnp.where(side < 64, mixed[2], 0.0)
    third = jnp.concatenate([third[64:], third[:64]], axis=0).astype(LOW).T
    packed = jnp.concatenate([third, first], axis=1)
    mixed_ref[...] = packed
    out_ref[...] = total_ref[...] + product(packed, weights_ref[512:768, :])


def head_tiles(proj, head):
    if head < 2:
        return proj[:, 0:128], proj[:, 128:256], proj[:, 256:384]
    both = proj[:, 384:512]
    return both, jnp.concatenate([both[:, 64:], both[:, :64]], axis=1), proj[:, 512:640]


def attend(place, lengths, h, total, biases, weights):
    count, depth = h.shape
    seqs = count // SEQ_LEN
    loaded = len(weights) == 2
    rows = lambda width: pl.BlockSpec((SEQ_LEN, width), lambda i, *_: (i, 0))
    logs = pl.BlockSpec((None, HEADS, SEQ_LEN), lambda i, *_: (i, 0, 0))
    outs = [
        kept((count, 640)),
        kept((count, 256)),
        kept((seqs, HEADS, SEQ_LEN), WIDE),
        kept((count, depth), WIDE),
    ]
    out_specs = [rows(640), rows(256), logs, rows(depth)]
    scratch = []
    if loaded:
        outs.append(kept((768, depth)))
        out_specs.append(whole((768, depth)))
        scratch = [pltpu.SemaphoreType.DMA((8,))]
    return call(
        functools.partial(attend_kernel, loaded),
        "attend",
        outs,
        (seqs,),
        [rows(depth), rows(depth), whole((1, 576))] + ([ANYWHERE] * 2 if loaded else [whole((768, depth))]),
        out_specs,
        scratch,
        scalars=2,
        flops=count * depth * 768 * 2,
        moved=count * depth * 12,
        aliases={3: 3},
    )(place, lengths, h, total, biases, *weights)


def attend_back_kernel(relative, first, place_ref, live_ref, weights_ref, proj_ref, mixed_ref, log_ref, branch_ref, ht_ref, bt_ref, *refs):
    e_ref = None
    if not first:
        e_ref, refs = refs[0], refs[1:]
    if relative:
        out_ref, keep_ref, send_ref, sums_ref, held_ref, turned_ref = refs
    else:
        out_ref, keep_ref, sums_ref, held_ref, turned_ref = refs
        send_ref = None
    step = pl.program_id(0)
    count = held_ref.shape[0]
    seqs = count // SEQ_LEN

    @pl.when(step < seqs)
    def _():
        live = live_ref[jnp.minimum(step, seqs - 1)]
        lane = lax.broadcasted_iota(jnp.int32, (1, 128), 1)
        row = lax.broadcasted_iota(jnp.int32, (SEQ_LEN, 1), 0)
        mask = jnp.where(row < live, 0.0, MASKED).astype(LOW)
        proj = proj_ref[...]
        mixed = mixed_ref[...]
        grad_mixed = product(branch_ref[...], weights_ref[512:768, :], NT).astype(LOW)
        totals = []
        for head in range(HEADS):
            upper = head == 1
            own = (lane >= 64) if upper else (lane < 64)
            spare = spare_lane(upper)
            query, keys, values = head_tiles(proj, head)
            if head < 2:
                grad, held = grad_mixed[:, 128:256], mixed[:, 128:256]
            else:
                grad, held = (jnp.concatenate([m[:, 64:128], m[:, 0:64]], axis=1) for m in (grad_mixed, mixed))
            query = query * jnp.asarray(SCALE, LOW)
            zero, one = jnp.zeros_like(query), jnp.ones_like(query)
            grad = jnp.where(own, grad, zero)
            wide_grad = grad.astype(WIDE)
            inner = jnp.sum(wide_grad * held.astype(WIDE), axis=-1, keepdims=True)
            parts = three_parts(-inner)
            shifted = wide_grad
            for place in range(3):
                shifted = jnp.where(lane == spare + place, parts[place], shifted)
            masked_query = jnp.where(own, query, jnp.where(lane == spare, one, zero))
            masked_keys = jnp.where(own, keys, jnp.where(lane == spare, mask, zero))
            spread_values = jnp.where(own, values, jnp.where((lane >= spare) & (lane < spare + 3), one, zero))
            probs = jnp.exp(product(masked_keys, masked_query, NT) - log_ref[head : head + 1, :])
            centred = product(spread_values, shifted.astype(LOW), NT)
            grad_scores = (probs * centred).astype(LOW)
            parts = (
                (product(jnp.where(own, keys, zero), grad_scores, TN) * SCALE).astype(LOW).T,
                product(grad_scores, jnp.where(own, query, zero)).astype(LOW),
                product(probs.astype(LOW), grad).astype(LOW),
            )
            totals.append(parts)
        pair = [a + b for a, b in zip(totals[0], totals[1])]
        gq, gk, gv = totals[2]
        both = gq + jnp.concatenate([gk[:, 64:], gk[:, :64]], axis=1)
        packed = jnp.concatenate(pair + [both, gv], axis=1)
        start = pl.multiple_of(step * SEQ_LEN, 16)
        held_ref[pl.ds(start, SEQ_LEN), 0:640] = packed
        held_ref[pl.ds(start, SEQ_LEN), 640:896] = mixed
        term = product(packed, weights_ref[0:640, :])
        out_ref[...] = term if e_ref is None else e_ref[...] + term
        sums = jnp.sum(packed.astype(WIDE), axis=0, keepdims=True)

        @pl.when(step == 0)
        def _():
            sums_ref[...] = sums

        @pl.when(step > 0)
        def _():
            sums_ref[...] += sums

    @pl.when(step == seqs)
    def _():
        lane = lax.broadcasted_iota(jnp.int32, (1, 128), 1)
        grads = product(ht_ref[...], held_ref[:, 0:640])
        outs = product(bt_ref[...], held_ref[:, 640:896])
        full = jnp.concatenate([grads[:, :512], grads[:, 512:] + outs[:, :128], outs[:, 128:]], axis=1)
        scatter_rows(relative, place_ref, full.astype(LOW), turned_ref, keep_ref, send_ref, 0)


def scatter_rows(relative, place_ref, values, turned_ref, keep_ref, send_ref, column):
    width = values.shape[1]
    columns = slice(column, column + width)
    if not relative:
        keep_ref[:, columns] = values
        return
    part = values.shape[0] // 8
    for block in range(8):
        other = place_ref[0] ^ block
        start = ((other & 1) * 4 + (other >> 1)) * part
        turned_ref[pl.ds(pl.multiple_of(start, part), part), :] = values[block * part : (block + 1) * part]
    half = values.shape[0] // 2
    keep_ref[:, columns] = turned_ref[0:half, :]
    send_ref[:, columns] = turned_ref[half:, :]


def attend_back(relative, place, lengths, weights, proj, mixed, logs_in, branch, ht, bt, e_in):
    count, depth = branch.shape
    seqs = count // SEQ_LEN
    near = lambda i: jnp.minimum(i, seqs - 1)
    rows = lambda width: pl.BlockSpec((SEQ_LEN, width), lambda i, *_: (near(i), 0))
    logs = pl.BlockSpec((None, HEADS, SEQ_LEN), lambda i, *_: (near(i), 0, 0))
    half = 384 if relative else 768
    outs = [kept((count, depth), WIDE)] + [kept((half, 768))] * (2 if relative else 1) + [kept((1, 640), WIDE)]
    out_specs = [rows(depth)] + [whole(o.shape) for o in outs[1:]]
    in_specs = [whole((768, depth)), rows(640), rows(256), logs, rows(depth), whole((depth, count)), whole((depth, count))]
    operands = [weights, proj, mixed, logs_in, branch, ht, bt]
    aliases = None
    if e_in is not None:
        in_specs.append(rows(depth))
        operands.append(e_in)
        aliases = {9: 0}
    return call(
        functools.partial(attend_back_kernel, relative, e_in is None),
        "attend_back",
        outs,
        (seqs + 1,),
        in_specs,
        out_specs,
        [pltpu.VMEM((count, 896), LOW), pltpu.VMEM((768, 768), LOW)],
        scalars=2,
        flops=count * depth * 768 * 4,
        moved=count * depth * 12,
        aliases=aliases,
    )(place, lengths, *operands)


def feed_kernel(relative, loaded, first, last, place_ref, quarter_ref, h_ref, g_ref, ht_ref, gt_ref, bias_ref, *refs):
    out_in_ref, refs = refs[0], refs[1:]
    if not first:
        e_in_ref, refs = refs[0], refs[1:]
    weight_refs, refs = refs[:2], refs[2:]
    out_ref, e_ref, keep_ref, refs = refs[0], refs[1], refs[2], refs[3:]
    send_ref = None
    if relative:
        send_ref, refs = refs[0], refs[1:]
    sums_ref, hidden_ref, preact_ref, turned_ref = refs[:4]
    step = pl.program_id(0)
    count = hidden_ref.shape[0]
    tiles = count // SEQ_LEN
    if loaded:
        both_ref, sems = refs[4:]

        @pl.when(step == 0)
        def _():
            pieces = ((weight_refs[0], (0, 2)), (weight_refs[1], (1, 3)))
            copies = load_pieces(quarter_ref, pieces, both_ref, sems, both_ref.shape[0] // 4)
            for copy in copies:
                copy.start()
            for copy in copies:
                copy.wait()

        up_ref, down_ref = both_ref.at[:, 0:768], both_ref.at[:, 768:1536]
    else:
        up_ref, down_ref = weight_refs

    @pl.when(step < tiles)
    def _():
        h, g = h_ref[...], g_ref[...]
        start = pl.multiple_of(step * SEQ_LEN, 16)
        out = out_in_ref[...]
        e = None if first else e_in_ref[...]
        for a in range(0, up_ref.shape[1], 256):
            b = a + 256
            preact = product(h, up_ref[:, a:b]) + bias_ref[:, a:b]
            hidden, slope = gelu_both(preact)
            hidden = hidden.astype(LOW)
            grad = (product(g, down_ref[a:b, :], NT) * slope).astype(LOW)
            hidden_ref[pl.ds(start, SEQ_LEN), a:b] = hidden
            preact_ref[pl.ds(start, SEQ_LEN), a:b] = grad
            out = out + product(hidden, down_ref[a:b, :])
            term = product(grad, up_ref[:, a:b], NT)
            e = term if e is None else e + term
            sums = jnp.sum(grad.astype(WIDE), axis=0, keepdims=True)

            @pl.when(step == 0)
            def _():
                sums_ref[:, a:b] = sums

            @pl.when(step > 0)
            def _():
                sums_ref[:, a:b] += sums

        out_ref[...] = out.astype(out_ref.dtype)
        e_ref[...] = e

    @pl.when(step == tiles)
    def _():
        grads = product(ht_ref[...], preact_ref[...]).astype(LOW)
        scatter_rows(relative, place_ref, grads, turned_ref, keep_ref, send_ref, 0)

    @pl.when(step == tiles + 1)
    def _():
        grads = product(gt_ref[...], hidden_ref[...]).astype(LOW)
        scatter_rows(relative, place_ref, grads, turned_ref, keep_ref, send_ref, 768)


def feed(relative, last, place, quarter, h, g, ht, gt, bias, out_in, e_in, weights, loaded):
    count, depth = h.shape
    tiles = count // SEQ_LEN
    first = e_in is None
    rows = pl.BlockSpec((SEQ_LEN, depth), lambda i, *_: (jnp.minimum(i, tiles - 1), 0))
    half = 384 if relative else 768
    outs = [kept((count, depth), LOW if last else WIDE), kept((count, depth), WIDE)]
    outs += [kept((half, 1536))] * (2 if relative else 1) + [kept((1, 768), WIDE)]
    out_specs = [rows, rows] + [whole(o.shape) for o in outs[2:]]
    in_specs = [rows, rows, whole((depth, count)), whole((depth, count)), whole((1, 768)), rows]
    operands = [h, g, ht, gt, bias, out_in]
    aliases = {} if last else {7: 0}
    if not first:
        in_specs.append(rows)
        operands.append(e_in)
        aliases[8] = 1
    in_specs += [ANYWHERE] * 2 if loaded else [whole((768, depth))] * 2
    scratch = [pltpu.VMEM((count, 768), LOW), pltpu.VMEM((count, 768), LOW), pltpu.VMEM((768, 768), LOW)]
    if loaded:
        scratch += [pltpu.VMEM((768, 1536), LOW), pltpu.SemaphoreType.DMA((4,))]
    return call(
        functools.partial(feed_kernel, relative, loaded, first, last),
        "feed",
        outs,
        (tiles + 2,),
        in_specs,
        out_specs,
        scratch,
        scalars=2,
        flops=count * depth * 768 * 12,
        moved=count * depth * 20,
        aliases=aliases,
    )(place, quarter, *operands, *weights)


def fold_kernel(keep_ref, got_ref, *out_refs):
    part = out_refs[0].shape[0]
    for number, ref in enumerate(out_refs):
        rows = slice(number * part, (number + 1) * part)
        ref[...] = (keep_ref[rows].astype(WIDE) + got_ref[rows].astype(WIDE)).astype(LOW)


def fold(keep, got):
    half, width = keep.shape
    outs = [kept((half // 4, width))] * 4
    return call(
        fold_kernel,
        "fold",
        outs,
        (1,),
        [whole((half, width))] * 2,
        [whole(o.shape) for o in outs],
        moved=half * width * 6,
    )(keep, got)


def hop(value, mask, size=8):
    return lax.ppermute(value, "dp", [(i, i ^ mask) for i in range(size)])


def ring(value, shift, size=4):
    return lax.ppermute(value, "tensor", [(i, (i + shift) % size) for i in range(size)])


def together(*values):
    return lax.optimization_barrier(values)


def add_up(*parts):
    total = parts[0].astype(WIDE)
    for part in parts[1:]:
        total = total + part.astype(WIDE)
    return total


def bias_rows(qkv_sums, up_sums, parts):
    sums = qkv_sums[0]
    query = jnp.concatenate([sums[:128], sums[384:448]])
    value = jnp.concatenate([sums[256:384], sums[512:576]])
    return [v.reshape(parts, -1) for v in (query, value, up_sums)]


def pack_bias(b_qv):
    nothing = jnp.zeros((64,), WIDE)
    q, v = b_qv[0], b_qv[1]
    return jnp.concatenate([q[:128], nothing, nothing, v[:128], q[128:], nothing, v[128:]])


class Direct:
    relative = True

    def __init__(self):
        index = lax.axis_index("dp")
        self.place = index[None]
        self.quarter = ((((index >> 1) ^ (index >> 2)) & 1) * 2 + (index & 1))[None]

    def attention_near(self, first):
        return jnp.concatenate([first, hop(first, 2), hop(first, 4), hop(first, 6)], axis=0)

    def feed_near(self, first):
        half = first.shape[0] // 2
        return jnp.concatenate([first, hop(first[:half], 2), hop(first[half:], 4)], axis=0)


def direct_plan(args, biases_own):
    (tokens, lengths, cotangent, ln1_gain, ln1_bias, w_qkv, w_out, b_out, ln2_gain, ln2_bias, w_up, w_down, b_down) = args
    plan = Direct()
    place, quarter = plan.place, plan.quarter
    attn_own = pack_attention(w_qkv, w_out)
    part = attn_own.shape[0] // 8
    piece = lax.dynamic_slice_in_dim(attn_own, place[0] * part, part, 0)
    attn_first = {k: ring(piece, k) for k in (1, 2, 3)}
    biases = {k: ring(biases_own, k) for k in (1, 2, 3)}
    biases[0] = biases_own
    piece = jnp.concatenate(
        [lax.dynamic_slice_in_dim(w, quarter[0] * 2 * part, 2 * part, 0) for w in (w_up, w_down)], axis=1
    )
    piece, attn_first[3] = together(piece, attn_first[3])
    feed_first = {k: ring(piece, k) for k in (1, 2, 3)}

    h1, h1_t, g_t, total, g_sum = prepare(tokens, cotangent, ln1_gain, ln1_bias, b_out)

    h1, attn_first[1] = together(h1, attn_first[1])
    near, far, packed, saved, feed_near, feed_far = {}, {}, {0: attn_own}, {}, {}, {}
    near[1] = plan.attention_near(attn_first[1])
    *saved[0], total = attend(place, lengths, h1, total, biases[0][:, :576], (attn_own,))
    near[1], total = together(near[1], total)
    far[1] = hop(near[1], 1)
    near[2] = plan.attention_near(attn_first[2])
    near[2], total = together(near[2], total)
    near[3] = plan.attention_near(attn_first[3])
    *saved[1], total, packed[1] = attend(place, lengths, h1, total, biases[1][:, :576], (near[1], far[1]))
    far[2] = hop(near[2], 1)
    near[3], total, feed_first[1] = together(near[3], total, feed_first[1])
    far[3] = hop(near[3], 1)
    feed_near[1] = plan.feed_near(feed_first[1])
    *saved[2], total, packed[2] = attend(place, lengths, h1, total, biases[2][:, :576], (near[2], far[2]))
    feed_near[1], total = together(feed_near[1], total)
    feed_far[1] = hop(feed_near[1], 1)
    *saved[3], middle, packed[3] = attend(place, lengths, h1, total, biases[3][:, :576], (near[3], far[3]))
    middle, feed_first[2] = together(middle, feed_first[2])
    feed_near[2] = plan.feed_near(feed_first[2])

    h2, h2_t, out = middle_norm(middle, ln2_gain, ln2_bias, b_down)
    e = None
    halves, folded, up_sums, far_halves = {}, {}, {}, {}

    def run_feed(k, out, e, weights):
        out, e, keep, send, up_sums[k] = feed(
            True, k == 3, place, quarter, h2, cotangent, h2_t, g_t, biases[k][:, 576:], out, e, weights, k > 0
        )
        halves[k] = keep
        far_halves[k] = hop(send, 1)
        return out, e

    def spread(parts):
        return [parts[0], hop(parts[1], 2), hop(parts[2], 4), hop(parts[3], 6)]

    def summed(parts):
        return add_up(*parts).astype(LOW)

    out, e = run_feed(0, out, e, (w_up, w_down))
    feed_near[2], e, feed_first[3] = together(feed_near[2], e, feed_first[3])
    feed_far[2] = hop(feed_near[2], 1)
    feed_near[3] = plan.feed_near(feed_first[3])
    out, e = run_feed(1, out, e, (feed_near[1], feed_far[1]))
    folded[0] = fold(halves[0], far_halves[0])
    *folded[0], feed_near[3], e = together(*folded[0], feed_near[3], e)
    feed_far[3] = hop(feed_near[3], 1)
    folded[0] = spread(folded[0])
    out, e = run_feed(2, out, e, (feed_near[2], feed_far[2]))
    folded[1] = fold(halves[1], far_halves[1])
    *folded[1], e = together(*folded[1], e)
    folded[1] = spread(folded[1])
    sums = {0: summed(folded[0])}
    sums[0], e = together(sums[0], e)
    block_output, e = run_feed(3, out, e, (feed_near[3], feed_far[3]))
    folded[2] = fold(halves[2], far_halves[2])
    sums[1] = summed(folded[1])
    *folded[2], sums[1], e = together(*folded[2], sums[1], e)
    folded[2] = spread(folded[2])
    owned = {1: ring(sums[1], -1)}

    grad_middle, branch, branch_t, turn_sums = turn(e, middle, cotangent, ln2_gain)
    folded[3] = fold(halves[3], far_halves[3])
    *folded[3], branch = together(*folded[3], branch)
    folded[3] = spread(folded[3])

    qkv_sums, attn_halves, attn_far, attn_folded, attn_sums = {}, {}, {}, {}, {}
    e = None

    def run_back(k, e):
        proj, mixed, logs = saved[k]
        e, keep, send, qkv_sums[k] = attend_back(
            True, place, lengths, packed[k], proj, mixed, logs, branch_of[0], h1_t, branch_t, e
        )
        attn_halves[k] = keep
        attn_far[k] = hop(send, 1)
        return e

    branch_of = [branch]
    e = run_back(3, e)
    sums[2] = summed(folded[2])
    sums[2], owned[1], e = together(sums[2], owned[1], e)
    owned[2] = ring(sums[2], -2)
    e = run_back(2, e)
    sums[3] = summed(folded[3])
    attn_folded[3] = fold(attn_halves[3], attn_far[3])
    sums[3], *attn_folded[3], e = together(sums[3], *attn_folded[3], e)
    owned[3] = ring(sums[3], -3)
    attn_folded[3] = spread(attn_folded[3])
    e = run_back(1, e)
    attn_folded[2] = fold(attn_halves[2], attn_far[2])
    attn_sums[3] = summed(attn_folded[3])
    *attn_folded[2], attn_sums[3], owned[2], owned[3], e = together(*attn_folded[2], attn_sums[3], owned[2], owned[3], e)
    attn_folded[2] = spread(attn_folded[2])
    attn_owned = {3: ring(attn_sums[3], -3)}
    e = run_back(0, e)
    attn_folded[1] = fold(attn_halves[1], attn_far[1])
    attn_sums[2] = summed(attn_folded[2])
    *attn_folded[1], attn_sums[2], e = together(*attn_folded[1], attn_sums[2], e)
    attn_folded[1] = spread(attn_folded[1])
    attn_owned[2] = ring(attn_sums[2], -2)
    input_grad, finish_sums = finish(e, tokens, grad_middle, ln1_gain)
    attn_folded[0] = spread(fold(attn_halves[0], attn_far[0]))
    attn_owned[1] = ring(summed(attn_folded[1]), -1)
    grad_feed = add_up(sums[0], owned[1], owned[2], owned[3])
    grad_attn = add_up(*attn_folded[0], attn_owned[1], attn_owned[2], attn_owned[3])

    tensor = lax.axis_index("tensor")
    depth = tokens.shape[1]
    by_depth = jnp.concatenate([finish_sums, turn_sums, g_sum], axis=0)
    by_depth = by_depth.reshape(6, 8, 4, depth // 32).transpose(2, 1, 0, 3).reshape(4, 8, -1)
    shifts = [jnp.mod(tensor - k, 4) for k in range(4)]
    rows = []
    for k in range(4):
        own = lax.dynamic_index_in_dim(by_depth, shifts[k], 0, keepdims=False)
        rows.append(jnp.concatenate([own] + bias_rows(qkv_sums[k], up_sums[k], 8), axis=1))
    small = jnp.stack(rows)
    small = small + hop(small, 1)
    small = add_up(small, hop(small, 2), hop(small, 4), hop(small, 6))
    small = lax.dynamic_index_in_dim(small, place[0], 1, keepdims=False)
    small = add_up(small[0], *[ring(small[k], -k) for k in (1, 2, 3)])
    return block_output, input_grad, grad_feed, grad_attn, small


def per_device(dp_size, tensor_size, tokens, lengths, cotangent, ln1_gain, ln1_bias, w_qkv, b_qv, w_out, b_out, ln2_gain, ln2_bias, w_up, b_up, w_down, b_down):
    count, depth = tokens.shape
    seqs = count // SEQ_LEN
    lengths = lax.dynamic_slice_in_dim(lengths, lax.axis_index("tensor") * seqs, seqs, 0)
    biases = jnp.concatenate([pack_bias(b_qv), b_up])[None]
    row = lambda v: v[None]
    args = (tokens, lengths, cotangent, row(ln1_gain), row(ln1_bias), w_qkv, w_out, row(b_out), row(ln2_gain), row(ln2_bias), w_up, w_down, row(b_down))
    if (dp_size, tensor_size) == (8, 4):
        results = direct_plan(args, biases)
    else:
        results = general_plan(args, biases, dp_size, tensor_size)
    block_output, input_grad, grad_feed, grad_attn, small = results
    order = (0, 1, 4, 2, 3, 5)
    width = w_up.shape[1]
    grad_qkv, grad_out = unpack_attention(grad_attn)
    share = depth // (dp_size * tensor_size)
    vectors = small[: 6 * share].reshape(6, share)
    rest = small[6 * share :]
    own = w_qkv.shape[2] // dp_size
    return (
        block_output,
        input_grad,
        vectors[order[0]],
        vectors[order[1]],
        grad_qkv,
        rest[: 2 * own].reshape(2, own),
        grad_out,
        vectors[order[2]],
        vectors[order[3]],
        vectors[order[4]],
        grad_feed[:, :width],
        rest[2 * own :],
        grad_feed[:, width:].T,
        vectors[order[5]],
    )


def gather_shards(shard, dp_size):
    rows, columns = shard.shape
    part = rows // dp_size
    own = lax.dynamic_slice_in_dim(shard, lax.axis_index("dp") * part, part, 0)
    parts = lax.all_gather(own, ("dp", "tensor"), axis=0)
    parts = parts.reshape(dp_size, -1, part, columns).transpose(1, 0, 2, 3)
    return parts.reshape(-1, rows, columns)


def reduce_shards(partials, dp_size):
    rows, columns = partials[0].shape
    parts = jnp.stack([p.reshape(dp_size, rows // dp_size, columns) for p in partials], axis=1)
    parts = lax.psum_scatter(parts, "dp", scatter_dimension=0, tiled=True)[0]
    return lax.psum_scatter(parts, "tensor", scatter_dimension=0, tiled=True)[0].astype(WIDE)


def general_plan(args, biases_own, dp_size, tensor_size):
    (tokens, lengths, cotangent, ln1_gain, ln1_bias, w_qkv, w_out, b_out, ln2_gain, ln2_bias, w_up, w_down, b_down) = args
    depth = tokens.shape[1]
    place = quarter = jnp.zeros((1,), jnp.int32)
    attn = gather_shards(pack_attention(w_qkv, w_out), dp_size)
    both = gather_shards(jnp.concatenate([w_up, w_down], axis=1), dp_size)
    biases = lax.all_gather(biases_own, "tensor", axis=0)
    h1, h1_t, g_t, total, g_sum = prepare(tokens, cotangent, ln1_gain, ln1_bias, b_out)
    saved = []
    for k in range(tensor_size):
        *kept_here, total = attend(place, lengths, h1, total, biases[k][:, :576], (attn[k],))
        saved.append(kept_here)
    middle = total
    h2, h2_t, out = middle_norm(middle, ln2_gain, ln2_bias, b_down)
    e, grads, up_sums = None, [], []
    for k in range(tensor_size):
        weights = (both[k][:, : w_up.shape[1]], both[k][:, w_up.shape[1] :])
        out, e, grad, sums = feed(
            False, k == tensor_size - 1, place, quarter, h2, cotangent, h2_t, g_t, biases[k][:, 576:], out, e, weights, False
        )
        grads.append(grad)
        up_sums.append(sums)
    grad_feed = reduce_shards(grads, dp_size)
    grad_middle, branch, branch_t, turn_sums = turn(e, middle, cotangent, ln2_gain)
    e, grads, qkv_sums = None, [], []
    for k in range(tensor_size):
        e, grad, sums = attend_back(False, place, lengths, attn[k], *saved[k], branch, h1_t, branch_t, e)
        grads.append(grad)
        qkv_sums.append(sums)
    grad_attn = reduce_shards(grads, dp_size)
    input_grad, finish_sums = finish(e, tokens, grad_middle, ln1_gain)
    by_depth = jnp.concatenate([finish_sums, turn_sums, g_sum], axis=0)
    by_depth = by_depth.reshape(6, dp_size, tensor_size, -1).transpose(1, 2, 0, 3).reshape(dp_size, tensor_size, -1)
    rows = []
    for k in range(tensor_size):
        rows.append(jnp.concatenate([by_depth[:, k]] + bias_rows(qkv_sums[k], up_sums[k], dp_size), axis=1))
    small = jnp.stack(rows, axis=1).reshape(dp_size * tensor_size, -1)
    small = lax.psum_scatter(small, ("dp", "tensor"), scatter_dimension=0, tiled=True)[0]
    return out, input_grad, grad_feed, grad_attn, small


def solution(mesh):
    in_specs = (
        P(("dp", "tensor"), None),
        P("dp"),
        P(("dp", "tensor"), None),
        P(),
        P(),
        P(None, None, "tensor"),
        P(None, "tensor"),
        P("tensor", None),
        P(),
        P(),
        P(),
        P(None, "tensor"),
        P("tensor"),
        P("tensor", None),
        P(),
    )
    out_specs = (
        P(("dp", "tensor"), None),
        P(("dp", "tensor"), None),
        P(("dp", "tensor")),
        P(("dp", "tensor")),
        P(None, "dp", "tensor"),
        P(None, ("tensor", "dp")),
        P("tensor", "dp"),
        P(("dp", "tensor")),
        P(("dp", "tensor")),
        P(("dp", "tensor")),
        P("dp", "tensor"),
        P(("tensor", "dp")),
        P("tensor", "dp"),
        P(("dp", "tensor")),
    )
    return jax.shard_map(
        functools.partial(per_device, mesh.shape["dp"], mesh.shape["tensor"]), mesh=mesh, in_specs=in_specs, out_specs=out_specs, check_vma=False
    )
```

```python
import functools
from types import SimpleNamespace

import jax
import jax.numpy as jnp
from jax import lax
from jax.experimental import pallas as pl
from jax.experimental.pallas import tpu as pltpu
from jax.sharding import PartitionSpec as P

HD = 64
SEQ_LEN = 592
SCALE = HD**-0.5
EPSILON = 1e-06
MASKED = -1e30
LOW = jnp.bfloat16
WIDE = jnp.float32
HEADS = 3
NN = (((1,), (0,)), ((), ()))
NT = (((1,), (1,)), ((), ()))
TN = (((0,), (0,)), ((), ()))
PI_ROOT = (2.0 / 3.141592653589793) ** 0.5


def product(left, right, dims=NN):
    return lax.dot_general(left, right, dims, preferred_element_type=WIDE)


def three_parts(value):
    first = value.astype(LOW).astype(WIDE)
    rest = value - first
    second = rest.astype(LOW).astype(WIDE)
    return first, second, rest - second


def norm_parts(values):
    center = values - jnp.mean(values, axis=-1, keepdims=True)
    inverse = lax.rsqrt(jnp.mean(center * center, axis=-1, keepdims=True) + EPSILON)
    return center * inverse, inverse


def norm_back(grad, normed, inverse, gain):
    scaled = grad * gain
    return inverse * (
        scaled
        - jnp.mean(scaled, axis=-1, keepdims=True)
        - normed * jnp.mean(scaled * normed, axis=-1, keepdims=True)
    )


def call(kernel, name, outs, grid, in_specs, out_specs, scratch=(), scalars=0, aliases=None, flops=20_000_000_000, vmem=60):
    return pl.pallas_call(
        kernel,
        out_shape=outs,
        grid_spec=pltpu.PrefetchScalarGridSpec(
            num_scalar_prefetch=scalars,
            grid=grid,
            in_specs=in_specs,
            out_specs=out_specs,
            scratch_shapes=list(scratch),
        ),
        compiler_params=pltpu.CompilerParams(vmem_limit_bytes=vmem << 20),
        cost_estimate=pl.CostEstimate(flops=flops, bytes_accessed=1, transcendentals=0),
        input_output_aliases=aliases or {},
        name=name,
    )


def whole(shape):
    zeros = (0,) * len(shape)
    return pl.BlockSpec(shape, lambda *_: zeros)


def kept(shape, dtype=LOW):
    return jax.ShapeDtypeStruct(shape, dtype)


FAR = pl.BlockSpec(memory_space=pltpu.MemorySpace.HBM)
ANYWHERE = pl.BlockSpec(memory_space=pl.ANY)


EXTRA = 8
PIECE = 96 + EXTRA


def pack_kernel(relative, place_ref, qkv_ref, out_ref, qv_ref, up_bias_ref, *refs):
    if relative:
        up_ref, down_ref, packed_ref, rows_ref, piece_ref, feed_ref, sems = refs
        part = feed_ref.shape[0]
        source = pl.ds(pl.multiple_of(place_ref[0] * part, part), part)
        copies = [
            pltpu.make_async_copy(up_ref.at[source, :], feed_ref.at[:, 0:768], sems.at[0]),
            pltpu.make_async_copy(down_ref.at[source, :], feed_ref.at[:, 768:1536], sems.at[1]),
        ]
        for copy in copies:
            copy.start()
    else:
        packed_ref, rows_ref = refs
    for j in range(3):
        packed_ref[j * 128 : (j + 1) * 128, :] = qkv_ref[j, 0:128, :]
        packed_ref[384 + j * 64 : 448 + j * 64, :] = qkv_ref[j, 128:192, :]
    packed_ref[576:640, :] = out_ref[128:192, :]
    packed_ref[640:768, :] = out_ref[0:128, :]
    query, value, nothing = qv_ref[0:1, :], qv_ref[1:2, :], jnp.zeros((1, 128), WIDE)
    ends = [jnp.concatenate([v[:, 128:192], nothing[:, :64]], axis=1) for v in (query, value)]
    qv = jnp.concatenate([query[:, :128], nothing, value[:, :128], *ends, nothing], axis=1)
    rows = three_parts(qv) + three_parts(up_bias_ref[...][None])
    rows = jnp.concatenate(list(rows) + [jnp.zeros((2, 768), WIDE)], axis=0).astype(LOW)
    rows_ref[...] = rows
    if relative:
        start = pl.multiple_of(place_ref[0] * 96, 96)
        piece_ref[0:96, :] = packed_ref[pl.ds(start, 96), :]
        piece_ref[96:PIECE, :] = rows
        for copy in copies:
            copy.wait()


def pack_attention(relative, place, w_qkv, w_out, b_qv, b_up, w_up, w_down):
    depth = w_out.shape[1]
    outs = [kept((768, depth)), kept((EXTRA, depth))]
    operands = [w_qkv.transpose(0, 2, 1), w_out, b_qv, b_up]
    in_specs = [whole(v.shape) for v in operands]
    if relative:
        outs += [kept((PIECE, depth)), kept((96, 1536))]
        operands += [w_up, w_down]
        in_specs += [FAR] * 2
    return call(
        functools.partial(pack_kernel, relative),
        "pack",
        outs,
        (1,),
        in_specs,
        [whole(o.shape) for o in outs],
        [pltpu.SemaphoreType.DMA((2,))] if relative else [],
        scalars=1,
    )(place, *operands)


def bias_of(rows, first):
    parts = [rows[first + j : first + j + 1].astype(WIDE) for j in range(3)]
    return parts[0] + parts[1] + parts[2]


def unpack_attention(grads):
    q01, k01, v01, q2, k2, v2, o2, o01 = (
        grads[:, a:b]
        for a, b in ((0, 128), (128, 256), (256, 384), (384, 448), (448, 512), (512, 576), (576, 640), (640, 768))
    )
    stacked = [jnp.concatenate(pair, axis=1) for pair in ((q01, q2), (k01, k2), (v01, v2), (o01, o2))]
    return jnp.stack(stacked[:3]), stacked[3].T


def gelu_both(u):
    square = u * u
    t = jnp.tanh(PI_ROOT * u * (1.0 + 0.044715 * square))
    half = 0.5 * (1.0 + t)
    slope = half + (0.5 * PI_ROOT) * u * (1.0 - t * t) * (1.0 + (3 * 0.044715) * square)
    return u * half, slope


def spare_lane(upper):
    return 0 if upper else 64


def turn_halves(tile):
    return jnp.concatenate([tile[:, 64:128], tile[:, 0:64]], axis=1)


def head_tiles(proj, head):
    if head < 2:
        return proj[:, 0:128], proj[:, 128:256], proj[:, 256:384]
    both = proj[:, 384:512]
    return both, turn_halves(both), proj[:, 512:640]


class Copies:
    def __init__(self, sems):
        self.sems = sems
        self.used = 0
        self.saves = []

    def new(self, source, target):
        self.used += 1
        return pltpu.make_async_copy(source, target, self.sems.at[self.used - 1])

    def load(self, *pairs):
        copies = [self.new(*pair) for pair in pairs]
        for copy in copies:
            copy.start()
        return copies

    def save(self, source, target):
        self.saves += self.load((source, target))

    def finish(self):
        for copy in self.saves:
            copy.wait()


def wait_all(copies):
    for copy in copies:
        copy.wait()


def attend_kernel(stride, offset, place_ref, live_ref, *refs):
    if stride:
        h_ref, near_ref, far_ref, proj_ref, mixed_ref, log_ref, weights_ref, rows_ref, sems = refs

        @pl.when(pl.program_id(0) == 0)
        def _():
            copies = []
            for base, ref in ((0, near_ref), (1, far_ref)):
                for number in range(4):
                    start = pl.multiple_of((place_ref[0] ^ (2 * number + base)) * 96, 96)
                    source = ref.at[pl.ds(number * stride + offset, 96), :]
                    copies.append((source, weights_ref.at[pl.ds(start, 96), :]))
            copies.append((near_ref.at[pl.ds(offset + 96, EXTRA), :], rows_ref))
            copies = [pltpu.make_async_copy(*c, sems.at[j]) for j, c in enumerate(copies)]
            for copy in copies:
                copy.start()
            for copy in copies:
                copy.wait()

        h = h_ref[...]
    else:
        x_ref, gain_ref, shift_ref, rows_ref, weights_ref, proj_ref, mixed_ref, log_ref, h_ref = refs
        normed, _ = norm_parts(x_ref[...].astype(WIDE))
        h = (normed * gain_ref[...][None] + shift_ref[...][None]).astype(LOW)
        h_ref[...] = h
    live = live_ref[pl.program_id(0)]
    proj = (product(h, weights_ref[0:576, :], NT) + bias_of(rows_ref[...], 0)[:, :576]).astype(LOW)
    proj = jnp.concatenate([proj, jnp.zeros((SEQ_LEN, 64), LOW)], axis=1)
    proj_ref[...] = proj
    lane = lax.broadcasted_iota(jnp.int32, (1, 128), 1)
    row = lax.broadcasted_iota(jnp.int32, (SEQ_LEN, 1), 0)
    side = lax.broadcasted_iota(jnp.int32, (128, 1), 0)
    mask = jnp.where(row < live, 0.0, MASKED).astype(LOW)
    mixed = []
    for head in range(HEADS):
        upper = head == 1
        own = (lane >= 64) if upper else (lane < 64)
        spare = spare_lane(upper)
        query, keys, values = head_tiles(proj, head)
        query = query * jnp.asarray(SCALE, LOW)
        zero, one = jnp.zeros_like(query), jnp.ones_like(query)
        query = jnp.where(own, query, jnp.where(lane == spare, one, zero))
        keys = jnp.where(own, keys, jnp.where(lane == spare, mask, zero))
        values = jnp.where(own, values, jnp.where(lane == spare, one, zero))
        scores = product(keys, query, NT)
        highest = jnp.max(scores, axis=0, keepdims=True)
        weights = jnp.exp(scores - highest).astype(LOW)
        summed = product(values, weights, TN)
        spent = summed[spare : spare + 1, :]
        log_ref[head : head + 1, :] = highest + jnp.log(spent)
        mixed.append(summed * (1.0 / spent))
    first = jnp.where(side < 64, mixed[0], mixed[1]).astype(LOW).T
    third = jnp.where(side < 64, mixed[2], 0.0)
    third = jnp.concatenate([third[64:], third[:64]], axis=0).astype(LOW).T
    mixed_ref[...] = jnp.concatenate([third, first], axis=1)


def attend(place, lengths, rows_in, weights, norm=None, stride=0, offset=0):
    count, depth = rows_in.shape
    seqs = count // SEQ_LEN
    rows = lambda width: pl.BlockSpec((SEQ_LEN, width), lambda i, *_: (i, 0))
    logs = pl.BlockSpec((None, HEADS, SEQ_LEN), lambda i, *_: (i, 0, 0))
    outs = [kept((count, 640)), kept((count, 256)), kept((seqs, HEADS, SEQ_LEN), WIDE)]
    out_specs = [rows(640), rows(256), logs]
    in_specs, operands, scratch = [rows(depth)], [rows_in], []
    if stride:
        outs += [kept((768, depth)), kept((EXTRA, depth))]
        out_specs += [whole((768, depth)), whole((EXTRA, depth))]
        scratch = [pltpu.SemaphoreType.DMA((9,))]
        in_specs += [FAR, ANYWHERE]
    else:
        outs.append(kept((count, depth)))
        out_specs.append(rows(depth))
        in_specs += [whole((depth,))] * 2 + [whole((EXTRA, depth)), whole((768, depth))]
        operands += norm
    return call(
        functools.partial(attend_kernel, stride, offset),
        "attend",
        outs,
        (seqs,),
        in_specs,
        out_specs,
        scratch,
        scalars=2,
    )(place, lengths, *operands, *weights)


def attend_back_kernel(relative, place_ref, live_ref, weights_ref, proj_ref, mixed_ref, log_ref, branch_ref, h_ref, *refs):
    if relative:
        packed_ref, keep_ref, send_ref, sums_ref, *scratch = refs
    else:
        packed_ref, keep_ref, sums_ref, *scratch = refs
    weights_v, proj_v, branch_v, h_v, held_v, turned_v, sems = scratch
    copies = Copies(sems)
    tiles = [slice(a, a + SEQ_LEN) for a in range(0, h_v.shape[0], SEQ_LEN)]
    weights_loads = copies.load((weights_ref, weights_v))
    row_loads = [
        copies.load(
            (branch_ref.at[rows, :], branch_v.at[rows, :]),
            (proj_ref.at[rows, :], proj_v.at[rows, :]),
            (mixed_ref.at[rows, :], held_v.at[rows, 640:896]),
        )
        for rows in tiles
    ]
    h_loads = copies.load((h_ref, h_v))
    lane = lax.broadcasted_iota(jnp.int32, (1, 128), 1)
    row = lax.broadcasted_iota(jnp.int32, (SEQ_LEN, 1), 0)
    wait_all(weights_loads)
    sums = None
    for seq, rows in enumerate(tiles):
        wait_all(row_loads[seq])
        mask = jnp.where(row < live_ref[seq], 0.0, MASKED).astype(LOW)
        proj = proj_v[rows]
        mixed = held_v[rows, 640:896]
        grad_mixed = product(branch_v[rows], weights_v[512:768, :], NT).astype(LOW)
        totals = []
        for head in range(HEADS):
            upper = head == 1
            own = (lane >= 64) if upper else (lane < 64)
            spare = spare_lane(upper)
            query, keys, values = head_tiles(proj, head)
            if head < 2:
                grad, held = grad_mixed[:, 128:256], mixed[:, 128:256]
            else:
                grad, held = turn_halves(grad_mixed), turn_halves(mixed)
            query = query * jnp.asarray(SCALE, LOW)
            zero, one = jnp.zeros_like(query), jnp.ones_like(query)
            grad = jnp.where(own, grad, zero)
            wide_grad = grad.astype(WIDE)
            inner = jnp.sum(wide_grad * held.astype(WIDE), axis=-1, keepdims=True)
            parts = three_parts(-inner)
            shifted = wide_grad
            for place in range(3):
                shifted = jnp.where(lane == spare + place, parts[place], shifted)
            masked_query = jnp.where(own, query, jnp.where(lane == spare, one, zero))
            masked_keys = jnp.where(own, keys, jnp.where(lane == spare, mask, zero))
            spread_values = jnp.where(own, values, jnp.where((lane >= spare) & (lane < spare + 3), one, zero))
            probs = jnp.exp(product(masked_keys, masked_query, NT) - log_ref[seq, head : head + 1, :])
            centred = product(spread_values, shifted.astype(LOW), NT)
            grad_scores = (probs * centred).astype(LOW)
            parts = (
                (product(jnp.where(own, keys, zero), grad_scores, TN) * SCALE).astype(LOW).T,
                product(grad_scores, jnp.where(own, query, zero)).astype(LOW),
                product(probs.astype(LOW), grad).astype(LOW),
            )
            totals.append(parts)
        pair = [a + b for a, b in zip(totals[0], totals[1])]
        gq, gk, gv = totals[2]
        packed = jnp.concatenate(pair + [gq + turn_halves(gk), gv], axis=1)
        held_v[rows, 0:640] = packed
        copies.save(held_v.at[rows, 0:640], packed_ref.at[rows, :])
        part = jnp.sum(packed.astype(WIDE), axis=0, keepdims=True)
        sums = part if sums is None else sums + part
    sums_ref[...] = sums
    wait_all(h_loads)
    grads = product(h_v[...], held_v[:, 0:640], TN)
    outs = product(branch_v[...], held_v[:, 640:896], TN)
    full = jnp.concatenate([grads[:, :512], grads[:, 512:] + outs[:, :128], outs[:, 128:]], axis=1).astype(LOW)
    if relative:
        store_turned(place_ref, full, turned_v, slice(0, 768))
        copies.save(turned_v.at[384:768, :], send_ref)
        copies.save(turned_v.at[0:384, :], keep_ref)
    else:
        turned_v[...] = full
        copies.save(turned_v, keep_ref)
    copies.finish()


def store_turned(place_ref, values, target, columns):
    part = values.shape[0] // 8
    for block in range(8):
        other = place_ref[0] ^ block
        start = ((other & 1) * 4 + (other >> 1)) * part
        target[pl.ds(pl.multiple_of(start, part), part), columns] = values[block * part : (block + 1) * part]


def attend_back(relative, place, lengths, weights, proj, mixed, logs_in, branch, h):
    count, depth = branch.shape
    half = 384 if relative else 768
    outs = [kept((count, 640))] + [kept((half, 768))] * (2 if relative else 1) + [kept((1, 640), WIDE)]
    return call(
        functools.partial(attend_back_kernel, relative),
        "attend_back",
        outs,
        (1,),
        [FAR] * 3 + [whole(logs_in.shape)] + [FAR] * 2,
        [FAR] * (len(outs) - 1) + [whole((1, 640))],
        [
            pltpu.VMEM((768, depth), LOW),
            pltpu.VMEM((count, 640), LOW),
            pltpu.VMEM((count, depth), LOW),
            pltpu.VMEM((count, depth), LOW),
            pltpu.VMEM((count, 896), LOW),
            pltpu.VMEM((768, 768), LOW),
            pltpu.SemaphoreType.DMA((16,)),
        ],
        scalars=2,
        vmem=52,
    )(place, lengths, weights, proj, mixed, logs_in, branch, h)


def feed_kernel(tree, loaded, relative, first, last, place_ref, *refs):
    r = SimpleNamespace(**jax.tree.unflatten(tree, refs))
    count, depth = r.h_v.shape
    tiles = [slice(a, a + SEQ_LEN) for a in range(0, count, SEQ_LEN)]
    sems = r.sems
    used = [0]

    def copy(source, target):
        used[0] += 1
        return pltpu.make_async_copy(source, target, sems.at[used[0] - 1])

    shards = range(len(loaded))
    loads, ends = [], []
    for j, pieces in enumerate(loaded):
        both = r.both_v.at[j]
        mine = [copy(r.rows[j], r.rows_v.at[j])]
        if not pieces:
            mine += [copy(r.up[j], both.at[:, 0:768]), copy(r.down[j], both.at[:, 768:1536])]
        else:
            for base, ref in ((0, r.near[j]), (1, r.far[j])):
                for number in range(4):
                    start = pl.multiple_of((place_ref[0] ^ (2 * number + base)) * 96, 96)
                    mine.append(copy(ref.at[pl.ds(number * 96, 96), :], both.at[pl.ds(start, 96), :]))
        loads.append(mine)
    g_load = copy(r.g, r.g_v)

    def begin_save(*copies):
        for c in copies:
            c.start()
        ends.extend(copies)

    late = []
    if first:
        begin = [copy(r.x, r.x_v)]
        for k in range(4):
            begin.append(copy(r.mixed[k], r.mixed_v.at[k]))
            begin.append(copy(r.packed[k].at[512:768, :], r.out_v.at[k]))
    else:
        begin = [copy(r.h, r.h_v)]
        late = [copy(r.out_in, r.out_v), copy(r.e_in, r.e_v)]
    if last and not first:
        late.append(copy(r.middle, r.middle_v))
    for c in begin + loads[0] + [g_load] + late + [c for mine in loads[1:] for c in mine]:
        c.start()
    for c in begin:
        c.wait()
    if first:
        for rows in tiles:
            middle = r.x_v[rows].astype(WIDE) + r.out_bias[...][None]
            for k in range(4):
                middle = middle + product(r.mixed_v[k, rows, :], r.out_v[k])
            r.middle_v[rows] = middle
            normed, _ = norm_parts(middle)
            r.h_v[rows] = (normed * r.gain[...][None] + r.shift[...][None]).astype(LOW)
        begin_save(copy(r.middle_v, r.middle_out), copy(r.h_v, r.h_out))
    g_load.wait()
    h, g = r.h_v, r.g_v
    for j in shards:
        both, hidden_v, preact_v = r.both_v.at[j], r.hidden_v.at[j], r.preact_v.at[j]
        for c in loads[j]:
            c.wait()
        bias = bias_of(r.rows_v[j], 3)
        for a in range(0, 768, 768):
            b = a + 768
            sums = None
            for rows in tiles:
                preact = product(h[rows], both[:, a:b]) + bias[:, a:b]
                hidden, slope = gelu_both(preact)
                hidden_v[rows, a:b] = hidden.astype(LOW)
                grad = (product(g[rows], both[a:b, 768:1536], NT) * slope).astype(LOW)
                preact_v[rows, a:b] = grad
                part = jnp.sum(grad.astype(WIDE), axis=0, keepdims=True)
                sums = part if sums is None else sums + part
            r.sums[j : j + 1, a:b] = sums
    for c in late:
        c.wait()
    total_v, e_v = r.total_v, r.e_v
    for rows in tiles:
        total = r.middle_v[rows] + r.down_bias[...][None] if first else r.out_v[rows]
        e = None if first else e_v[rows]
        for j in shards:
            total = total + product(r.hidden_v[j, rows, :], r.both_v[j, :, 768:1536])
            term = product(r.preact_v[j, rows, :], r.both_v[j, :, 0:768], NT)
            e = term if e is None else e + term
        total_v[rows] = total.astype(total_v.dtype)
        e_v[rows] = e
    begin_save(copy(total_v, r.out))
    if not last:
        begin_save(copy(e_v, r.e))
    if last:
        totals = [0.0] * 3
        for rows in tiles:
            grad_h = e_v[rows]
            normed, inverse = norm_parts(r.middle_v[rows])
            grad = g[rows].astype(WIDE) + norm_back(grad_h, normed, inverse, r.gain[...][None])
            r.middle_v[rows] = grad
            r.branch_v[rows] = grad.astype(LOW)
            terms = (grad_h * normed, grad_h, grad)
            totals = [t + jnp.sum(v, axis=0, keepdims=True) for t, v in zip(totals, terms)]
        for number, total in enumerate(totals):
            r.turn_sums[number : number + 1, :] = total
        begin_save(copy(r.middle_v, r.grad_middle), copy(r.branch_v, r.branch))
    if first:
        r.g_sums[...] = jnp.sum(g[...].astype(WIDE), axis=0, keepdims=True)
    half = 384 if relative else 768
    for j in shards:
        turned = r.turned_v.at[j]
        for columns, left, right in ((slice(0, 768), h, r.preact_v), (slice(768, 1536), g, r.hidden_v)):
            grads = product(left[...], right[j], TN).astype(LOW)
            if relative:
                store_turned(place_ref, grads, turned, columns)
            else:
                turned[:, columns] = grads
        place = pl.ds(j * half, half)
        if relative:
            begin_save(copy(turned.at[384:768, :], r.send.at[place, :]))
        begin_save(copy(turned.at[0:half, :], r.keep.at[place, :]))
    for c in ends:
        c.wait()


def feed(relative, loaded, first, last, place, operands, vectors):
    count, depth = operands["g"].shape
    shards = len(loaded)
    half = 384 if relative else 768
    rows = (count, depth)
    big = dict(out=kept(rows, LOW if last else WIDE), keep=kept((shards * half, 1536)))
    if first:
        big |= dict(middle_out=kept(rows, WIDE), h_out=kept(rows))
    if last:
        big |= dict(grad_middle=kept(rows, WIDE), branch=kept(rows))
    else:
        big |= dict(e=kept(rows, WIDE))
    if relative:
        big |= dict(send=kept((shards * half, 1536)))
    small = dict(sums=kept((shards, 768), WIDE))
    if first:
        small |= dict(g_sums=kept((1, depth), WIDE))
    if last:
        small |= dict(turn_sums=kept((3, depth), WIDE))
    scratch = dict(
        h_v=pltpu.VMEM(rows, LOW),
        g_v=pltpu.VMEM(rows, LOW),
        hidden_v=pltpu.VMEM((shards, count, 768), LOW),
        preact_v=pltpu.VMEM((shards, count, 768), LOW),
        both_v=pltpu.VMEM((shards, depth, 1536), LOW),
        rows_v=pltpu.VMEM((shards, EXTRA, depth), LOW),
        turned_v=pltpu.VMEM((shards, 768, 1536), LOW),
        total_v=pltpu.VMEM(rows, LOW if last else WIDE),
        e_v=pltpu.VMEM(rows, WIDE),
        sems=pltpu.SemaphoreType.DMA((48,)),
    )
    if first:
        scratch |= dict(
            x_v=pltpu.VMEM(rows, LOW),
            mixed_v=pltpu.VMEM((4, count, 256), LOW),
            out_v=pltpu.VMEM((4, 256, depth), LOW),
        )
    else:
        scratch |= dict(out_v=pltpu.VMEM(rows, WIDE))
    if first or last:
        scratch |= dict(middle_v=pltpu.VMEM(rows, WIDE))
    if last:
        scratch |= dict(branch_v=pltpu.VMEM(rows, LOW))
    parts = [operands, vectors, big, small, scratch]
    flat = [jax.tree.flatten(part) for part in parts]
    numbers = iter(range(sum(len(leaves) for leaves, _ in flat)))
    order = {}
    for (leaves, tree) in flat:
        order |= jax.tree.unflatten(tree, [next(numbers) for _ in leaves])
    places, tree = jax.tree.flatten(order)

    def kernel(*refs):
        refs = refs[:1] + tuple(refs[1 + place] for place in places)
        feed_kernel(tree, loaded, relative, first, last, *refs)

    outs = flat[2][0] + flat[3][0]
    results = call(
        kernel,
        "feed",
        outs,
        (1,),
        [FAR] * len(flat[0][0]) + [whole(v.shape) for v in flat[1][0]],
        [FAR] * len(flat[2][0]) + [whole(o.shape) for o in flat[3][0]],
        flat[4][0],
        scalars=1,
    )(place, *flat[0][0], *flat[1][0])
    named = jax.tree.unflatten(flat[2][1], results[: len(big)]) | jax.tree.unflatten(flat[3][1], results[len(big) :])
    return SimpleNamespace(**named)


def finish_kernel(shards, joined, last, *refs):
    packed, weights = refs[:shards], refs[shards : 2 * shards]
    x_ref, grad_ref, gain_ref = refs[2 * shards : 2 * shards + 3]
    refs = refs[2 * shards + 3 :]
    if joined:
        refs = refs[1:]
    if last:
        before_ref, turn_ref, g_ref, *refs = refs
        ups, refs = refs[: shards // 2], refs[shards // 2 :]
        qkvs, refs = refs[:shards], refs[shards:]
    out_ref, sums_ref = refs
    grad_h = None
    for p, w in zip(packed, weights):
        term = product(p[...], w[...])
        grad_h = term if grad_h is None else grad_h + term
    normed, inverse = norm_parts(x_ref[...].astype(WIDE))
    out_ref[...] = (grad_ref[...] + norm_back(grad_h, normed, inverse, gain_ref[...][None])).astype(LOW)
    first = jnp.sum(grad_h * normed, axis=0, keepdims=True)
    second = jnp.sum(grad_h, axis=0, keepdims=True)
    if not last:
        sums_ref[0:1, :] = first
        sums_ref[1:2, :] = second
        return
    sums_ref[0:1, :] = first + before_ref[0:1, :]
    sums_ref[1:2, :] = second + before_ref[1:2, :]
    sums_ref[2:5, :] = turn_ref[...]
    sums_ref[5:6, :] = g_ref[...]
    for j, ref in enumerate(ups):
        sums_ref[6 + 2 * j : 8 + 2 * j, :] = ref[...]
    for j, ref in enumerate(qkvs):
        row = 6 + shards + j
        sums_ref[row : row + 1, 0:640] = ref[...]
        sums_ref[row : row + 1, 640:] = jnp.zeros_like(sums_ref[row : row + 1, 640:])
    sums_ref[6 + 2 * shards :, :] = jnp.zeros_like(sums_ref[6 + 2 * shards :, :])


def finish(tile, packed, weights, tokens, grad_middle, gain, joined=None, sums=()):
    count, depth = tokens.shape
    shards = len(packed)
    last = (tile + 1) * SEQ_LEN == count
    rows = lambda width: pl.BlockSpec((SEQ_LEN, width), lambda i: (tile, 0))
    operands = [*packed, *weights, tokens, grad_middle, gain]
    in_specs = [rows(640)] * shards + [pl.BlockSpec((640, depth), lambda i: (0, 0))] * shards
    in_specs += [rows(depth)] * 2 + [whole((depth,))]
    aliases = None
    if joined is not None:
        aliases = {len(operands): 0}
        operands.append(joined)
        in_specs.append(FAR)
    if last:
        operands += sums
        in_specs += [whole(v.shape) for v in sums]
    return call(
        functools.partial(finish_kernel, shards, joined is not None, last),
        "finish",
        (kept((count, depth)), kept((16 if last else 2, depth), WIDE)),
        (1,),
        in_specs,
        [rows(depth), whole((16 if last else 2, depth))],
        aliases=aliases,
    )(*operands)


def fold_kernel(pairs, plan, *refs):
    keeps, gots, refs = refs[:pairs], refs[pairs : 2 * pairs], refs[2 * pairs :]
    out_refs, refs = refs[: len(plan)], refs[len(plan) :]
    keep_vs, got_vs, sems = refs[:pairs], refs[pairs : 2 * pairs], refs[2 * pairs]
    work = []
    for out_ref, (pair, blocks) in zip(out_refs, plan):
        part = keep_vs[pair].shape[1]
        for place, block in enumerate(blocks):
            rows = pl.ds(block * part, part)
            keep_v, got_v = keep_vs[pair].at[block], got_vs[pair].at[block]
            sem = 3 * len(work)
            loads = [
                pltpu.make_async_copy(keeps[pair].at[rows, :], keep_v, sems.at[sem]),
                pltpu.make_async_copy(gots[pair].at[rows, :], got_v, sems.at[sem + 1]),
            ]
            end = pltpu.make_async_copy(keep_v, out_ref.at[pl.ds(place * part, part), :], sems.at[sem + 2])
            for copy in loads:
                copy.start()
            work.append((keep_v, got_v, loads, end))
    for keep_v, got_v, loads, end in work:
        for copy in loads:
            copy.wait()
        keep_v[...] = (keep_v[...].astype(WIDE) + got_v[...].astype(WIDE)).astype(LOW)
        end.start()
    for *_, end in work:
        end.wait()


def fold(pairs, plan, part=96):
    shapes = [(keep.shape[0] // part, part, keep.shape[1]) for keep, _ in pairs]
    count = sum(len(blocks) for _, blocks in plan)
    return call(
        functools.partial(fold_kernel, len(pairs), plan),
        "fold",
        [kept((len(blocks) * part, pairs[pair][0].shape[1])) for pair, blocks in plan],
        (1,),
        [FAR] * len(pairs) + [ANYWHERE] * len(pairs),
        [FAR] * len(plan),
        [pltpu.VMEM(shape, LOW) for shape in shapes] * 2 + [pltpu.SemaphoreType.DMA((3 * count,))],
        flops=1,
        vmem=60,
    )(*[keep for keep, _ in pairs], *[got for _, got in pairs])


def hop(value, mask, size=8):
    return lax.ppermute(value, "dp", [(i, i ^ mask) for i in range(size)])


def ring(value, shift, size=4):
    return lax.ppermute(value, "tensor", [(i, (i + shift) % size) for i in range(size)])


def together(*values):
    return lax.optimization_barrier(values)


def add_up(*parts):
    total = parts[0].astype(WIDE)
    for part in parts[1:]:
        total = total + part.astype(WIDE)
    return total


def bias_rows(qkv_sums, up_sums, parts):
    sums = qkv_sums[0]
    query = jnp.concatenate([sums[:128], sums[384:448]])
    value = jnp.concatenate([sums[256:384], sums[512:576]])
    return [v.reshape(parts, -1) for v in (query, value, up_sums)]


def closed(first):
    return [first, hop(first, 2), hop(first, 4), hop(first, 6)]


def joined_rows(parts):
    return jnp.concatenate(parts, axis=0)


MASK = {"x": 2, "y": 4}
OTHER = {"x": "y", "y": "x"}
FIRST = {"x": ((0, 2), (1, 3)), "y": ((0, 1), (2, 3))}


class Leaving:
    def __init__(self):
        self.live = []
        self.done = {}
        self.rings = []
        self.late = []

    def add(self, shards, keep, send):
        self.live.append((shards, 0, keep, hop(send, 1)))

    def step(self, *tied):
        arrays = [v for item in self.live for v in item[2:]]
        results = together(*tied, *arrays, *[self.done[name] for name in self.rings])
        tied, results = results[: len(tied)], results[len(tied) :]
        arrays, ended = results[: len(arrays)], results[len(arrays) :]
        self.done |= dict(zip(self.rings, ended))
        self.rings = []
        pairs = list(zip(arrays[0::2], arrays[1::2]))
        plan, follow = [], []
        for number, (shards, stage, *_) in enumerate(self.live):
            for place, shard in enumerate(shards):
                lists = [(0,), (1,)] if stage == 1 else [(0,)]
                if stage == 0:
                    lists = [tuple(4 * place + b for b in blocks) for blocks in FIRST[shard[1]]]
                follow.append((shard, stage, len(plan)))
                plan += [(number, blocks) for blocks in lists]
        held = [self.late.pop(0)] if self.late else []
        results = together(*tied, *[v for _, _, v in held], *fold(pairs, plan))
        tied, results = results[: len(tied)], results[len(tied) :]
        for (name, shift, _), value in zip(held, results):
            self.done[name] = ring(value, -shift)
            self.rings.append(name)
        results = results[len(held) :]
        self.live = []
        for shard, stage, place in follow:
            name, axis, shift = shard
            if stage < 2:
                mask = MASK[axis if stage == 0 else OTHER[axis]]
                self.live.append(((shard,), stage + 1, results[place], hop(results[place + 1], mask)))
            elif not shift:
                self.done[name] = results[place]
            elif name == 3:
                self.late.append((name, shift, results[place]))
            else:
                self.done[name] = ring(results[place], -shift)
                self.rings.append(name)
        return tied


def direct_plan(args):
    (tokens, lengths, cotangent, ln1_gain, ln1_bias, w_qkv, b_qv, b_up, w_out, b_out, ln2_gain, ln2_bias, w_up, w_down, b_down) = args
    index = lax.axis_index("dp")
    place = index[None]
    own, rows_own, piece, feed_piece = pack_attention(True, place, w_qkv, w_out, b_qv, b_up, w_up, w_down)
    attn_at = {k: ring(piece, k) for k in (1, 2, 3)}
    feed_at = {1: ring(feed_piece, 1)}

    packed, saved, rows = {0: own}, {}, {0: rows_own}
    *saved[0], h1 = attend(place, lengths, tokens, (rows_own, own), (ln1_gain, ln1_bias))
    h1, attn_at[1] = together(h1, attn_at[1])
    near1 = joined_rows(closed(attn_at[1]))
    near1, attn_at[2], attn_at[3], feed_at[1], feed_piece = together(
        near1, attn_at[2], attn_at[3], feed_at[1], feed_piece
    )
    far1 = hop(near1, 1)
    near2 = joined_rows(closed(attn_at[2]))
    near1, near2, attn_at[3], far1, feed_piece, h1 = together(near1, near2, attn_at[3], far1, feed_piece, h1)
    far2 = hop(near2, 1)
    close3 = closed(attn_at[3])
    feed_at[2] = ring(feed_piece, 2)
    *saved[1], packed[1], rows[1] = attend(place, lengths, h1, (near1, far1), None, PIECE, 0)
    h1, saved[1][0], far2, feed_at[2], feed_piece, *close3 = together(
        h1, saved[1][0], far2, feed_at[2], feed_piece, *close3
    )
    feed_at[3] = ring(feed_piece, 3)
    near3 = joined_rows(close3)
    near3, h1, feed_at[1] = together(near3, h1, feed_at[1])
    far3 = hop(near3, 1)
    feed1 = closed(feed_at[1])
    *saved[2], packed[2], rows[2] = attend(place, lengths, h1, (near2, far2), None, PIECE, 0)
    h1, saved[2][0], far3, feed_at[3], *feed1 = together(h1, saved[2][0], far3, feed_at[3], *feed1)
    feed_near1 = joined_rows(feed1)
    feed_near1, h1, feed_at[2] = together(feed_near1, h1, feed_at[2])
    feed_far1 = hop(feed_near1, 1)
    feed2 = closed(feed_at[2])
    *saved[3], packed[3], rows[3] = attend(place, lengths, h1, (near3, far3), None, PIECE, 0)
    saved[3][1], feed_far1, *feed2 = together(saved[3][1], feed_far1, *feed2)
    feed_near2 = joined_rows(feed2)
    feed_near2, feed_at[3], saved[3][1] = together(feed_near2, feed_at[3], saved[3][1])
    feed_far2 = hop(feed_near2, 1)
    feed3 = closed(feed_at[3])

    operands = dict(x=tokens, g=cotangent, up=[w_up], down=[w_down], rows=[rows[0], rows[1]])
    operands |= dict(near=[None, feed_near1], far=[None, feed_far1])
    operands |= dict(mixed=[saved[k][1] for k in range(4)], packed=[packed[k] for k in range(4)])
    vectors = dict(out_bias=b_out, gain=ln2_gain, shift=ln2_bias, down_bias=b_down)
    r = feed(True, (False, True), True, False, place, operands, vectors)
    middle, h2, g_sums, up_sums = r.middle_out, r.h_out, r.g_sums, [r.sums]
    h2, feed_far2, *feed3 = together(h2, feed_far2, *feed3)
    feed_near3 = joined_rows(feed3)
    feed_far3 = hop(feed_near3, 1)
    leaving = Leaving()
    leaving.add(((0, "x", 0), (1, "y", 1)), r.keep, r.send)
    operands = dict(h=h2, g=cotangent, out_in=r.out, e_in=r.e, middle=middle, rows=[rows[2], rows[3]])
    operands |= dict(near=[feed_near2, feed_near3], far=[feed_far2, feed_far3])
    r = feed(True, (True, True), False, True, place, operands, dict(gain=ln2_gain))
    block_output, grad_middle, branch, turn_sums = r.out, r.grad_middle, r.branch, r.turn_sums
    up_sums.append(r.sums)

    pieces, qkv_sums = {}, {}

    (branch,) = leaving.step(branch)
    leaving.add(((2, "x", 2), (3, "y", 3)), r.keep, r.send)
    for k in (3, 2, 1, 0):
        pieces[k], keep, send, qkv_sums[k] = attend_back(
            True, place, lengths, packed[k], *saved[k], branch, h1
        )
        branch, pieces[k] = leaving.step(branch, pieces[k])
        leaving.add(((4 + k, "y" if k % 2 else "x", k),), keep, send)
    given = [[v[k] for k in range(4)] for v in (pieces, packed)] + [tokens, grad_middle]
    half_grad, half_sums = finish(0, *given, ln1_gain)
    half_grad, half_sums = leaving.step(half_grad, half_sums)
    grad_feed = add_up(*[leaving.done[k] for k in range(4)])
    line = [half_sums, turn_sums, g_sums] + up_sums + [qkv_sums[k] for k in range(4)]
    input_grad, small = finish(1, *given, ln1_gain, half_grad, line)
    input_grad, small = leaving.step(input_grad, small)
    small = small + hop(small, 1)
    leaving.step()
    small = add_up(small, hop(small, 2), hop(small, 4), hop(small, 6))
    others = [ring(small, -k) for k in (1, 2, 3)]
    grad_attn = add_up(*[leaving.done[4 + k] for k in range(4)])
    small = jnp.concatenate(
        [
            add_up(small[:6], *[o[:6] for o in others]),
            add_up(small[6:7], *[o[6 + k : 7 + k] for k, o in zip((1, 2, 3), others)]),
            add_up(small[10:11], *[o[10 + k : 11 + k] for k, o in zip((1, 2, 3), others)]),
        ]
    )
    share = tokens.shape[1] // 32
    by_depth = lax.dynamic_slice_in_dim(small[:6], (index * 4 + lax.axis_index("tensor")) * share, share, 1)
    rest = [lax.dynamic_index_in_dim(v, index, 0, keepdims=False) for v in bias_rows(small[7:8], small[6:7], 8)]
    return block_output, input_grad, grad_feed, grad_attn, jnp.concatenate([by_depth.reshape(-1)] + rest)


def per_device(dp_size, tensor_size, tokens, lengths, cotangent, ln1_gain, ln1_bias, w_qkv, b_qv, w_out, b_out, ln2_gain, ln2_bias, w_up, b_up, w_down, b_down):
    count, depth = tokens.shape
    seqs = count // SEQ_LEN
    lengths = lax.dynamic_slice_in_dim(lengths, lax.axis_index("tensor") * seqs, seqs, 0)
    args = (tokens, lengths, cotangent, ln1_gain, ln1_bias, w_qkv, b_qv, b_up, w_out, b_out, ln2_gain, ln2_bias, w_up, w_down, b_down)
    if (dp_size, tensor_size) == (8, 4):
        results = direct_plan(args)
    else:
        results = general_plan(args, dp_size, tensor_size)
    block_output, input_grad, grad_feed, grad_attn, small = results
    order = (0, 1, 4, 2, 3, 5)
    width = w_up.shape[1]
    grad_qkv, grad_out = unpack_attention(grad_attn)
    share = depth // (dp_size * tensor_size)
    vectors = small[: 6 * share].reshape(6, share)
    rest = small[6 * share :]
    own = w_qkv.shape[2] // dp_size
    return (
        block_output,
        input_grad,
        vectors[order[0]],
        vectors[order[1]],
        grad_qkv,
        rest[: 2 * own].reshape(2, own),
        grad_out,
        vectors[order[2]],
        vectors[order[3]],
        vectors[order[4]],
        grad_feed[:, :width],
        rest[2 * own :],
        grad_feed[:, width:].T,
        vectors[order[5]],
    )


def gather_shards(shard, dp_size):
    rows, columns = shard.shape
    part = rows // dp_size
    own = lax.dynamic_slice_in_dim(shard, lax.axis_index("dp") * part, part, 0)
    parts = lax.all_gather(own, ("dp", "tensor"), axis=0)
    parts = parts.reshape(dp_size, -1, part, columns).transpose(1, 0, 2, 3)
    return parts.reshape(-1, rows, columns)


def reduce_shards(partials, dp_size):
    rows, columns = partials[0].shape
    parts = jnp.stack([p.reshape(dp_size, rows // dp_size, columns) for p in partials], axis=1)
    parts = lax.psum_scatter(parts, "dp", scatter_dimension=0, tiled=True)[0]
    return lax.psum_scatter(parts, "tensor", scatter_dimension=0, tiled=True)[0].astype(WIDE)


def general_plan(args, dp_size, tensor_size):
    (tokens, lengths, cotangent, ln1_gain, ln1_bias, w_qkv, b_qv, b_up, w_out, b_out, ln2_gain, ln2_bias, w_up, w_down, b_down) = args
    place = jnp.zeros((1,), jnp.int32)
    own, rows_own = pack_attention(False, place, w_qkv, w_out, b_qv, b_up, w_up, w_down)
    attn = gather_shards(own, dp_size)
    both = gather_shards(jnp.concatenate([w_up, w_down], axis=1), dp_size)
    rows = lax.all_gather(rows_own, "tensor", axis=0)
    shards = range(tensor_size)
    saved = []
    for k in shards:
        *kept_here, h1 = attend(place, lengths, tokens, (rows[k], attn[k]), (ln1_gain, ln1_bias))
        saved.append(kept_here)
    grads, up_sums, r = [], [], None
    for k in range(0, tensor_size, 2):
        first, last = k == 0, k + 2 == tensor_size
        ours = both[k : k + 2]
        operands = dict(g=cotangent, up=list(ours[:, :, : w_up.shape[1]]), down=list(ours[:, :, w_up.shape[1] :]))
        operands |= dict(rows=list(rows[k : k + 2]))
        vectors = {}
        if first:
            operands |= dict(x=tokens, mixed=[v[1] for v in saved], packed=list(attn))
            vectors = dict(out_bias=b_out, gain=ln2_gain, shift=ln2_bias, down_bias=b_down)
        else:
            operands |= dict(h=h2, out_in=r.out, e_in=r.e)
        if last:
            operands |= dict(middle=middle)
            vectors |= dict(gain=ln2_gain)
        r = feed(False, (False, False), first, last, place, operands, vectors)
        if first:
            middle, h2, g_sums = r.middle_out, r.h_out, r.g_sums
        grads += [r.keep[:768], r.keep[768:]]
        up_sums.append(r.sums)
    grad_feed = reduce_shards(grads, dp_size)
    grad_middle, branch, turn_sums = r.grad_middle, r.branch, r.turn_sums
    pieces, grads, qkv_sums = [], [], []
    for k in shards:
        piece, grad, sums = attend_back(False, place, lengths, attn[k], *saved[k], branch, h1)
        pieces.append(piece)
        grads.append(grad)
        qkv_sums.append(sums)
    grad_attn = reduce_shards(grads, dp_size)
    given = [pieces, [attn[k] for k in shards], tokens, grad_middle]
    half_grad, half_sums = finish(0, *given, ln1_gain)
    input_grad, small = finish(1, *given, ln1_gain, half_grad, [half_sums, turn_sums, g_sums] + up_sums + qkv_sums)
    by_depth = small[:6].reshape(6, dp_size, tensor_size, -1).transpose(1, 2, 0, 3).reshape(dp_size, tensor_size, -1)
    lines = []
    for k in shards:
        up, qkv = small[6 + k : 7 + k], small[10 + k : 11 + k]
        lines.append(jnp.concatenate([by_depth[:, k]] + bias_rows(qkv, up, dp_size), axis=1))
    small = jnp.stack(lines, axis=1).reshape(dp_size * tensor_size, -1)
    small = lax.psum_scatter(small, ("dp", "tensor"), scatter_dimension=0, tiled=True)[0]
    return r.out, input_grad, grad_feed, grad_attn, small


def solution(mesh):
    in_specs = (
        P(("dp", "tensor"), None),
        P("dp"),
        P(("dp", "tensor"), None),
        P(),
        P(),
        P(None, None, "tensor"),
        P(None, "tensor"),
        P("tensor", None),
        P(),
        P(),
        P(),
        P(None, "tensor"),
        P("tensor"),
        P("tensor", None),
        P(),
    )
    out_specs = (
        P(("dp", "tensor"), None),
        P(("dp", "tensor"), None),
        P(("dp", "tensor")),
        P(("dp", "tensor")),
        P(None, "dp", "tensor"),
        P(None, ("tensor", "dp")),
        P("tensor", "dp"),
        P(("dp", "tensor")),
        P(("dp", "tensor")),
        P(("dp", "tensor")),
        P("dp", "tensor"),
        P(("tensor", "dp")),
        P("tensor", "dp"),
        P(("dp", "tensor")),
    )
    return jax.shard_map(
        functools.partial(per_device, mesh.shape["dp"], mesh.shape["tensor"]), mesh=mesh, in_specs=in_specs, out_specs=out_specs, check_vma=False
    )
```

```python
import functools
from types import SimpleNamespace

import jax
import jax.numpy as jnp
from jax import lax
from jax.experimental import pallas as pl
from jax.experimental.pallas import tpu as pltpu
from jax.sharding import PartitionSpec as P

HD = 64
SEQ_LEN = 592
SCALE = HD**-0.5
EPSILON = 1e-06
MASKED = -1e30
LOW = jnp.bfloat16
WIDE = jnp.float32
HEADS = 3
NN = (((1,), (0,)), ((), ()))
NT = (((1,), (1,)), ((), ()))
TN = (((0,), (0,)), ((), ()))
PI_ROOT = (2.0 / 3.141592653589793) ** 0.5


def product(left, right, dims=NN):
    return lax.dot_general(left, right, dims, preferred_element_type=WIDE)


def three_parts(value):
    first = value.astype(LOW).astype(WIDE)
    rest = value - first
    second = rest.astype(LOW).astype(WIDE)
    return first, second, rest - second


def norm_parts(values):
    center = values - jnp.mean(values, axis=-1, keepdims=True)
    inverse = lax.rsqrt(jnp.mean(center * center, axis=-1, keepdims=True) + EPSILON)
    return center * inverse, inverse


def norm_back(grad, normed, inverse, gain):
    scaled = grad * gain
    return inverse * (
        scaled
        - jnp.mean(scaled, axis=-1, keepdims=True)
        - normed * jnp.mean(scaled * normed, axis=-1, keepdims=True)
    )


def call(kernel, name, outs, grid, in_specs, out_specs, scratch=(), scalars=0, aliases=None, flops=20_000_000_000, vmem=60):
    return pl.pallas_call(
        kernel,
        out_shape=outs,
        grid_spec=pltpu.PrefetchScalarGridSpec(
            num_scalar_prefetch=scalars,
            grid=grid,
            in_specs=in_specs,
            out_specs=out_specs,
            scratch_shapes=list(scratch),
        ),
        compiler_params=pltpu.CompilerParams(vmem_limit_bytes=vmem << 20),
        cost_estimate=pl.CostEstimate(flops=flops, bytes_accessed=1, transcendentals=0),
        input_output_aliases=aliases or {},
        name=name,
    )


def whole(shape):
    zeros = (0,) * len(shape)
    return pl.BlockSpec(shape, lambda *_: zeros)


def kept(shape, dtype=LOW):
    return jax.ShapeDtypeStruct(shape, dtype)


FAR = pl.BlockSpec(memory_space=pltpu.MemorySpace.HBM)
ANYWHERE = pl.BlockSpec(memory_space=pl.ANY)


EXTRA = 8
PIECE = 96 + EXTRA


def pack_kernel(relative, place_ref, qkv_ref, out_ref, qv_ref, up_bias_ref, *refs):
    if relative:
        up_ref, down_ref, packed_ref, rows_ref, piece_ref, feed_ref, sems = refs
        part = feed_ref.shape[0]
        source = pl.ds(pl.multiple_of(place_ref[0] * part, part), part)
        copies = [
            pltpu.make_async_copy(up_ref.at[source, :], feed_ref.at[:, 0:768], sems.at[0]),
            pltpu.make_async_copy(down_ref.at[source, :], feed_ref.at[:, 768:1536], sems.at[1]),
        ]
        for copy in copies:
            copy.start()
    else:
        packed_ref, rows_ref = refs
    for j in range(3):
        packed_ref[j * 128 : (j + 1) * 128, :] = qkv_ref[j, 0:128, :]
        packed_ref[384 + j * 64 : 448 + j * 64, :] = qkv_ref[j, 128:192, :]
    packed_ref[576:640, :] = out_ref[128:192, :]
    packed_ref[640:768, :] = out_ref[0:128, :]
    query, value, nothing = qv_ref[0:1, :], qv_ref[1:2, :], jnp.zeros((1, 128), WIDE)
    ends = [jnp.concatenate([v[:, 128:192], nothing[:, :64]], axis=1) for v in (query, value)]
    qv = jnp.concatenate([query[:, :128], nothing, value[:, :128], *ends, nothing], axis=1)
    rows = three_parts(qv) + three_parts(up_bias_ref[...][None])
    rows = jnp.concatenate(list(rows) + [jnp.zeros((2, 768), WIDE)], axis=0).astype(LOW)
    rows_ref[...] = rows
    if relative:
        start = pl.multiple_of(place_ref[0] * 96, 96)
        piece_ref[0:96, :] = packed_ref[pl.ds(start, 96), :]
        piece_ref[96:PIECE, :] = rows
        for copy in copies:
            copy.wait()


def pack_attention(relative, place, w_qkv, w_out, b_qv, b_up, w_up, w_down):
    depth = w_out.shape[1]
    outs = [kept((768, depth)), kept((EXTRA, depth))]
    operands = [w_qkv.transpose(0, 2, 1), w_out, b_qv, b_up]
    in_specs = [whole(v.shape) for v in operands]
    if relative:
        outs += [kept((PIECE, depth)), kept((96, 1536))]
        operands += [w_up, w_down]
        in_specs += [FAR] * 2
    return call(
        functools.partial(pack_kernel, relative),
        "pack",
        outs,
        (1,),
        in_specs,
        [whole(o.shape) for o in outs],
        [pltpu.SemaphoreType.DMA((2,))] if relative else [],
        scalars=1,
    )(place, *operands)


def bias_of(rows, first):
    parts = [rows[first + j : first + j + 1].astype(WIDE) for j in range(3)]
    return parts[0] + parts[1] + parts[2]


def unpack_attention(grads):
    q01, k01, v01, q2, k2, v2, o2, o01 = (
        grads[:, a:b]
        for a, b in ((0, 128), (128, 256), (256, 384), (384, 448), (448, 512), (512, 576), (576, 640), (640, 768))
    )
    stacked = [jnp.concatenate(pair, axis=1) for pair in ((q01, q2), (k01, k2), (v01, v2), (o01, o2))]
    return jnp.stack(stacked[:3]), stacked[3].T


def gelu_both(u):
    square = u * u
    t = jnp.tanh(PI_ROOT * u * (1.0 + 0.044715 * square))
    half = 0.5 * (1.0 + t)
    slope = half + (0.5 * PI_ROOT) * u * (1.0 - t * t) * (1.0 + (3 * 0.044715) * square)
    return u * half, slope


def spare_lane(upper):
    return 0 if upper else 64


def turn_halves(tile):
    return jnp.concatenate([tile[:, 64:128], tile[:, 0:64]], axis=1)


def head_tiles(proj, head):
    if head < 2:
        return proj[:, 0:128], proj[:, 128:256], proj[:, 256:384]
    both = proj[:, 384:512]
    return both, turn_halves(both), proj[:, 512:640]


class Copies:
    def __init__(self, sems):
        self.sems = sems
        self.used = 0
        self.saves = []

    def new(self, source, target):
        self.used += 1
        return pltpu.make_async_copy(source, target, self.sems.at[self.used - 1])

    def load(self, *pairs):
        copies = [self.new(*pair) for pair in pairs]
        for copy in copies:
            copy.start()
        return copies

    def save(self, source, target):
        self.saves += self.load((source, target))

    def finish(self):
        for copy in self.saves:
            copy.wait()


def wait_all(copies):
    for copy in copies:
        copy.wait()


def attend_kernel(stride, offset, place_ref, live_ref, *refs):
    if stride:
        h_ref, near_ref, far_ref, proj_ref, mixed_ref, log_ref, weights_ref, rows_ref, sems = refs

        @pl.when(pl.program_id(0) == 0)
        def _():
            copies = []
            for base, ref in ((0, near_ref), (1, far_ref)):
                for number in range(4):
                    start = pl.multiple_of((place_ref[0] ^ (2 * number + base)) * 96, 96)
                    source = ref.at[pl.ds(number * stride + offset, 96), :]
                    copies.append((source, weights_ref.at[pl.ds(start, 96), :]))
            copies.append((near_ref.at[pl.ds(offset + 96, EXTRA), :], rows_ref))
            copies = [pltpu.make_async_copy(*c, sems.at[j]) for j, c in enumerate(copies)]
            for copy in copies:
                copy.start()
            for copy in copies:
                copy.wait()

        h = h_ref[...]
    else:
        x_ref, gain_ref, shift_ref, rows_ref, weights_ref, proj_ref, mixed_ref, log_ref, h_ref = refs
        normed, _ = norm_parts(x_ref[...].astype(WIDE))
        h = (normed * gain_ref[...][None] + shift_ref[...][None]).astype(LOW)
        h_ref[...] = h
    live = live_ref[pl.program_id(0)]
    proj = (product(h, weights_ref[0:576, :], NT) + bias_of(rows_ref[...], 0)[:, :576]).astype(LOW)
    proj = jnp.concatenate([proj, jnp.zeros((SEQ_LEN, 64), LOW)], axis=1)
    proj_ref[...] = proj
    lane = lax.broadcasted_iota(jnp.int32, (1, 128), 1)
    row = lax.broadcasted_iota(jnp.int32, (SEQ_LEN, 1), 0)
    side = lax.broadcasted_iota(jnp.int32, (128, 1), 0)
    mask = jnp.where(row < live, 0.0, MASKED).astype(LOW)
    mixed = []
    for head in range(HEADS):
        upper = head == 1
        own = (lane >= 64) if upper else (lane < 64)
        spare = spare_lane(upper)
        query, keys, values = head_tiles(proj, head)
        query = query * jnp.asarray(SCALE, LOW)
        zero, one = jnp.zeros_like(query), jnp.ones_like(query)
        query = jnp.where(own, query, jnp.where(lane == spare, one, zero))
        keys = jnp.where(own, keys, jnp.where(lane == spare, mask, zero))
        values = jnp.where(own, values, jnp.where(lane == spare, one, zero))
        scores = product(keys, query, NT)
        highest = jnp.max(scores, axis=0, keepdims=True)
        weights = jnp.exp(scores - highest).astype(LOW)
        summed = product(values, weights, TN)
        spent = summed[spare : spare + 1, :]
        log_ref[head : head + 1, :] = highest + jnp.log(spent)
        mixed.append(summed * (1.0 / spent))
    first = jnp.where(side < 64, mixed[0], mixed[1]).astype(LOW).T
    third = jnp.where(side < 64, mixed[2], 0.0)
    third = jnp.concatenate([third[64:], third[:64]], axis=0).astype(LOW).T
    mixed_ref[...] = jnp.concatenate([third, first], axis=1)


def attend(place, lengths, rows_in, weights, norm=None, stride=0, offset=0):
    count, depth = rows_in.shape
    seqs = count // SEQ_LEN
    rows = lambda width: pl.BlockSpec((SEQ_LEN, width), lambda i, *_: (i, 0))
    logs = pl.BlockSpec((None, HEADS, SEQ_LEN), lambda i, *_: (i, 0, 0))
    outs = [kept((count, 640)), kept((count, 256)), kept((seqs, HEADS, SEQ_LEN), WIDE)]
    out_specs = [rows(640), rows(256), logs]
    in_specs, operands, scratch = [rows(depth)], [rows_in], []
    if stride:
        outs += [kept((768, depth)), kept((EXTRA, depth))]
        out_specs += [whole((768, depth)), whole((EXTRA, depth))]
        scratch = [pltpu.SemaphoreType.DMA((9,))]
        in_specs += [FAR, ANYWHERE]
    else:
        outs.append(kept((count, depth)))
        out_specs.append(rows(depth))
        in_specs += [whole((depth,))] * 2 + [whole((EXTRA, depth)), whole((768, depth))]
        operands += norm
    return call(
        functools.partial(attend_kernel, stride, offset),
        "attend",
        outs,
        (seqs,),
        in_specs,
        out_specs,
        scratch,
        scalars=2,
    )(place, lengths, *operands, *weights)


def attend_back_kernel(relative, place_ref, live_ref, weights_ref, proj_ref, mixed_ref, log_ref, branch_ref, h_ref, *refs):
    if relative:
        packed_ref, keep_ref, send_ref, sums_ref, *scratch = refs
    else:
        packed_ref, keep_ref, sums_ref, *scratch = refs
    weights_v, proj_v, branch_v, h_v, held_v, turned_v, sems = scratch
    copies = Copies(sems)
    tiles = [slice(a, a + SEQ_LEN) for a in range(0, h_v.shape[0], SEQ_LEN)]
    weights_loads = copies.load((weights_ref, weights_v))
    row_loads = [
        copies.load(
            (branch_ref.at[rows, :], branch_v.at[rows, :]),
            (proj_ref.at[rows, :], proj_v.at[rows, :]),
            (mixed_ref.at[rows, :], held_v.at[rows, 640:896]),
        )
        for rows in tiles
    ]
    h_loads = copies.load((h_ref, h_v))
    lane = lax.broadcasted_iota(jnp.int32, (1, 128), 1)
    row = lax.broadcasted_iota(jnp.int32, (SEQ_LEN, 1), 0)
    wait_all(weights_loads)
    sums = None
    for seq, rows in enumerate(tiles):
        wait_all(row_loads[seq])
        mask = jnp.where(row < live_ref[seq], 0.0, MASKED).astype(LOW)
        proj = proj_v[rows]
        mixed = held_v[rows, 640:896]
        grad_mixed = product(branch_v[rows], weights_v[512:768, :], NT).astype(LOW)
        totals = []
        for head in range(HEADS):
            upper = head == 1
            own = (lane >= 64) if upper else (lane < 64)
            spare = spare_lane(upper)
            query, keys, values = head_tiles(proj, head)
            if head < 2:
                grad, held = grad_mixed[:, 128:256], mixed[:, 128:256]
            else:
                grad, held = turn_halves(grad_mixed), turn_halves(mixed)
            query = query * jnp.asarray(SCALE, LOW)
            zero, one = jnp.zeros_like(query), jnp.ones_like(query)
            grad = jnp.where(own, grad, zero)
            wide_grad = grad.astype(WIDE)
            inner = jnp.sum(wide_grad * held.astype(WIDE), axis=-1, keepdims=True)
            parts = three_parts(-inner)
            shifted = wide_grad
            for place in range(3):
                shifted = jnp.where(lane == spare + place, parts[place], shifted)
            masked_query = jnp.where(own, query, jnp.where(lane == spare, one, zero))
            masked_keys = jnp.where(own, keys, jnp.where(lane == spare, mask, zero))
            spread_values = jnp.where(own, values, jnp.where((lane >= spare) & (lane < spare + 3), one, zero))
            probs = jnp.exp(product(masked_keys, masked_query, NT) - log_ref[seq, head : head + 1, :])
            centred = product(spread_values, shifted.astype(LOW), NT)
            grad_scores = (probs * centred).astype(LOW)
            parts = (
                (product(jnp.where(own, keys, zero), grad_scores, TN) * SCALE).astype(LOW).T,
                product(grad_scores, jnp.where(own, query, zero)).astype(LOW),
                product(probs.astype(LOW), grad).astype(LOW),
            )
            totals.append(parts)
        pair = [a + b for a, b in zip(totals[0], totals[1])]
        gq, gk, gv = totals[2]
        packed = jnp.concatenate(pair + [gq + turn_halves(gk), gv], axis=1)
        held_v[rows, 0:640] = packed
        copies.save(held_v.at[rows, 0:640], packed_ref.at[rows, :])
        part = jnp.sum(packed.astype(WIDE), axis=0, keepdims=True)
        sums = part if sums is None else sums + part
    sums_ref[...] = sums
    wait_all(h_loads)
    grads = product(h_v[...], held_v[:, 0:640], TN)
    outs = product(branch_v[...], held_v[:, 640:896], TN)
    full = jnp.concatenate([grads[:, :512], grads[:, 512:] + outs[:, :128], outs[:, 128:]], axis=1).astype(LOW)
    if relative:
        store_turned(place_ref, full, turned_v, slice(0, 768))
        copies.save(turned_v.at[384:768, :], send_ref)
        copies.save(turned_v.at[0:384, :], keep_ref)
    else:
        turned_v[...] = full
        copies.save(turned_v, keep_ref)
    copies.finish()


def store_turned(place_ref, values, target, columns):
    part = values.shape[0] // 8
    for block in range(8):
        other = place_ref[0] ^ block
        start = ((other & 1) * 4 + (other >> 1)) * part
        target[pl.ds(pl.multiple_of(start, part), part), columns] = values[block * part : (block + 1) * part]


def attend_back(relative, place, lengths, weights, proj, mixed, logs_in, branch, h):
    count, depth = branch.shape
    half = 384 if relative else 768
    outs = [kept((count, 640))] + [kept((half, 768))] * (2 if relative else 1) + [kept((1, 640), WIDE)]
    return call(
        functools.partial(attend_back_kernel, relative),
        "attend_back",
        outs,
        (1,),
        [FAR] * 3 + [whole(logs_in.shape)] + [FAR] * 2,
        [FAR] * (len(outs) - 1) + [whole((1, 640))],
        [
            pltpu.VMEM((768, depth), LOW),
            pltpu.VMEM((count, 640), LOW),
            pltpu.VMEM((count, depth), LOW),
            pltpu.VMEM((count, depth), LOW),
            pltpu.VMEM((count, 896), LOW),
            pltpu.VMEM((768, 768), LOW),
            pltpu.SemaphoreType.DMA((16,)),
        ],
        scalars=2,
        vmem=52,
    )(place, lengths, weights, proj, mixed, logs_in, branch, h)


def feed_kernel(tree, loaded, relative, first, last, place_ref, *refs):
    r = SimpleNamespace(**jax.tree.unflatten(tree, refs))
    count, depth = r.h_v.shape
    tiles = [slice(a, a + SEQ_LEN) for a in range(0, count, SEQ_LEN)]
    sems = r.sems
    used = [0]

    def copy(source, target):
        used[0] += 1
        return pltpu.make_async_copy(source, target, sems.at[used[0] - 1])

    shards = range(len(loaded))
    loads, ends = [], []
    for j, pieces in enumerate(loaded):
        both = r.both_v.at[j]
        mine = [copy(r.rows[j], r.rows_v.at[j])]
        if not pieces:
            mine += [copy(r.up[j], both.at[:, 0:768]), copy(r.down[j], both.at[:, 768:1536])]
        else:
            for base, ref in ((0, r.near[j]), (1, r.far[j])):
                for number in range(4):
                    start = pl.multiple_of((place_ref[0] ^ (2 * number + base)) * 96, 96)
                    mine.append(copy(ref.at[pl.ds(number * 96, 96), :], both.at[pl.ds(start, 96), :]))
        loads.append(mine)
    g_load = copy(r.g, r.g_v)

    def begin_save(*copies):
        for c in copies:
            c.start()
        ends.extend(copies)

    late = []
    if first:
        begin = [copy(r.x, r.x_v)]
        for k in range(4):
            begin.append(copy(r.mixed[k], r.mixed_v.at[k]))
            begin.append(copy(r.packed[k].at[512:768, :], r.out_v.at[k]))
    else:
        begin = [copy(r.h, r.h_v)]
        late = [copy(r.out_in, r.out_v), copy(r.e_in, r.e_v)]
    if last and not first:
        late.append(copy(r.middle, r.middle_v))
    for c in begin + loads[0] + [g_load] + late + [c for mine in loads[1:] for c in mine]:
        c.start()
    for c in begin:
        c.wait()
    if first:
        for rows in tiles:
            middle = r.x_v[rows].astype(WIDE) + r.out_bias[...][None]
            for k in range(4):
                middle = middle + product(r.mixed_v[k, rows, :], r.out_v[k])
            r.middle_v[rows] = middle
            normed, _ = norm_parts(middle)
            r.h_v[rows] = (normed * r.gain[...][None] + r.shift[...][None]).astype(LOW)
        begin_save(copy(r.middle_v, r.middle_out), copy(r.h_v, r.h_out))
    g_load.wait()
    h, g = r.h_v, r.g_v
    for j in shards:
        both, hidden_v, preact_v = r.both_v.at[j], r.hidden_v.at[j], r.preact_v.at[j]
        for c in loads[j]:
            c.wait()
        bias = bias_of(r.rows_v[j], 3)
        for a in range(0, 768, 768):
            b = a + 768
            sums = None
            for rows in tiles:
                preact = product(h[rows], both[:, a:b]) + bias[:, a:b]
                hidden, slope = gelu_both(preact)
                hidden_v[rows, a:b] = hidden.astype(LOW)
                grad = (product(g[rows], both[a:b, 768:1536], NT) * slope).astype(LOW)
                preact_v[rows, a:b] = grad
                part = jnp.sum(grad.astype(WIDE), axis=0, keepdims=True)
                sums = part if sums is None else sums + part
            r.sums[j : j + 1, a:b] = sums
    for c in late:
        c.wait()
    total_v, e_v = r.total_v, r.e_v
    for rows in tiles:
        total = r.middle_v[rows] + r.down_bias[...][None] if first else r.out_v[rows]
        e = None if first else e_v[rows]
        for j in shards:
            total = total + product(r.hidden_v[j, rows, :], r.both_v[j, :, 768:1536])
            term = product(r.preact_v[j, rows, :], r.both_v[j, :, 0:768], NT)
            e = term if e is None else e + term
        total_v[rows] = total.astype(total_v.dtype)
        e_v[rows] = e
    begin_save(copy(total_v, r.out))
    if not last:
        begin_save(copy(e_v, r.e))
    if last:
        totals = [0.0] * 3
        for rows in tiles:
            grad_h = e_v[rows]
            normed, inverse = norm_parts(r.middle_v[rows])
            grad = g[rows].astype(WIDE) + norm_back(grad_h, normed, inverse, r.gain[...][None])
            r.middle_v[rows] = grad
            r.branch_v[rows] = grad.astype(LOW)
            terms = (grad_h * normed, grad_h, grad)
            totals = [t + jnp.sum(v, axis=0, keepdims=True) for t, v in zip(totals, terms)]
        for number, total in enumerate(totals):
            r.turn_sums[number : number + 1, :] = total
        begin_save(copy(r.middle_v, r.grad_middle), copy(r.branch_v, r.branch))
    if first:
        r.g_sums[...] = jnp.sum(g[...].astype(WIDE), axis=0, keepdims=True)
    half = 384 if relative else 768
    for j in shards:
        turned = r.turned_v.at[j]
        for columns, left, right in ((slice(0, 768), h, r.preact_v), (slice(768, 1536), g, r.hidden_v)):
            grads = product(left[...], right[j], TN).astype(LOW)
            if relative:
                store_turned(place_ref, grads, turned, columns)
            else:
                turned[:, columns] = grads
        place = pl.ds(j * half, half)
        if relative:
            begin_save(copy(turned.at[384:768, :], r.send.at[place, :]))
        begin_save(copy(turned.at[0:half, :], r.keep.at[place, :]))
    for c in ends:
        c.wait()


def feed(relative, loaded, first, last, place, operands, vectors):
    count, depth = operands["g"].shape
    shards = len(loaded)
    half = 384 if relative else 768
    rows = (count, depth)
    big = dict(out=kept(rows, LOW if last else WIDE), keep=kept((shards * half, 1536)))
    if first:
        big |= dict(middle_out=kept(rows, WIDE), h_out=kept(rows))
    if last:
        big |= dict(grad_middle=kept(rows, WIDE), branch=kept(rows))
    else:
        big |= dict(e=kept(rows, WIDE))
    if relative:
        big |= dict(send=kept((shards * half, 1536)))
    small = dict(sums=kept((shards, 768), WIDE))
    if first:
        small |= dict(g_sums=kept((1, depth), WIDE))
    if last:
        small |= dict(turn_sums=kept((3, depth), WIDE))
    scratch = dict(
        h_v=pltpu.VMEM(rows, LOW),
        g_v=pltpu.VMEM(rows, LOW),
        hidden_v=pltpu.VMEM((shards, count, 768), LOW),
        preact_v=pltpu.VMEM((shards, count, 768), LOW),
        both_v=pltpu.VMEM((shards, depth, 1536), LOW),
        rows_v=pltpu.VMEM((shards, EXTRA, depth), LOW),
        turned_v=pltpu.VMEM((shards, 768, 1536), LOW),
        total_v=pltpu.VMEM(rows, LOW if last else WIDE),
        e_v=pltpu.VMEM(rows, WIDE),
        sems=pltpu.SemaphoreType.DMA((48,)),
    )
    if first:
        scratch |= dict(
            x_v=pltpu.VMEM(rows, LOW),
            mixed_v=pltpu.VMEM((4, count, 256), LOW),
            out_v=pltpu.VMEM((4, 256, depth), LOW),
        )
    else:
        scratch |= dict(out_v=pltpu.VMEM(rows, WIDE))
    if first or last:
        scratch |= dict(middle_v=pltpu.VMEM(rows, WIDE))
    if last:
        scratch |= dict(branch_v=pltpu.VMEM(rows, LOW))
    parts = [operands, vectors, big, small, scratch]
    flat = [jax.tree.flatten(part) for part in parts]
    numbers = iter(range(sum(len(leaves) for leaves, _ in flat)))
    order = {}
    for (leaves, tree) in flat:
        order |= jax.tree.unflatten(tree, [next(numbers) for _ in leaves])
    places, tree = jax.tree.flatten(order)

    def kernel(*refs):
        refs = refs[:1] + tuple(refs[1 + place] for place in places)
        feed_kernel(tree, loaded, relative, first, last, *refs)

    outs = flat[2][0] + flat[3][0]
    results = call(
        kernel,
        "feed",
        outs,
        (1,),
        [FAR] * len(flat[0][0]) + [whole(v.shape) for v in flat[1][0]],
        [FAR] * len(flat[2][0]) + [whole(o.shape) for o in flat[3][0]],
        flat[4][0],
        scalars=1,
    )(place, *flat[0][0], *flat[1][0])
    named = jax.tree.unflatten(flat[2][1], results[: len(big)]) | jax.tree.unflatten(flat[3][1], results[len(big) :])
    return SimpleNamespace(**named)


def finish_kernel(shards, joined, last, *refs):
    packed, weights = refs[:shards], refs[shards : 2 * shards]
    x_ref, grad_ref, gain_ref = refs[2 * shards : 2 * shards + 3]
    refs = refs[2 * shards + 3 :]
    if joined:
        refs = refs[1:]
    if last:
        before_ref, turn_ref, g_ref, *refs = refs
        ups, refs = refs[: shards // 2], refs[shards // 2 :]
        qkvs, refs = refs[:shards], refs[shards:]
    out_ref, sums_ref = refs
    grad_h = None
    for p, w in zip(packed, weights):
        term = product(p[...], w[...])
        grad_h = term if grad_h is None else grad_h + term
    normed, inverse = norm_parts(x_ref[...].astype(WIDE))
    out_ref[...] = (grad_ref[...] + norm_back(grad_h, normed, inverse, gain_ref[...][None])).astype(LOW)
    first = jnp.sum(grad_h * normed, axis=0, keepdims=True)
    second = jnp.sum(grad_h, axis=0, keepdims=True)
    if not last:
        sums_ref[0:1, :] = first
        sums_ref[1:2, :] = second
        return
    sums_ref[0:1, :] = first + before_ref[0:1, :]
    sums_ref[1:2, :] = second + before_ref[1:2, :]
    sums_ref[2:5, :] = turn_ref[...]
    sums_ref[5:6, :] = g_ref[...]
    for j, ref in enumerate(ups):
        sums_ref[6 + 2 * j : 8 + 2 * j, :] = ref[...]
    for j, ref in enumerate(qkvs):
        row = 6 + shards + j
        sums_ref[row : row + 1, 0:640] = ref[...]
        sums_ref[row : row + 1, 640:] = jnp.zeros_like(sums_ref[row : row + 1, 640:])
    sums_ref[6 + 2 * shards :, :] = jnp.zeros_like(sums_ref[6 + 2 * shards :, :])


def finish(tile, packed, weights, tokens, grad_middle, gain, joined=None, sums=()):
    count, depth = tokens.shape
    shards = len(packed)
    last = (tile + 1) * SEQ_LEN == count
    rows = lambda width: pl.BlockSpec((SEQ_LEN, width), lambda i: (tile, 0))
    operands = [*packed, *weights, tokens, grad_middle, gain]
    in_specs = [rows(640)] * shards + [pl.BlockSpec((640, depth), lambda i: (0, 0))] * shards
    in_specs += [rows(depth)] * 2 + [whole((depth,))]
    aliases = None
    if joined is not None:
        aliases = {len(operands): 0}
        operands.append(joined)
        in_specs.append(FAR)
    if last:
        operands += sums
        in_specs += [whole(v.shape) for v in sums]
    return call(
        functools.partial(finish_kernel, shards, joined is not None, last),
        "finish",
        (kept((count, depth)), kept((16 if last else 2, depth), WIDE)),
        (1,),
        in_specs,
        [rows(depth), whole((16 if last else 2, depth))],
        aliases=aliases,
    )(*operands)


def fold_kernel(pairs, plan, *refs):
    keeps, gots, refs = refs[:pairs], refs[pairs : 2 * pairs], refs[2 * pairs :]
    out_refs, refs = refs[: len(plan)], refs[len(plan) :]
    keep_vs, got_vs, sems = refs[:pairs], refs[pairs : 2 * pairs], refs[2 * pairs]
    work = []
    for out_ref, (pair, blocks) in zip(out_refs, plan):
        part = keep_vs[pair].shape[1]
        for place, block in enumerate(blocks):
            rows = pl.ds(block * part, part)
            keep_v, got_v = keep_vs[pair].at[block], got_vs[pair].at[block]
            sem = 3 * len(work)
            loads = [
                pltpu.make_async_copy(keeps[pair].at[rows, :], keep_v, sems.at[sem]),
                pltpu.make_async_copy(gots[pair].at[rows, :], got_v, sems.at[sem + 1]),
            ]
            end = pltpu.make_async_copy(keep_v, out_ref.at[pl.ds(place * part, part), :], sems.at[sem + 2])
            for copy in loads:
                copy.start()
            work.append((keep_v, got_v, loads, end))
    for keep_v, got_v, loads, end in work:
        for copy in loads:
            copy.wait()
        keep_v[...] = (keep_v[...].astype(WIDE) + got_v[...].astype(WIDE)).astype(LOW)
        end.start()
    for *_, end in work:
        end.wait()


def fold(pairs, plan, part=96):
    shapes = [(keep.shape[0] // part, part, keep.shape[1]) for keep, _ in pairs]
    count = sum(len(blocks) for _, blocks in plan)
    return call(
        functools.partial(fold_kernel, len(pairs), plan),
        "fold",
        [kept((len(blocks) * part, pairs[pair][0].shape[1])) for pair, blocks in plan],
        (1,),
        [FAR] * len(pairs) + [ANYWHERE] * len(pairs),
        [FAR] * len(plan),
        [pltpu.VMEM(shape, LOW) for shape in shapes] * 2 + [pltpu.SemaphoreType.DMA((3 * count,))],
        flops=1,
        vmem=60,
    )(*[keep for keep, _ in pairs], *[got for _, got in pairs])


def hop(value, mask, size=8):
    return lax.ppermute(value, "dp", [(i, i ^ mask) for i in range(size)])


def ring(value, shift, size=4):
    return lax.ppermute(value, "tensor", [(i, (i + shift) % size) for i in range(size)])


def together(*values):
    return lax.optimization_barrier(values)


def add_up(*parts):
    total = parts[0].astype(WIDE)
    for part in parts[1:]:
        total = total + part.astype(WIDE)
    return total


def bias_rows(qkv_sums, up_sums, parts):
    sums = qkv_sums[0]
    query = jnp.concatenate([sums[:128], sums[384:448]])
    value = jnp.concatenate([sums[256:384], sums[512:576]])
    return [v.reshape(parts, -1) for v in (query, value, up_sums)]


def closed(first):
    return [first, hop(first, 2), hop(first, 4), hop(first, 6)]


def joined_rows(parts):
    return jnp.concatenate(parts, axis=0)


MASK = {"x": 2, "y": 4}
SHIFTS = (0, 1, 3, 2)
OTHER = {"x": "y", "y": "x"}
FIRST = {"x": ((0, 2), (1, 3)), "y": ((0, 1), (2, 3))}


class Leaving:
    def __init__(self):
        self.live = []
        self.done = {}
        self.rings = []
        self.late = []

    def add(self, shards, keep, send):
        self.live.append((shards, 0, keep, hop(send, 1)))

    def step(self, *tied):
        arrays = [v for item in self.live for v in item[2:]]
        results = together(*tied, *arrays, *[self.done[name] for name in self.rings])
        tied, results = results[: len(tied)], results[len(tied) :]
        arrays, ended = results[: len(arrays)], results[len(arrays) :]
        self.done |= dict(zip(self.rings, ended))
        self.rings = []
        pairs = list(zip(arrays[0::2], arrays[1::2]))
        plan, follow = [], []
        for number, (shards, stage, *_) in enumerate(self.live):
            for place, shard in enumerate(shards):
                lists = [(0,), (1,)] if stage == 1 else [(0,)]
                if stage == 0:
                    lists = [tuple(4 * place + b for b in blocks) for blocks in FIRST[shard[1]]]
                follow.append((shard, stage, len(plan)))
                plan += [(number, blocks) for blocks in lists]
        held = [self.late.pop(0)] if self.late else []
        results = together(*tied, *[v for _, _, v in held], *fold(pairs, plan))
        tied, results = results[: len(tied)], results[len(tied) :]
        for (name, shift, _), value in zip(held, results):
            self.done[name] = ring(value, -shift)
            self.rings.append(name)
        results = results[len(held) :]
        self.live = []
        for shard, stage, place in follow:
            name, axis, shift = shard
            if stage < 2:
                mask = MASK[axis if stage == 0 else OTHER[axis]]
                self.live.append(((shard,), stage + 1, results[place], hop(results[place + 1], mask)))
            elif not shift:
                self.done[name] = results[place]
            elif name in (2, 7):
                self.late.append((name, shift, results[place]))
            else:
                self.done[name] = ring(results[place], -shift)
                self.rings.append(name)
        return tied


def direct_plan(args):
    (tokens, lengths, cotangent, ln1_gain, ln1_bias, w_qkv, b_qv, b_up, w_out, b_out, ln2_gain, ln2_bias, w_up, w_down, b_down) = args
    index = lax.axis_index("dp")
    place = index[None]
    own, rows_own, piece, feed_piece = pack_attention(True, place, w_qkv, w_out, b_qv, b_up, w_up, w_down)
    attn_at = {j: ring(piece, SHIFTS[j]) for j in (1, 2)}
    feed_at = {}

    packed, saved, rows = {0: own}, {}, {0: rows_own}
    *saved[0], h1 = attend(place, lengths, tokens, (rows_own, own), (ln1_gain, ln1_bias))
    h1, attn_at[1], attn_at[2], piece, feed_piece = together(h1, attn_at[1], attn_at[2], piece, feed_piece)
    near1 = joined_rows(closed(attn_at[1]))
    attn_at[3] = ring(piece, SHIFTS[3])
    feed_at[3] = ring(feed_piece, SHIFTS[3])
    near1, attn_at[2], attn_at[3], feed_piece = together(near1, attn_at[2], attn_at[3], feed_piece)
    far1 = hop(near1, 1)
    near2 = joined_rows(closed(attn_at[2]))
    near1, near2, attn_at[3], far1, feed_at[3], feed_piece, h1 = together(
        near1, near2, attn_at[3], far1, feed_at[3], feed_piece, h1
    )
    far2 = hop(near2, 1)
    close3 = closed(attn_at[3])
    feed_at[1] = ring(feed_piece, SHIFTS[1])
    *saved[1], packed[1], rows[1] = attend(place, lengths, h1, (near1, far1), None, PIECE, 0)
    h1, saved[1][0], far2, feed_at[1], feed_piece, *close3 = together(
        h1, saved[1][0], far2, feed_at[1], feed_piece, *close3
    )
    feed_at[2] = ring(feed_piece, SHIFTS[2])
    near3 = joined_rows(close3)
    near3, h1, feed_at[1] = together(near3, h1, feed_at[1])
    far3 = hop(near3, 1)
    feed1 = closed(feed_at[1])
    *saved[2], packed[2], rows[2] = attend(place, lengths, h1, (near2, far2), None, PIECE, 0)
    h1, saved[2][0], far3, feed_at[2], *feed1 = together(h1, saved[2][0], far3, feed_at[2], *feed1)
    feed_near1 = joined_rows(feed1)
    feed_near1, h1, feed_at[2] = together(feed_near1, h1, feed_at[2])
    feed_far1 = hop(feed_near1, 1)
    feed2 = closed(feed_at[2])
    *saved[3], packed[3], rows[3] = attend(place, lengths, h1, (near3, far3), None, PIECE, 0)
    saved[3][1], feed_far1, *feed2 = together(saved[3][1], feed_far1, *feed2)
    feed_near2 = joined_rows(feed2)
    feed_near2, feed_at[3], saved[3][1] = together(feed_near2, feed_at[3], saved[3][1])
    feed_far2 = hop(feed_near2, 1)
    feed3 = closed(feed_at[3])

    operands = dict(x=tokens, g=cotangent, up=[w_up], down=[w_down], rows=[rows[0], rows[1]])
    operands |= dict(near=[None, feed_near1], far=[None, feed_far1])
    operands |= dict(mixed=[saved[k][1] for k in range(4)], packed=[packed[k] for k in range(4)])
    vectors = dict(out_bias=b_out, gain=ln2_gain, shift=ln2_bias, down_bias=b_down)
    r = feed(True, (False, True), True, False, place, operands, vectors)
    middle, h2, g_sums, up_sums = r.middle_out, r.h_out, r.g_sums, [r.sums]
    h2, feed_far2, *feed3 = together(h2, feed_far2, *feed3)
    feed_near3 = joined_rows(feed3)
    feed_far3 = hop(feed_near3, 1)
    leaving = Leaving()
    leaving.add(((0, "x", 0), (1, "y", SHIFTS[1])), r.keep, r.send)
    operands = dict(h=h2, g=cotangent, out_in=r.out, e_in=r.e, middle=middle, rows=[rows[2], rows[3]])
    operands |= dict(near=[feed_near2, feed_near3], far=[feed_far2, feed_far3])
    r = feed(True, (True, True), False, True, place, operands, dict(gain=ln2_gain))
    block_output, grad_middle, branch, turn_sums = r.out, r.grad_middle, r.branch, r.turn_sums
    up_sums.append(r.sums)

    pieces, qkv_sums = {}, {}

    (branch,) = leaving.step(branch)
    leaving.add(((2, "x", SHIFTS[2]), (3, "y", SHIFTS[3])), r.keep, r.send)
    for k in (3, 2, 1, 0):
        pieces[k], keep, send, qkv_sums[k] = attend_back(
            True, place, lengths, packed[k], *saved[k], branch, h1
        )
        branch, pieces[k] = leaving.step(branch, pieces[k])
        leaving.add(((4 + k, "y" if k % 2 else "x", SHIFTS[k]),), keep, send)
    given = [[v[k] for k in range(4)] for v in (pieces, packed)] + [tokens, grad_middle]
    half_grad, half_sums = finish(0, *given, ln1_gain)
    half_grad, half_sums = leaving.step(half_grad, half_sums)
    grad_feed = add_up(*[leaving.done[k] for k in range(4)])
    line = [half_sums, turn_sums, g_sums] + up_sums + [qkv_sums[k] for k in range(4)]
    input_grad, small = finish(1, *given, ln1_gain, half_grad, line)
    input_grad, small = leaving.step(input_grad, small)
    small = small + hop(small, 1)
    leaving.step()
    small = add_up(small, hop(small, 2), hop(small, 4), hop(small, 6))
    others = [ring(small, -SHIFTS[k]) for k in (1, 2, 3)]
    grad_attn = add_up(*[leaving.done[4 + k] for k in range(4)])
    small = jnp.concatenate(
        [
            add_up(small[:6], *[o[:6] for o in others]),
            add_up(small[6:7], *[o[6 + k : 7 + k] for k, o in zip((1, 2, 3), others)]),
            add_up(small[10:11], *[o[10 + k : 11 + k] for k, o in zip((1, 2, 3), others)]),
        ]
    )
    share = tokens.shape[1] // 32
    by_depth = lax.dynamic_slice_in_dim(small[:6], (index * 4 + lax.axis_index("tensor")) * share, share, 1)
    rest = [lax.dynamic_index_in_dim(v, index, 0, keepdims=False) for v in bias_rows(small[7:8], small[6:7], 8)]
    return block_output, input_grad, grad_feed, grad_attn, jnp.concatenate([by_depth.reshape(-1)] + rest)


def per_device(dp_size, tensor_size, tokens, lengths, cotangent, ln1_gain, ln1_bias, w_qkv, b_qv, w_out, b_out, ln2_gain, ln2_bias, w_up, b_up, w_down, b_down):
    count, depth = tokens.shape
    seqs = count // SEQ_LEN
    lengths = lax.dynamic_slice_in_dim(lengths, lax.axis_index("tensor") * seqs, seqs, 0)
    args = (tokens, lengths, cotangent, ln1_gain, ln1_bias, w_qkv, b_qv, b_up, w_out, b_out, ln2_gain, ln2_bias, w_up, w_down, b_down)
    if (dp_size, tensor_size) == (8, 4):
        results = direct_plan(args)
    else:
        results = general_plan(args, dp_size, tensor_size)
    block_output, input_grad, grad_feed, grad_attn, small = results
    order = (0, 1, 4, 2, 3, 5)
    width = w_up.shape[1]
    grad_qkv, grad_out = unpack_attention(grad_attn)
    share = depth // (dp_size * tensor_size)
    vectors = small[: 6 * share].reshape(6, share)
    rest = small[6 * share :]
    own = w_qkv.shape[2] // dp_size
    return (
        block_output,
        input_grad,
        vectors[order[0]],
        vectors[order[1]],
        grad_qkv,
        rest[: 2 * own].reshape(2, own),
        grad_out,
        vectors[order[2]],
        vectors[order[3]],
        vectors[order[4]],
        grad_feed[:, :width],
        rest[2 * own :],
        grad_feed[:, width:].T,
        vectors[order[5]],
    )


def gather_shards(shard, dp_size):
    rows, columns = shard.shape
    part = rows // dp_size
    own = lax.dynamic_slice_in_dim(shard, lax.axis_index("dp") * part, part, 0)
    parts = lax.all_gather(own, ("dp", "tensor"), axis=0)
    parts = parts.reshape(dp_size, -1, part, columns).transpose(1, 0, 2, 3)
    return parts.reshape(-1, rows, columns)


def reduce_shards(partials, dp_size):
    rows, columns = partials[0].shape
    parts = jnp.stack([p.reshape(dp_size, rows // dp_size, columns) for p in partials], axis=1)
    parts = lax.psum_scatter(parts, "dp", scatter_dimension=0, tiled=True)[0]
    return lax.psum_scatter(parts, "tensor", scatter_dimension=0, tiled=True)[0].astype(WIDE)


def general_plan(args, dp_size, tensor_size):
    (tokens, lengths, cotangent, ln1_gain, ln1_bias, w_qkv, b_qv, b_up, w_out, b_out, ln2_gain, ln2_bias, w_up, w_down, b_down) = args
    place = jnp.zeros((1,), jnp.int32)
    own, rows_own = pack_attention(False, place, w_qkv, w_out, b_qv, b_up, w_up, w_down)
    attn = gather_shards(own, dp_size)
    both = gather_shards(jnp.concatenate([w_up, w_down], axis=1), dp_size)
    rows = lax.all_gather(rows_own, "tensor", axis=0)
    shards = range(tensor_size)
    saved = []
    for k in shards:
        *kept_here, h1 = attend(place, lengths, tokens, (rows[k], attn[k]), (ln1_gain, ln1_bias))
        saved.append(kept_here)
    grads, up_sums, r = [], [], None
    for k in range(0, tensor_size, 2):
        first, last = k == 0, k + 2 == tensor_size
        ours = both[k : k + 2]
        operands = dict(g=cotangent, up=list(ours[:, :, : w_up.shape[1]]), down=list(ours[:, :, w_up.shape[1] :]))
        operands |= dict(rows=list(rows[k : k + 2]))
        vectors = {}
        if first:
            operands |= dict(x=tokens, mixed=[v[1] for v in saved], packed=list(attn))
            vectors = dict(out_bias=b_out, gain=ln2_gain, shift=ln2_bias, down_bias=b_down)
        else:
            operands |= dict(h=h2, out_in=r.out, e_in=r.e)
        if last:
            operands |= dict(middle=middle)
            vectors |= dict(gain=ln2_gain)
        r = feed(False, (False, False), first, last, place, operands, vectors)
        if first:
            middle, h2, g_sums = r.middle_out, r.h_out, r.g_sums
        grads += [r.keep[:768], r.keep[768:]]
        up_sums.append(r.sums)
    grad_feed = reduce_shards(grads, dp_size)
    grad_middle, branch, turn_sums = r.grad_middle, r.branch, r.turn_sums
    pieces, grads, qkv_sums = [], [], []
    for k in shards:
        piece, grad, sums = attend_back(False, place, lengths, attn[k], *saved[k], branch, h1)
        pieces.append(piece)
        grads.append(grad)
        qkv_sums.append(sums)
    grad_attn = reduce_shards(grads, dp_size)
    given = [pieces, [attn[k] for k in shards], tokens, grad_middle]
    half_grad, half_sums = finish(0, *given, ln1_gain)
    input_grad, small = finish(1, *given, ln1_gain, half_grad, [half_sums, turn_sums, g_sums] + up_sums + qkv_sums)
    by_depth = small[:6].reshape(6, dp_size, tensor_size, -1).transpose(1, 2, 0, 3).reshape(dp_size, tensor_size, -1)
    lines = []
    for k in shards:
        up, qkv = small[6 + k : 7 + k], small[10 + k : 11 + k]
        lines.append(jnp.concatenate([by_depth[:, k]] + bias_rows(qkv, up, dp_size), axis=1))
    small = jnp.stack(lines, axis=1).reshape(dp_size * tensor_size, -1)
    small = lax.psum_scatter(small, ("dp", "tensor"), scatter_dimension=0, tiled=True)[0]
    return r.out, input_grad, grad_feed, grad_attn, small


def solution(mesh):
    in_specs = (
        P(("dp", "tensor"), None),
        P("dp"),
        P(("dp", "tensor"), None),
        P(),
        P(),
        P(None, None, "tensor"),
        P(None, "tensor"),
        P("tensor", None),
        P(),
        P(),
        P(),
        P(None, "tensor"),
        P("tensor"),
        P("tensor", None),
        P(),
    )
    out_specs = (
        P(("dp", "tensor"), None),
        P(("dp", "tensor"), None),
        P(("dp", "tensor")),
        P(("dp", "tensor")),
        P(None, "dp", "tensor"),
        P(None, ("tensor", "dp")),
        P("tensor", "dp"),
        P(("dp", "tensor")),
        P(("dp", "tensor")),
        P(("dp", "tensor")),
        P("dp", "tensor"),
        P(("tensor", "dp")),
        P("tensor", "dp"),
        P(("dp", "tensor")),
    )
    return jax.shard_map(
        functools.partial(per_device, mesh.shape["dp"], mesh.shape["tensor"]), mesh=mesh, in_specs=in_specs, out_specs=out_specs, check_vma=False
    )
```

```python
import functools
from types import SimpleNamespace

import jax
import jax.numpy as jnp
from jax import lax
from jax.experimental import pallas as pl
from jax.experimental.pallas import tpu as pltpu
from jax.sharding import PartitionSpec as P

HD = 64
SEQ_LEN = 592
SCALE = HD**-0.5
EPSILON = 1e-06
MASKED = -1e30
LOW = jnp.bfloat16
WIDE = jnp.float32
HEADS = 3
NN = (((1,), (0,)), ((), ()))
NT = (((1,), (1,)), ((), ()))
TN = (((0,), (0,)), ((), ()))
PI_ROOT = (2.0 / 3.141592653589793) ** 0.5


def product(left, right, dims=NN):
    return lax.dot_general(left, right, dims, preferred_element_type=WIDE)


def three_parts(value):
    first = value.astype(LOW).astype(WIDE)
    rest = value - first
    second = rest.astype(LOW).astype(WIDE)
    return first, second, rest - second


def norm_parts(values):
    center = values - jnp.mean(values, axis=-1, keepdims=True)
    inverse = lax.rsqrt(jnp.mean(center * center, axis=-1, keepdims=True) + EPSILON)
    return center * inverse, inverse


def norm_back(grad, normed, inverse, gain):
    scaled = grad * gain
    return inverse * (
        scaled
        - jnp.mean(scaled, axis=-1, keepdims=True)
        - normed * jnp.mean(scaled * normed, axis=-1, keepdims=True)
    )


def call(kernel, name, outs, grid, in_specs, out_specs, scratch=(), scalars=0, aliases=None, flops=20_000_000_000, vmem=60):
    return pl.pallas_call(
        kernel,
        out_shape=outs,
        grid_spec=pltpu.PrefetchScalarGridSpec(
            num_scalar_prefetch=scalars,
            grid=grid,
            in_specs=in_specs,
            out_specs=out_specs,
            scratch_shapes=list(scratch),
        ),
        compiler_params=pltpu.CompilerParams(vmem_limit_bytes=vmem << 20),
        cost_estimate=pl.CostEstimate(flops=flops, bytes_accessed=1, transcendentals=0),
        input_output_aliases=aliases or {},
        name=name,
    )


def whole(shape):
    zeros = (0,) * len(shape)
    return pl.BlockSpec(shape, lambda *_: zeros)


def kept(shape, dtype=LOW):
    return jax.ShapeDtypeStruct(shape, dtype)


FAR = pl.BlockSpec(memory_space=pltpu.MemorySpace.HBM)
ANYWHERE = pl.BlockSpec(memory_space=pl.ANY)


EXTRA = 8
PIECE = 96 + EXTRA


def pack_kernel(relative, place_ref, qkv_ref, out_ref, qv_ref, up_bias_ref, *refs):
    if relative:
        up_ref, down_ref, packed_ref, rows_ref, piece_ref, feed_ref, sems = refs
        part = feed_ref.shape[0]
        source = pl.ds(pl.multiple_of(place_ref[0] * part, part), part)
        copies = [
            pltpu.make_async_copy(up_ref.at[source, :], feed_ref.at[:, 0:768], sems.at[0]),
            pltpu.make_async_copy(down_ref.at[source, :], feed_ref.at[:, 768:1536], sems.at[1]),
        ]
        for copy in copies:
            copy.start()
    else:
        packed_ref, rows_ref = refs
    for j in range(3):
        packed_ref[j * 128 : (j + 1) * 128, :] = qkv_ref[j, 0:128, :]
        packed_ref[384 + j * 64 : 448 + j * 64, :] = qkv_ref[j, 128:192, :]
    packed_ref[576:640, :] = out_ref[128:192, :]
    packed_ref[640:768, :] = out_ref[0:128, :]
    query, value, nothing = qv_ref[0:1, :], qv_ref[1:2, :], jnp.zeros((1, 128), WIDE)
    ends = [jnp.concatenate([v[:, 128:192], nothing[:, :64]], axis=1) for v in (query, value)]
    qv = jnp.concatenate([query[:, :128], nothing, value[:, :128], *ends, nothing], axis=1)
    rows = three_parts(qv) + three_parts(up_bias_ref[...][None])
    rows = jnp.concatenate(list(rows) + [jnp.zeros((2, 768), WIDE)], axis=0).astype(LOW)
    rows_ref[...] = rows
    if relative:
        start = pl.multiple_of(place_ref[0] * 96, 96)
        piece_ref[0:96, :] = packed_ref[pl.ds(start, 96), :]
        piece_ref[96:PIECE, :] = rows
        for copy in copies:
            copy.wait()


def pack_attention(relative, place, w_qkv, w_out, b_qv, b_up, w_up, w_down):
    depth = w_out.shape[1]
    outs = [kept((768, depth)), kept((EXTRA, depth))]
    operands = [w_qkv.transpose(0, 2, 1), w_out, b_qv, b_up]
    in_specs = [whole(v.shape) for v in operands]
    if relative:
        outs += [kept((PIECE, depth)), kept((96, 1536))]
        operands += [w_up, w_down]
        in_specs += [FAR] * 2
    return call(
        functools.partial(pack_kernel, relative),
        "pack",
        outs,
        (1,),
        in_specs,
        [whole(o.shape) for o in outs],
        [pltpu.SemaphoreType.DMA((2,))] if relative else [],
        scalars=1,
    )(place, *operands)


def bias_of(rows, first):
    parts = [rows[first + j : first + j + 1].astype(WIDE) for j in range(3)]
    return parts[0] + parts[1] + parts[2]


def unpack_attention(grads):
    q01, k01, v01, q2, k2, v2, o2, o01 = (
        grads[:, a:b]
        for a, b in ((0, 128), (128, 256), (256, 384), (384, 448), (448, 512), (512, 576), (576, 640), (640, 768))
    )
    stacked = [jnp.concatenate(pair, axis=1) for pair in ((q01, q2), (k01, k2), (v01, v2), (o01, o2))]
    return jnp.stack(stacked[:3]), stacked[3].T


def gelu_both(u):
    square = u * u
    t = jnp.tanh(PI_ROOT * u * (1.0 + 0.044715 * square))
    half = 0.5 * (1.0 + t)
    slope = half + (0.5 * PI_ROOT) * u * (1.0 - t * t) * (1.0 + (3 * 0.044715) * square)
    return u * half, slope


def spare_lane(upper):
    return 0 if upper else 64


def turn_halves(tile):
    return jnp.concatenate([tile[:, 64:128], tile[:, 0:64]], axis=1)


def head_tiles(proj, head):
    if head < 2:
        return proj[:, 0:128], proj[:, 128:256], proj[:, 256:384]
    both = proj[:, 384:512]
    return both, turn_halves(both), proj[:, 512:640]


class Copies:
    def __init__(self, sems):
        self.sems = sems
        self.used = 0
        self.saves = []

    def new(self, source, target):
        self.used += 1
        return pltpu.make_async_copy(source, target, self.sems.at[self.used - 1])

    def load(self, *pairs):
        copies = [self.new(*pair) for pair in pairs]
        for copy in copies:
            copy.start()
        return copies

    def save(self, source, target):
        self.saves += self.load((source, target))

    def finish(self):
        for copy in self.saves:
            copy.wait()


def wait_all(copies):
    for copy in copies:
        copy.wait()


def attend_kernel(stride, offset, place_ref, live_ref, *refs):
    if stride:
        h_ref, near_ref, far_ref, proj_ref, mixed_ref, log_ref, weights_ref, rows_ref, sems = refs

        @pl.when(pl.program_id(0) == 0)
        def _():
            copies = []
            for base, ref in ((0, near_ref), (1, far_ref)):
                for number in range(4):
                    start = pl.multiple_of((place_ref[0] ^ (2 * number + base)) * 96, 96)
                    source = ref.at[pl.ds(number * stride + offset, 96), :]
                    copies.append((source, weights_ref.at[pl.ds(start, 96), :]))
            copies.append((near_ref.at[pl.ds(offset + 96, EXTRA), :], rows_ref))
            copies = [pltpu.make_async_copy(*c, sems.at[j]) for j, c in enumerate(copies)]
            for copy in copies:
                copy.start()
            for copy in copies:
                copy.wait()

        h = h_ref[...]
    else:
        x_ref, gain_ref, shift_ref, rows_ref, weights_ref, proj_ref, mixed_ref, log_ref, h_ref = refs
        normed, _ = norm_parts(x_ref[...].astype(WIDE))
        h = (normed * gain_ref[...][None] + shift_ref[...][None]).astype(LOW)
        h_ref[...] = h
    live = live_ref[pl.program_id(0)]
    proj = (product(h, weights_ref[0:576, :], NT) + bias_of(rows_ref[...], 0)[:, :576]).astype(LOW)
    proj = jnp.concatenate([proj, jnp.zeros((SEQ_LEN, 64), LOW)], axis=1)
    proj_ref[...] = proj
    lane = lax.broadcasted_iota(jnp.int32, (1, 128), 1)
    row = lax.broadcasted_iota(jnp.int32, (SEQ_LEN, 1), 0)
    side = lax.broadcasted_iota(jnp.int32, (128, 1), 0)
    mask = jnp.where(row < live, 0.0, MASKED).astype(LOW)
    mixed = []
    for head in range(HEADS):
        upper = head == 1
        own = (lane >= 64) if upper else (lane < 64)
        spare = spare_lane(upper)
        query, keys, values = head_tiles(proj, head)
        query = query * jnp.asarray(SCALE, LOW)
        zero, one = jnp.zeros_like(query), jnp.ones_like(query)
        query = jnp.where(own, query, jnp.where(lane == spare, one, zero))
        keys = jnp.where(own, keys, jnp.where(lane == spare, mask, zero))
        values = jnp.where(own, values, jnp.where(lane == spare, one, zero))
        scores = product(keys, query, NT)
        highest = jnp.max(scores, axis=0, keepdims=True)
        weights = jnp.exp(scores - highest).astype(LOW)
        summed = product(values, weights, TN)
        spent = summed[spare : spare + 1, :]
        log_ref[head : head + 1, :] = highest + jnp.log(spent)
        mixed.append(summed * (1.0 / spent))
    first = jnp.where(side < 64, mixed[0], mixed[1]).astype(LOW).T
    third = jnp.where(side < 64, mixed[2], 0.0)
    third = jnp.concatenate([third[64:], third[:64]], axis=0).astype(LOW).T
    mixed_ref[...] = jnp.concatenate([third, first], axis=1)


def attend(place, lengths, rows_in, weights, norm=None, stride=0, offset=0):
    count, depth = rows_in.shape
    seqs = count // SEQ_LEN
    rows = lambda width: pl.BlockSpec((SEQ_LEN, width), lambda i, *_: (i, 0))
    logs = pl.BlockSpec((None, HEADS, SEQ_LEN), lambda i, *_: (i, 0, 0))
    outs = [kept((count, 640)), kept((count, 256)), kept((seqs, HEADS, SEQ_LEN), WIDE)]
    out_specs = [rows(640), rows(256), logs]
    in_specs, operands, scratch = [rows(depth)], [rows_in], []
    if stride:
        outs += [kept((768, depth)), kept((EXTRA, depth))]
        out_specs += [whole((768, depth)), whole((EXTRA, depth))]
        scratch = [pltpu.SemaphoreType.DMA((9,))]
        in_specs += [FAR, ANYWHERE]
    else:
        outs.append(kept((count, depth)))
        out_specs.append(rows(depth))
        in_specs += [whole((depth,))] * 2 + [whole((EXTRA, depth)), whole((768, depth))]
        operands += norm
    return call(
        functools.partial(attend_kernel, stride, offset),
        "attend",
        outs,
        (seqs,),
        in_specs,
        out_specs,
        scratch,
        scalars=2,
    )(place, lengths, *operands, *weights)


def attend_back_kernel(relative, place_ref, live_ref, weights_ref, proj_ref, mixed_ref, log_ref, branch_ref, h_ref, *refs):
    if relative:
        packed_ref, keep_ref, send_ref, sums_ref, *scratch = refs
    else:
        packed_ref, keep_ref, sums_ref, *scratch = refs
    weights_v, proj_v, branch_v, h_v, held_v, turned_v, sems = scratch
    copies = Copies(sems)
    tiles = [slice(a, a + SEQ_LEN) for a in range(0, h_v.shape[0], SEQ_LEN)]
    weights_loads = copies.load((weights_ref, weights_v))
    row_loads = [
        copies.load(
            (branch_ref.at[rows, :], branch_v.at[rows, :]),
            (proj_ref.at[rows, :], proj_v.at[rows, :]),
            (mixed_ref.at[rows, :], held_v.at[rows, 640:896]),
        )
        for rows in tiles
    ]
    h_loads = copies.load((h_ref, h_v))
    lane = lax.broadcasted_iota(jnp.int32, (1, 128), 1)
    row = lax.broadcasted_iota(jnp.int32, (SEQ_LEN, 1), 0)
    wait_all(weights_loads)
    sums = None
    for seq, rows in enumerate(tiles):
        wait_all(row_loads[seq])
        mask = jnp.where(row < live_ref[seq], 0.0, MASKED).astype(LOW)
        proj = proj_v[rows]
        mixed = held_v[rows, 640:896]
        grad_mixed = product(branch_v[rows], weights_v[512:768, :], NT).astype(LOW)
        totals = []
        for head in range(HEADS):
            upper = head == 1
            own = (lane >= 64) if upper else (lane < 64)
            spare = spare_lane(upper)
            query, keys, values = head_tiles(proj, head)
            if head < 2:
                grad, held = grad_mixed[:, 128:256], mixed[:, 128:256]
            else:
                grad, held = turn_halves(grad_mixed), turn_halves(mixed)
            query = query * jnp.asarray(SCALE, LOW)
            zero, one = jnp.zeros_like(query), jnp.ones_like(query)
            grad = jnp.where(own, grad, zero)
            wide_grad = grad.astype(WIDE)
            inner = jnp.sum(wide_grad * held.astype(WIDE), axis=-1, keepdims=True)
            parts = three_parts(-inner)
            shifted = wide_grad
            for place in range(3):
                shifted = jnp.where(lane == spare + place, parts[place], shifted)
            masked_query = jnp.where(own, query, jnp.where(lane == spare, one, zero))
            masked_keys = jnp.where(own, keys, jnp.where(lane == spare, mask, zero))
            spread_values = jnp.where(own, values, jnp.where((lane >= spare) & (lane < spare + 3), one, zero))
            probs = jnp.exp(product(masked_keys, masked_query, NT) - log_ref[seq, head : head + 1, :])
            centred = product(spread_values, shifted.astype(LOW), NT)
            grad_scores = (probs * centred).astype(LOW)
            parts = (
                (product(jnp.where(own, keys, zero), grad_scores, TN) * SCALE).astype(LOW).T,
                product(grad_scores, jnp.where(own, query, zero)).astype(LOW),
                product(probs.astype(LOW), grad).astype(LOW),
            )
            totals.append(parts)
        pair = [a + b for a, b in zip(totals[0], totals[1])]
        gq, gk, gv = totals[2]
        packed = jnp.concatenate(pair + [gq + turn_halves(gk), gv], axis=1)
        held_v[rows, 0:640] = packed
        copies.save(held_v.at[rows, 0:640], packed_ref.at[rows, :])
        part = jnp.sum(packed.astype(WIDE), axis=0, keepdims=True)
        sums = part if sums is None else sums + part
    sums_ref[...] = sums
    wait_all(h_loads)
    grads = product(h_v[...], held_v[:, 0:640], TN)
    outs = product(branch_v[...], held_v[:, 640:896], TN)
    full = jnp.concatenate([grads[:, :512], grads[:, 512:] + outs[:, :128], outs[:, 128:]], axis=1).astype(LOW)
    if relative:
        store_turned(place_ref, full, turned_v, slice(0, 768))
        copies.save(turned_v.at[384:768, :], send_ref)
        copies.save(turned_v.at[0:384, :], keep_ref)
    else:
        turned_v[...] = full
        copies.save(turned_v, keep_ref)
    copies.finish()


def store_turned(place_ref, values, target, columns):
    part = values.shape[0] // 8
    for block in range(8):
        other = place_ref[0] ^ block
        start = ((other & 1) * 4 + (other >> 1)) * part
        target[pl.ds(pl.multiple_of(start, part), part), columns] = values[block * part : (block + 1) * part]


def attend_back(relative, place, lengths, weights, proj, mixed, logs_in, branch, h):
    count, depth = branch.shape
    half = 384 if relative else 768
    outs = [kept((count, 640))] + [kept((half, 768))] * (2 if relative else 1) + [kept((1, 640), WIDE)]
    return call(
        functools.partial(attend_back_kernel, relative),
        "attend_back",
        outs,
        (1,),
        [FAR] * 3 + [whole(logs_in.shape)] + [FAR] * 2,
        [FAR] * (len(outs) - 1) + [whole((1, 640))],
        [
            pltpu.VMEM((768, depth), LOW),
            pltpu.VMEM((count, 640), LOW),
            pltpu.VMEM((count, depth), LOW),
            pltpu.VMEM((count, depth), LOW),
            pltpu.VMEM((count, 896), LOW),
            pltpu.VMEM((768, 768), LOW),
            pltpu.SemaphoreType.DMA((16,)),
        ],
        scalars=2,
        vmem=52,
    )(place, lengths, weights, proj, mixed, logs_in, branch, h)


def feed_kernel(tree, loaded, relative, first, last, place_ref, *refs):
    r = SimpleNamespace(**jax.tree.unflatten(tree, refs))
    count, depth = r.h_v.shape
    tiles = [slice(a, a + SEQ_LEN) for a in range(0, count, SEQ_LEN)]
    sems = r.sems
    used = [0]

    def copy(source, target):
        used[0] += 1
        return pltpu.make_async_copy(source, target, sems.at[used[0] - 1])

    shards = range(len(loaded))
    loads, ends = [], []
    for j, pieces in enumerate(loaded):
        both = r.both_v.at[j]
        mine = [copy(r.rows[j], r.rows_v.at[j])]
        if not pieces:
            mine += [copy(r.up[j], both.at[:, 0:768]), copy(r.down[j], both.at[:, 768:1536])]
        else:
            for base, ref in ((0, r.near[j]), (1, r.far[j])):
                for number in range(4):
                    start = pl.multiple_of((place_ref[0] ^ (2 * number + base)) * 96, 96)
                    mine.append(copy(ref.at[pl.ds(number * 96, 96), :], both.at[pl.ds(start, 96), :]))
        loads.append(mine)
    g_load = copy(r.g, r.g_v)

    def begin_save(*copies):
        for c in copies:
            c.start()
        ends.extend(copies)

    late = []
    if first:
        begin = [copy(r.x, r.x_v)]
        for k in range(4):
            begin.append(copy(r.mixed[k], r.mixed_v.at[k]))
            begin.append(copy(r.packed[k].at[512:768, :], r.out_v.at[k]))
    else:
        begin = [copy(r.h, r.h_v)]
        late = [copy(r.out_in, r.out_v), copy(r.e_in, r.e_v)]
    if last and not first:
        late.append(copy(r.middle, r.middle_v))
    for c in begin + loads[0] + [g_load] + late + [c for mine in loads[1:] for c in mine]:
        c.start()
    for c in begin:
        c.wait()
    if first:
        for rows in tiles:
            middle = r.x_v[rows].astype(WIDE) + r.out_bias[...][None]
            for k in range(4):
                middle = middle + product(r.mixed_v[k, rows, :], r.out_v[k])
            r.middle_v[rows] = middle
            normed, _ = norm_parts(middle)
            r.h_v[rows] = (normed * r.gain[...][None] + r.shift[...][None]).astype(LOW)
        begin_save(copy(r.middle_v, r.middle_out), copy(r.h_v, r.h_out))
    g_load.wait()
    h, g = r.h_v, r.g_v
    for j in shards:
        both, hidden_v, preact_v = r.both_v.at[j], r.hidden_v.at[j], r.preact_v.at[j]
        for c in loads[j]:
            c.wait()
        bias = bias_of(r.rows_v[j], 3)
        for a in range(0, 768, 768):
            b = a + 768
            sums = None
            for rows in tiles:
                preact = product(h[rows], both[:, a:b]) + bias[:, a:b]
                hidden, slope = gelu_both(preact)
                hidden_v[rows, a:b] = hidden.astype(LOW)
                grad = (product(g[rows], both[a:b, 768:1536], NT) * slope).astype(LOW)
                preact_v[rows, a:b] = grad
                part = jnp.sum(grad.astype(WIDE), axis=0, keepdims=True)
                sums = part if sums is None else sums + part
            r.sums[j : j + 1, a:b] = sums
    for c in late:
        c.wait()
    total_v, e_v = r.total_v, r.e_v
    for rows in tiles:
        total = r.middle_v[rows] + r.down_bias[...][None] if first else r.out_v[rows]
        e = None if first else e_v[rows]
        for j in shards:
            total = total + product(r.hidden_v[j, rows, :], r.both_v[j, :, 768:1536])
            term = product(r.preact_v[j, rows, :], r.both_v[j, :, 0:768], NT)
            e = term if e is None else e + term
        total_v[rows] = total.astype(total_v.dtype)
        e_v[rows] = e
    begin_save(copy(total_v, r.out))
    if not last:
        begin_save(copy(e_v, r.e))
    if last:
        totals = [0.0] * 3
        for rows in tiles:
            grad_h = e_v[rows]
            normed, inverse = norm_parts(r.middle_v[rows])
            grad = g[rows].astype(WIDE) + norm_back(grad_h, normed, inverse, r.gain[...][None])
            r.middle_v[rows] = grad
            r.branch_v[rows] = grad.astype(LOW)
            terms = (grad_h * normed, grad_h, grad)
            totals = [t + jnp.sum(v, axis=0, keepdims=True) for t, v in zip(totals, terms)]
        for number, total in enumerate(totals):
            r.turn_sums[number : number + 1, :] = total
        begin_save(copy(r.middle_v, r.grad_middle), copy(r.branch_v, r.branch))
    if first:
        r.g_sums[...] = jnp.sum(g[...].astype(WIDE), axis=0, keepdims=True)
    half = 384 if relative else 768
    for j in shards:
        turned = r.turned_v.at[j]
        for columns, left, right in ((slice(0, 768), h, r.preact_v), (slice(768, 1536), g, r.hidden_v)):
            grads = product(left[...], right[j], TN).astype(LOW)
            if relative:
                store_turned(place_ref, grads, turned, columns)
            else:
                turned[:, columns] = grads
        place = pl.ds(j * half, half)
        if relative:
            begin_save(copy(turned.at[384:768, :], r.send.at[place, :]))
        begin_save(copy(turned.at[0:half, :], r.keep.at[place, :]))
    for c in ends:
        c.wait()


def feed(relative, loaded, first, last, place, operands, vectors):
    count, depth = operands["g"].shape
    shards = len(loaded)
    half = 384 if relative else 768
    rows = (count, depth)
    big = dict(out=kept(rows, LOW if last else WIDE), keep=kept((shards * half, 1536)))
    if first:
        big |= dict(middle_out=kept(rows, WIDE), h_out=kept(rows))
    if last:
        big |= dict(grad_middle=kept(rows, WIDE), branch=kept(rows))
    else:
        big |= dict(e=kept(rows, WIDE))
    if relative:
        big |= dict(send=kept((shards * half, 1536)))
    small = dict(sums=kept((shards, 768), WIDE))
    if first:
        small |= dict(g_sums=kept((1, depth), WIDE))
    if last:
        small |= dict(turn_sums=kept((3, depth), WIDE))
    scratch = dict(
        h_v=pltpu.VMEM(rows, LOW),
        g_v=pltpu.VMEM(rows, LOW),
        hidden_v=pltpu.VMEM((shards, count, 768), LOW),
        preact_v=pltpu.VMEM((shards, count, 768), LOW),
        both_v=pltpu.VMEM((shards, depth, 1536), LOW),
        rows_v=pltpu.VMEM((shards, EXTRA, depth), LOW),
        turned_v=pltpu.VMEM((shards, 768, 1536), LOW),
        total_v=pltpu.VMEM(rows, LOW if last else WIDE),
        e_v=pltpu.VMEM(rows, WIDE),
        sems=pltpu.SemaphoreType.DMA((48,)),
    )
    if first:
        scratch |= dict(
            x_v=pltpu.VMEM(rows, LOW),
            mixed_v=pltpu.VMEM((4, count, 256), LOW),
            out_v=pltpu.VMEM((4, 256, depth), LOW),
        )
    else:
        scratch |= dict(out_v=pltpu.VMEM(rows, WIDE))
    if first or last:
        scratch |= dict(middle_v=pltpu.VMEM(rows, WIDE))
    if last:
        scratch |= dict(branch_v=pltpu.VMEM(rows, LOW))
    parts = [operands, vectors, big, small, scratch]
    flat = [jax.tree.flatten(part) for part in parts]
    numbers = iter(range(sum(len(leaves) for leaves, _ in flat)))
    order = {}
    for (leaves, tree) in flat:
        order |= jax.tree.unflatten(tree, [next(numbers) for _ in leaves])
    places, tree = jax.tree.flatten(order)

    def kernel(*refs):
        refs = refs[:1] + tuple(refs[1 + place] for place in places)
        feed_kernel(tree, loaded, relative, first, last, *refs)

    outs = flat[2][0] + flat[3][0]
    results = call(
        kernel,
        "feed",
        outs,
        (1,),
        [FAR] * len(flat[0][0]) + [whole(v.shape) for v in flat[1][0]],
        [FAR] * len(flat[2][0]) + [whole(o.shape) for o in flat[3][0]],
        flat[4][0],
        scalars=1,
    )(place, *flat[0][0], *flat[1][0])
    named = jax.tree.unflatten(flat[2][1], results[: len(big)]) | jax.tree.unflatten(flat[3][1], results[len(big) :])
    return SimpleNamespace(**named)


def finish_kernel(shards, joined, last, *refs):
    packed, weights = refs[:shards], refs[shards : 2 * shards]
    x_ref, grad_ref, gain_ref = refs[2 * shards : 2 * shards + 3]
    refs = refs[2 * shards + 3 :]
    if joined:
        refs = refs[1:]
    if last:
        before_ref, turn_ref, g_ref, *refs = refs
        ups, refs = refs[: shards // 2], refs[shards // 2 :]
        qkvs, refs = refs[:shards], refs[shards:]
    out_ref, sums_ref = refs
    grad_h = None
    for p, w in zip(packed, weights):
        term = product(p[...], w[...])
        grad_h = term if grad_h is None else grad_h + term
    normed, inverse = norm_parts(x_ref[...].astype(WIDE))
    out_ref[...] = (grad_ref[...] + norm_back(grad_h, normed, inverse, gain_ref[...][None])).astype(LOW)
    first = jnp.sum(grad_h * normed, axis=0, keepdims=True)
    second = jnp.sum(grad_h, axis=0, keepdims=True)
    if not last:
        sums_ref[0:1, :] = first
        sums_ref[1:2, :] = second
        return
    sums_ref[0:1, :] = first + before_ref[0:1, :]
    sums_ref[1:2, :] = second + before_ref[1:2, :]
    sums_ref[2:5, :] = turn_ref[...]
    sums_ref[5:6, :] = g_ref[...]
    for j, ref in enumerate(ups):
        sums_ref[6 + 2 * j : 8 + 2 * j, :] = ref[...]
    for j, ref in enumerate(qkvs):
        row = 6 + shards + j
        sums_ref[row : row + 1, 0:640] = ref[...]
        sums_ref[row : row + 1, 640:] = jnp.zeros_like(sums_ref[row : row + 1, 640:])
    sums_ref[6 + 2 * shards :, :] = jnp.zeros_like(sums_ref[6 + 2 * shards :, :])


def finish(tile, packed, weights, tokens, grad_middle, gain, joined=None, sums=()):
    count, depth = tokens.shape
    shards = len(packed)
    last = (tile + 1) * SEQ_LEN == count
    rows = lambda width: pl.BlockSpec((SEQ_LEN, width), lambda i: (tile, 0))
    operands = [*packed, *weights, tokens, grad_middle, gain]
    in_specs = [rows(640)] * shards + [pl.BlockSpec((640, depth), lambda i: (0, 0))] * shards
    in_specs += [rows(depth)] * 2 + [whole((depth,))]
    aliases = None
    if joined is not None:
        aliases = {len(operands): 0}
        operands.append(joined)
        in_specs.append(FAR)
    if last:
        operands += sums
        in_specs += [whole(v.shape) for v in sums]
    return call(
        functools.partial(finish_kernel, shards, joined is not None, last),
        "finish",
        (kept((count, depth)), kept((16 if last else 2, depth), WIDE)),
        (1,),
        in_specs,
        [rows(depth), whole((16 if last else 2, depth))],
        aliases=aliases,
    )(*operands)


def fold_kernel(pairs, plan, *refs):
    keeps, gots, refs = refs[:pairs], refs[pairs : 2 * pairs], refs[2 * pairs :]
    out_refs, refs = refs[: len(plan)], refs[len(plan) :]
    keep_vs, got_vs, sems = refs[:pairs], refs[pairs : 2 * pairs], refs[2 * pairs]
    work = []
    for out_ref, (pair, blocks) in zip(out_refs, plan):
        part = keep_vs[pair].shape[1]
        for place, block in enumerate(blocks):
            rows = pl.ds(block * part, part)
            keep_v, got_v = keep_vs[pair].at[block], got_vs[pair].at[block]
            sem = 3 * len(work)
            loads = [
                pltpu.make_async_copy(keeps[pair].at[rows, :], keep_v, sems.at[sem]),
                pltpu.make_async_copy(gots[pair].at[rows, :], got_v, sems.at[sem + 1]),
            ]
            end = pltpu.make_async_copy(keep_v, out_ref.at[pl.ds(place * part, part), :], sems.at[sem + 2])
            for copy in loads:
                copy.start()
            work.append((keep_v, got_v, loads, end))
    for keep_v, got_v, loads, end in work:
        for copy in loads:
            copy.wait()
        keep_v[...] = (keep_v[...].astype(WIDE) + got_v[...].astype(WIDE)).astype(LOW)
        end.start()
    for *_, end in work:
        end.wait()


def fold(pairs, plan, part=96):
    shapes = [(keep.shape[0] // part, part, keep.shape[1]) for keep, _ in pairs]
    count = sum(len(blocks) for _, blocks in plan)
    return call(
        functools.partial(fold_kernel, len(pairs), plan),
        "fold",
        [kept((len(blocks) * part, pairs[pair][0].shape[1])) for pair, blocks in plan],
        (1,),
        [FAR] * len(pairs) + [ANYWHERE] * len(pairs),
        [FAR] * len(plan),
        [pltpu.VMEM(shape, LOW) for shape in shapes] * 2 + [pltpu.SemaphoreType.DMA((3 * count,))],
        flops=1,
        vmem=24 if sum(keep.size for keep, _ in pairs) > 1_000_000 else 60,
    )(*[keep for keep, _ in pairs], *[got for _, got in pairs])


def hop(value, mask, size=8):
    return lax.ppermute(value, "dp", [(i, i ^ mask) for i in range(size)])


def ring(value, shift, size=4):
    return lax.ppermute(value, "tensor", [(i, (i + shift) % size) for i in range(size)])


def together(*values):
    return lax.optimization_barrier(values)


def add_up(*parts):
    total = parts[0].astype(WIDE)
    for part in parts[1:]:
        total = total + part.astype(WIDE)
    return total


def bias_rows(qkv_sums, up_sums, parts):
    sums = qkv_sums[0]
    query = jnp.concatenate([sums[:128], sums[384:448]])
    value = jnp.concatenate([sums[256:384], sums[512:576]])
    return [v.reshape(parts, -1) for v in (query, value, up_sums)]


def closed(first):
    return [first, hop(first, 2), hop(first, 4), hop(first, 6)]


def joined_rows(parts):
    return jnp.concatenate(parts, axis=0)


MASK = {"x": 2, "y": 4}
SHIFTS = (0, 1, 3, 2)
OTHER = {"x": "y", "y": "x"}
FIRST = {"x": ((0, 2), (1, 3)), "y": ((0, 1), (2, 3))}


class Leaving:
    def __init__(self):
        self.live = []
        self.done = {}
        self.rings = []
        self.late = []

    def add(self, shards, keep, send):
        self.live.append((shards, 0, keep, hop(send, 1)))

    def step(self, *tied):
        arrays = [v for item in self.live for v in item[2:]]
        results = together(*tied, *arrays, *[self.done[name] for name in self.rings])
        tied, results = results[: len(tied)], results[len(tied) :]
        arrays, ended = results[: len(arrays)], results[len(arrays) :]
        self.done |= dict(zip(self.rings, ended))
        self.rings = []
        pairs = list(zip(arrays[0::2], arrays[1::2]))
        plan, follow = [], []
        for number, (shards, stage, *_) in enumerate(self.live):
            for place, shard in enumerate(shards):
                lists = [(0,), (1,)] if stage == 1 else [(0,)]
                if stage == 0:
                    lists = [tuple(4 * place + b for b in blocks) for blocks in FIRST[shard[1]]]
                follow.append((shard, stage, len(plan)))
                plan += [(number, blocks) for blocks in lists]
        held = [self.late.pop(0)] if self.late else []
        results = together(*tied, *[v for _, _, v in held], *fold(pairs, plan))
        tied, results = results[: len(tied)], results[len(tied) :]
        for (name, shift, _), value in zip(held, results):
            self.done[name] = ring(value, -shift)
            self.rings.append(name)
        results = results[len(held) :]
        self.live = []
        for shard, stage, place in follow:
            name, axis, shift = shard
            if stage < 2:
                mask = MASK[axis if stage == 0 else OTHER[axis]]
                self.live.append(((shard,), stage + 1, results[place], hop(results[place + 1], mask)))
            elif not shift:
                self.done[name] = results[place]
            elif name in (2, 7):
                self.late.append((name, shift, results[place]))
            else:
                self.done[name] = ring(results[place], -shift)
                self.rings.append(name)
        return tied


def direct_plan(args):
    (tokens, lengths, cotangent, ln1_gain, ln1_bias, w_qkv, b_qv, b_up, w_out, b_out, ln2_gain, ln2_bias, w_up, w_down, b_down) = args
    index = lax.axis_index("dp")
    place = index[None]
    own, rows_own, piece, feed_piece = pack_attention(True, place, w_qkv, w_out, b_qv, b_up, w_up, w_down)
    attn_at = {j: ring(piece, SHIFTS[j]) for j in (1, 2)}
    feed_at = {}

    packed, saved, rows = {0: own}, {}, {0: rows_own}
    *saved[0], h1 = attend(place, lengths, tokens, (rows_own, own), (ln1_gain, ln1_bias))
    h1, attn_at[1], attn_at[2], piece, feed_piece = together(h1, attn_at[1], attn_at[2], piece, feed_piece)
    near1 = joined_rows(closed(attn_at[1]))
    attn_at[3] = ring(piece, SHIFTS[3])
    feed_at[3] = ring(feed_piece, SHIFTS[3])
    near1, attn_at[2], attn_at[3], feed_piece = together(near1, attn_at[2], attn_at[3], feed_piece)
    far1 = hop(near1, 1)
    near2 = joined_rows(closed(attn_at[2]))
    near1, near2, attn_at[3], far1, feed_at[3], feed_piece, h1 = together(
        near1, near2, attn_at[3], far1, feed_at[3], feed_piece, h1
    )
    far2 = hop(near2, 1)
    close3 = closed(attn_at[3])
    feed_at[1] = ring(feed_piece, SHIFTS[1])
    *saved[1], packed[1], rows[1] = attend(place, lengths, h1, (near1, far1), None, PIECE, 0)
    h1, saved[1][0], far2, feed_at[1], feed_piece, *close3 = together(
        h1, saved[1][0], far2, feed_at[1], feed_piece, *close3
    )
    feed_at[2] = ring(feed_piece, SHIFTS[2])
    near3 = joined_rows(close3)
    near3, h1, feed_at[1] = together(near3, h1, feed_at[1])
    far3 = hop(near3, 1)
    feed1 = closed(feed_at[1])
    *saved[2], packed[2], rows[2] = attend(place, lengths, h1, (near2, far2), None, PIECE, 0)
    h1, saved[2][0], far3, feed_at[2], *feed1 = together(h1, saved[2][0], far3, feed_at[2], *feed1)
    feed_near1 = joined_rows(feed1)
    feed_near1, h1, feed_at[2] = together(feed_near1, h1, feed_at[2])
    feed_far1 = hop(feed_near1, 1)
    feed2 = closed(feed_at[2])
    *saved[3], packed[3], rows[3] = attend(place, lengths, h1, (near3, far3), None, PIECE, 0)
    saved[3][1], feed_far1, *feed2 = together(saved[3][1], feed_far1, *feed2)
    feed_near2 = joined_rows(feed2)
    feed_near2, feed_at[3], saved[3][1] = together(feed_near2, feed_at[3], saved[3][1])
    feed_far2 = hop(feed_near2, 1)
    feed3 = closed(feed_at[3])

    operands = dict(x=tokens, g=cotangent, up=[w_up], down=[w_down], rows=[rows[0], rows[1]])
    operands |= dict(near=[None, feed_near1], far=[None, feed_far1])
    operands |= dict(mixed=[saved[k][1] for k in range(4)], packed=[packed[k] for k in range(4)])
    vectors = dict(out_bias=b_out, gain=ln2_gain, shift=ln2_bias, down_bias=b_down)
    r = feed(True, (False, True), True, False, place, operands, vectors)
    middle, h2, g_sums, up_sums = r.middle_out, r.h_out, r.g_sums, [r.sums]
    h2, feed_far2, *feed3 = together(h2, feed_far2, *feed3)
    feed_near3 = joined_rows(feed3)
    feed_far3 = hop(feed_near3, 1)
    leaving = Leaving()
    leaving.add(((0, "x", 0), (1, "y", SHIFTS[1])), r.keep, r.send)
    operands = dict(h=h2, g=cotangent, out_in=r.out, e_in=r.e, middle=middle, rows=[rows[2], rows[3]])
    operands |= dict(near=[feed_near2, feed_near3], far=[feed_far2, feed_far3])
    r = feed(True, (True, True), False, True, place, operands, dict(gain=ln2_gain))
    block_output, grad_middle, branch, turn_sums = r.out, r.grad_middle, r.branch, r.turn_sums
    up_sums.append(r.sums)

    pieces, qkv_sums = {}, {}

    (branch,) = leaving.step(branch)
    leaving.add(((2, "x", SHIFTS[2]), (3, "y", SHIFTS[3])), r.keep, r.send)
    for k in (3, 2, 1, 0):
        pieces[k], keep, send, qkv_sums[k] = attend_back(
            True, place, lengths, packed[k], *saved[k], branch, h1
        )
        branch, pieces[k] = leaving.step(branch, pieces[k])
        leaving.add(((4 + k, "y" if k % 2 else "x", SHIFTS[k]),), keep, send)
    given = [[v[k] for k in range(4)] for v in (pieces, packed)] + [tokens, grad_middle]
    half_grad, half_sums = finish(0, *given, ln1_gain)
    half_grad, half_sums = leaving.step(half_grad, half_sums)
    grad_feed = add_up(*[leaving.done[k] for k in range(4)])
    line = [half_sums, turn_sums, g_sums] + up_sums + [qkv_sums[k] for k in range(4)]
    input_grad, small = finish(1, *given, ln1_gain, half_grad, line)
    input_grad, small = leaving.step(input_grad, small)
    small = small + hop(small, 1)
    leaving.step()
    small = add_up(small, hop(small, 2), hop(small, 4), hop(small, 6))
    others = [ring(small, -SHIFTS[k]) for k in (1, 2, 3)]
    grad_attn = add_up(*[leaving.done[4 + k] for k in range(4)])
    small = jnp.concatenate(
        [
            add_up(small[:6], *[o[:6] for o in others]),
            add_up(small[6:7], *[o[6 + k : 7 + k] for k, o in zip((1, 2, 3), others)]),
            add_up(small[10:11], *[o[10 + k : 11 + k] for k, o in zip((1, 2, 3), others)]),
        ]
    )
    share = tokens.shape[1] // 32
    by_depth = lax.dynamic_slice_in_dim(small[:6], (index * 4 + lax.axis_index("tensor")) * share, share, 1)
    rest = [lax.dynamic_index_in_dim(v, index, 0, keepdims=False) for v in bias_rows(small[7:8], small[6:7], 8)]
    return block_output, input_grad, grad_feed, grad_attn, jnp.concatenate([by_depth.reshape(-1)] + rest)


def per_device(dp_size, tensor_size, tokens, lengths, cotangent, ln1_gain, ln1_bias, w_qkv, b_qv, w_out, b_out, ln2_gain, ln2_bias, w_up, b_up, w_down, b_down):
    count, depth = tokens.shape
    seqs = count // SEQ_LEN
    lengths = lax.dynamic_slice_in_dim(lengths, lax.axis_index("tensor") * seqs, seqs, 0)
    args = (tokens, lengths, cotangent, ln1_gain, ln1_bias, w_qkv, b_qv, b_up, w_out, b_out, ln2_gain, ln2_bias, w_up, w_down, b_down)
    if (dp_size, tensor_size) == (8, 4):
        results = direct_plan(args)
    else:
        results = general_plan(args, dp_size, tensor_size)
    block_output, input_grad, grad_feed, grad_attn, small = results
    order = (0, 1, 4, 2, 3, 5)
    width = w_up.shape[1]
    grad_qkv, grad_out = unpack_attention(grad_attn)
    share = depth // (dp_size * tensor_size)
    vectors = small[: 6 * share].reshape(6, share)
    rest = small[6 * share :]
    own = w_qkv.shape[2] // dp_size
    return (
        block_output,
        input_grad,
        vectors[order[0]],
        vectors[order[1]],
        grad_qkv,
        rest[: 2 * own].reshape(2, own),
        grad_out,
        vectors[order[2]],
        vectors[order[3]],
        vectors[order[4]],
        grad_feed[:, :width],
        rest[2 * own :],
        grad_feed[:, width:].T,
        vectors[order[5]],
    )


def gather_shards(shard, dp_size):
    rows, columns = shard.shape
    part = rows // dp_size
    own = lax.dynamic_slice_in_dim(shard, lax.axis_index("dp") * part, part, 0)
    parts = lax.all_gather(own, ("dp", "tensor"), axis=0)
    parts = parts.reshape(dp_size, -1, part, columns).transpose(1, 0, 2, 3)
    return parts.reshape(-1, rows, columns)


def reduce_shards(partials, dp_size):
    rows, columns = partials[0].shape
    parts = jnp.stack([p.reshape(dp_size, rows // dp_size, columns) for p in partials], axis=1)
    parts = lax.psum_scatter(parts, "dp", scatter_dimension=0, tiled=True)[0]
    return lax.psum_scatter(parts, "tensor", scatter_dimension=0, tiled=True)[0].astype(WIDE)


def general_plan(args, dp_size, tensor_size):
    (tokens, lengths, cotangent, ln1_gain, ln1_bias, w_qkv, b_qv, b_up, w_out, b_out, ln2_gain, ln2_bias, w_up, w_down, b_down) = args
    place = jnp.zeros((1,), jnp.int32)
    own, rows_own = pack_attention(False, place, w_qkv, w_out, b_qv, b_up, w_up, w_down)
    attn = gather_shards(own, dp_size)
    both = gather_shards(jnp.concatenate([w_up, w_down], axis=1), dp_size)
    rows = lax.all_gather(rows_own, "tensor", axis=0)
    shards = range(tensor_size)
    saved = []
    for k in shards:
        *kept_here, h1 = attend(place, lengths, tokens, (rows[k], attn[k]), (ln1_gain, ln1_bias))
        saved.append(kept_here)
    grads, up_sums, r = [], [], None
    for k in range(0, tensor_size, 2):
        first, last = k == 0, k + 2 == tensor_size
        ours = both[k : k + 2]
        operands = dict(g=cotangent, up=list(ours[:, :, : w_up.shape[1]]), down=list(ours[:, :, w_up.shape[1] :]))
        operands |= dict(rows=list(rows[k : k + 2]))
        vectors = {}
        if first:
            operands |= dict(x=tokens, mixed=[v[1] for v in saved], packed=list(attn))
            vectors = dict(out_bias=b_out, gain=ln2_gain, shift=ln2_bias, down_bias=b_down)
        else:
            operands |= dict(h=h2, out_in=r.out, e_in=r.e)
        if last:
            operands |= dict(middle=middle)
            vectors |= dict(gain=ln2_gain)
        r = feed(False, (False, False), first, last, place, operands, vectors)
        if first:
            middle, h2, g_sums = r.middle_out, r.h_out, r.g_sums
        grads += [r.keep[:768], r.keep[768:]]
        up_sums.append(r.sums)
    grad_feed = reduce_shards(grads, dp_size)
    grad_middle, branch, turn_sums = r.grad_middle, r.branch, r.turn_sums
    pieces, grads, qkv_sums = [], [], []
    for k in shards:
        piece, grad, sums = attend_back(False, place, lengths, attn[k], *saved[k], branch, h1)
        pieces.append(piece)
        grads.append(grad)
        qkv_sums.append(sums)
    grad_attn = reduce_shards(grads, dp_size)
    given = [pieces, [attn[k] for k in shards], tokens, grad_middle]
    half_grad, half_sums = finish(0, *given, ln1_gain)
    input_grad, small = finish(1, *given, ln1_gain, half_grad, [half_sums, turn_sums, g_sums] + up_sums + qkv_sums)
    by_depth = small[:6].reshape(6, dp_size, tensor_size, -1).transpose(1, 2, 0, 3).reshape(dp_size, tensor_size, -1)
    lines = []
    for k in shards:
        up, qkv = small[6 + k : 7 + k], small[10 + k : 11 + k]
        lines.append(jnp.concatenate([by_depth[:, k]] + bias_rows(qkv, up, dp_size), axis=1))
    small = jnp.stack(lines, axis=1).reshape(dp_size * tensor_size, -1)
    small = lax.psum_scatter(small, ("dp", "tensor"), scatter_dimension=0, tiled=True)[0]
    return r.out, input_grad, grad_feed, grad_attn, small


def solution(mesh):
    in_specs = (
        P(("dp", "tensor"), None),
        P("dp"),
        P(("dp", "tensor"), None),
        P(),
        P(),
        P(None, None, "tensor"),
        P(None, "tensor"),
        P("tensor", None),
        P(),
        P(),
        P(),
        P(None, "tensor"),
        P("tensor"),
        P("tensor", None),
        P(),
    )
    out_specs = (
        P(("dp", "tensor"), None),
        P(("dp", "tensor"), None),
        P(("dp", "tensor")),
        P(("dp", "tensor")),
        P(None, "dp", "tensor"),
        P(None, ("tensor", "dp")),
        P("tensor", "dp"),
        P(("dp", "tensor")),
        P(("dp", "tensor")),
        P(("dp", "tensor")),
        P("dp", "tensor"),
        P(("tensor", "dp")),
        P("tensor", "dp"),
        P(("dp", "tensor")),
    )
    return jax.shard_map(
        functools.partial(per_device, mesh.shape["dp"], mesh.shape["tensor"]), mesh=mesh, in_specs=in_specs, out_specs=out_specs, check_vma=False
    )
```

```python
import functools
from types import SimpleNamespace

import jax
import jax.numpy as jnp
from jax import lax
from jax.experimental import pallas as pl
from jax.experimental.pallas import tpu as pltpu
from jax.sharding import PartitionSpec as P

HD = 64
SEQ_LEN = 592
SCALE = HD**-0.5
EPSILON = 1e-06
MASKED = -1e30
LOW = jnp.bfloat16
WIDE = jnp.float32
HEADS = 3
NN = (((1,), (0,)), ((), ()))
NT = (((1,), (1,)), ((), ()))
TN = (((0,), (0,)), ((), ()))
PI_ROOT = (2.0 / 3.141592653589793) ** 0.5


def product(left, right, dims=NN):
    return lax.dot_general(left, right, dims, preferred_element_type=WIDE)


def three_parts(value):
    first = value.astype(LOW).astype(WIDE)
    rest = value - first
    second = rest.astype(LOW).astype(WIDE)
    return first, second, rest - second


def norm_parts(values):
    center = values - jnp.mean(values, axis=-1, keepdims=True)
    inverse = lax.rsqrt(jnp.mean(center * center, axis=-1, keepdims=True) + EPSILON)
    return center * inverse, inverse


def norm_back(grad, normed, inverse, gain):
    scaled = grad * gain
    return inverse * (
        scaled
        - jnp.mean(scaled, axis=-1, keepdims=True)
        - normed * jnp.mean(scaled * normed, axis=-1, keepdims=True)
    )


def call(kernel, name, outs, grid, in_specs, out_specs, scratch=(), scalars=0, aliases=None, flops=20_000_000_000, vmem=60):
    return pl.pallas_call(
        kernel,
        out_shape=outs,
        grid_spec=pltpu.PrefetchScalarGridSpec(
            num_scalar_prefetch=scalars,
            grid=grid,
            in_specs=in_specs,
            out_specs=out_specs,
            scratch_shapes=list(scratch),
        ),
        compiler_params=pltpu.CompilerParams(vmem_limit_bytes=vmem << 20),
        cost_estimate=pl.CostEstimate(flops=flops, bytes_accessed=1, transcendentals=0),
        input_output_aliases=aliases or {},
        name=name,
    )


def whole(shape):
    zeros = (0,) * len(shape)
    return pl.BlockSpec(shape, lambda *_: zeros)


def kept(shape, dtype=LOW):
    return jax.ShapeDtypeStruct(shape, dtype)


FAR = pl.BlockSpec(memory_space=pltpu.MemorySpace.HBM)
ANYWHERE = pl.BlockSpec(memory_space=pl.ANY)


EXTRA = 8
PIECE = 96 + EXTRA


def pack_kernel(relative, place_ref, qkv_ref, out_ref, qv_ref, up_bias_ref, *refs):
    if relative:
        up_ref, down_ref, packed_ref, rows_ref, piece_ref, feed_ref, sems = refs
        part = feed_ref.shape[0]
        source = pl.ds(pl.multiple_of(place_ref[0] * part, part), part)
        copies = [
            pltpu.make_async_copy(up_ref.at[source, :], feed_ref.at[:, 0:768], sems.at[0]),
            pltpu.make_async_copy(down_ref.at[source, :], feed_ref.at[:, 768:1536], sems.at[1]),
        ]
        for copy in copies:
            copy.start()
    else:
        packed_ref, rows_ref = refs
    for j in range(3):
        packed_ref[j * 128 : (j + 1) * 128, :] = qkv_ref[j, 0:128, :]
        packed_ref[384 + j * 64 : 448 + j * 64, :] = qkv_ref[j, 128:192, :]
    packed_ref[576:640, :] = out_ref[128:192, :]
    packed_ref[640:768, :] = out_ref[0:128, :]
    query, value, nothing = qv_ref[0:1, :], qv_ref[1:2, :], jnp.zeros((1, 128), WIDE)
    ends = [jnp.concatenate([v[:, 128:192], nothing[:, :64]], axis=1) for v in (query, value)]
    qv = jnp.concatenate([query[:, :128], nothing, value[:, :128], *ends, nothing], axis=1)
    rows = three_parts(qv) + three_parts(up_bias_ref[...][None])
    rows = jnp.concatenate(list(rows) + [jnp.zeros((2, 768), WIDE)], axis=0).astype(LOW)
    rows_ref[...] = rows
    if relative:
        start = pl.multiple_of(place_ref[0] * 96, 96)
        piece_ref[0:96, :] = packed_ref[pl.ds(start, 96), :]
        piece_ref[96:PIECE, :] = rows
        for copy in copies:
            copy.wait()


def pack_attention(relative, place, w_qkv, w_out, b_qv, b_up, w_up, w_down):
    depth = w_out.shape[1]
    outs = [kept((768, depth)), kept((EXTRA, depth))]
    operands = [w_qkv.transpose(0, 2, 1), w_out, b_qv, b_up]
    in_specs = [whole(v.shape) for v in operands]
    if relative:
        outs += [kept((PIECE, depth)), kept((96, 1536))]
        operands += [w_up, w_down]
        in_specs += [FAR] * 2
    return call(
        functools.partial(pack_kernel, relative),
        "pack",
        outs,
        (1,),
        in_specs,
        [whole(o.shape) for o in outs],
        [pltpu.SemaphoreType.DMA((2,))] if relative else [],
        scalars=1,
    )(place, *operands)


def bias_of(rows, first):
    parts = [rows[first + j : first + j + 1].astype(WIDE) for j in range(3)]
    return parts[0] + parts[1] + parts[2]


def unpack_attention(grads):
    q01, k01, v01, q2, k2, v2, o2, o01 = (
        grads[:, a:b]
        for a, b in ((0, 128), (128, 256), (256, 384), (384, 448), (448, 512), (512, 576), (576, 640), (640, 768))
    )
    stacked = [jnp.concatenate(pair, axis=1) for pair in ((q01, q2), (k01, k2), (v01, v2), (o01, o2))]
    return jnp.stack(stacked[:3]), stacked[3].T


def gelu_both(u):
    square = u * u
    t = jnp.tanh(PI_ROOT * u * (1.0 + 0.044715 * square))
    half = 0.5 * (1.0 + t)
    slope = half + (0.5 * PI_ROOT) * u * (1.0 - t * t) * (1.0 + (3 * 0.044715) * square)
    return u * half, slope


def spare_lane(upper):
    return 0 if upper else 64


def turn_halves(tile):
    return jnp.concatenate([tile[:, 64:128], tile[:, 0:64]], axis=1)


def head_tiles(proj, head):
    if head < 2:
        return proj[:, 0:128], proj[:, 128:256], proj[:, 256:384]
    both = proj[:, 384:512]
    return both, turn_halves(both), proj[:, 512:640]


class Copies:
    def __init__(self, sems):
        self.sems = sems
        self.used = 0
        self.saves = []

    def new(self, source, target):
        self.used += 1
        return pltpu.make_async_copy(source, target, self.sems.at[self.used - 1])

    def load(self, *pairs):
        copies = [self.new(*pair) for pair in pairs]
        for copy in copies:
            copy.start()
        return copies

    def save(self, source, target):
        self.saves += self.load((source, target))

    def finish(self):
        for copy in self.saves:
            copy.wait()


def wait_all(copies):
    for copy in copies:
        copy.wait()


def attend_kernel(stride, offset, place_ref, live_ref, *refs):
    if stride:
        h_ref, near_ref, far_ref, proj_ref, mixed_ref, log_ref, weights_ref, rows_ref, sems = refs

        @pl.when(pl.program_id(0) == 0)
        def _():
            copies = []
            for base, ref in ((0, near_ref), (1, far_ref)):
                for number in range(4):
                    start = pl.multiple_of((place_ref[0] ^ (2 * number + base)) * 96, 96)
                    source = ref.at[pl.ds(number * stride + offset, 96), :]
                    copies.append((source, weights_ref.at[pl.ds(start, 96), :]))
            copies.append((near_ref.at[pl.ds(offset + 96, EXTRA), :], rows_ref))
            copies = [pltpu.make_async_copy(*c, sems.at[j]) for j, c in enumerate(copies)]
            for copy in copies:
                copy.start()
            for copy in copies:
                copy.wait()

        h = h_ref[...]
    else:
        x_ref, gain_ref, shift_ref, rows_ref, weights_ref, proj_ref, mixed_ref, log_ref, h_ref = refs
        normed, _ = norm_parts(x_ref[...].astype(WIDE))
        h = (normed * gain_ref[...][None] + shift_ref[...][None]).astype(LOW)
        h_ref[...] = h
    live = live_ref[pl.program_id(0)]
    proj = (product(h, weights_ref[0:576, :], NT) + bias_of(rows_ref[...], 0)[:, :576]).astype(LOW)
    proj = jnp.concatenate([proj, jnp.zeros((SEQ_LEN, 64), LOW)], axis=1)
    proj_ref[...] = proj
    lane = lax.broadcasted_iota(jnp.int32, (1, 128), 1)
    row = lax.broadcasted_iota(jnp.int32, (SEQ_LEN, 1), 0)
    side = lax.broadcasted_iota(jnp.int32, (128, 1), 0)
    mask = jnp.where(row < live, 0.0, MASKED).astype(LOW)
    mixed = []
    for head in range(HEADS):
        upper = head == 1
        own = (lane >= 64) if upper else (lane < 64)
        spare = spare_lane(upper)
        query, keys, values = head_tiles(proj, head)
        query = query * jnp.asarray(SCALE, LOW)
        zero, one = jnp.zeros_like(query), jnp.ones_like(query)
        query = jnp.where(own, query, jnp.where(lane == spare, one, zero))
        keys = jnp.where(own, keys, jnp.where(lane == spare, mask, zero))
        values = jnp.where(own, values, jnp.where(lane == spare, one, zero))
        scores = product(keys, query, NT)
        highest = jnp.max(scores, axis=0, keepdims=True)
        weights = jnp.exp(scores - highest).astype(LOW)
        summed = product(values, weights, TN)
        spent = summed[spare : spare + 1, :]
        log_ref[head : head + 1, :] = highest + jnp.log(spent)
        mixed.append(summed * (1.0 / spent))
    first = jnp.where(side < 64, mixed[0], mixed[1]).astype(LOW).T
    third = jnp.where(side < 64, mixed[2], 0.0)
    third = jnp.concatenate([third[64:], third[:64]], axis=0).astype(LOW).T
    mixed_ref[...] = jnp.concatenate([third, first], axis=1)


def attend(place, lengths, rows_in, weights, norm=None, stride=0, offset=0):
    count, depth = rows_in.shape
    seqs = count // SEQ_LEN
    rows = lambda width: pl.BlockSpec((SEQ_LEN, width), lambda i, *_: (i, 0))
    logs = pl.BlockSpec((None, HEADS, SEQ_LEN), lambda i, *_: (i, 0, 0))
    outs = [kept((count, 640)), kept((count, 256)), kept((seqs, HEADS, SEQ_LEN), WIDE)]
    out_specs = [rows(640), rows(256), logs]
    in_specs, operands, scratch = [rows(depth)], [rows_in], []
    if stride:
        outs += [kept((768, depth)), kept((EXTRA, depth))]
        out_specs += [whole((768, depth)), whole((EXTRA, depth))]
        scratch = [pltpu.SemaphoreType.DMA((9,))]
        in_specs += [FAR, ANYWHERE]
    else:
        outs.append(kept((count, depth)))
        out_specs.append(rows(depth))
        in_specs += [whole((depth,))] * 2 + [whole((EXTRA, depth)), whole((768, depth))]
        operands += norm
    return call(
        functools.partial(attend_kernel, stride, offset),
        "attend",
        outs,
        (seqs,),
        in_specs,
        out_specs,
        scratch,
        scalars=2,
    )(place, lengths, *operands, *weights)


def attend_back_kernel(relative, place_ref, live_ref, weights_ref, proj_ref, mixed_ref, log_ref, branch_ref, h_ref, *refs):
    if relative:
        packed_ref, keep_ref, send_ref, sums_ref, *scratch = refs
    else:
        packed_ref, keep_ref, sums_ref, *scratch = refs
    weights_v, proj_v, branch_v, h_v, held_v, turned_v, sems = scratch
    copies = Copies(sems)
    tiles = [slice(a, a + SEQ_LEN) for a in range(0, h_v.shape[0], SEQ_LEN)]
    weights_loads = copies.load((weights_ref, weights_v))
    row_loads = [
        copies.load(
            (branch_ref.at[rows, :], branch_v.at[rows, :]),
            (proj_ref.at[rows, :], proj_v.at[rows, :]),
            (mixed_ref.at[rows, :], held_v.at[rows, 640:896]),
        )
        for rows in tiles
    ]
    h_loads = copies.load((h_ref, h_v))
    lane = lax.broadcasted_iota(jnp.int32, (1, 128), 1)
    row = lax.broadcasted_iota(jnp.int32, (SEQ_LEN, 1), 0)
    wait_all(weights_loads)
    sums = None
    for seq, rows in enumerate(tiles):
        wait_all(row_loads[seq])
        mask = jnp.where(row < live_ref[seq], 0.0, MASKED).astype(LOW)
        proj = proj_v[rows]
        mixed = held_v[rows, 640:896]
        grad_mixed = product(branch_v[rows], weights_v[512:768, :], NT).astype(LOW)
        totals = []
        for head in range(HEADS):
            upper = head == 1
            own = (lane >= 64) if upper else (lane < 64)
            spare = spare_lane(upper)
            query, keys, values = head_tiles(proj, head)
            if head < 2:
                grad, held = grad_mixed[:, 128:256], mixed[:, 128:256]
            else:
                grad, held = turn_halves(grad_mixed), turn_halves(mixed)
            query = query * jnp.asarray(SCALE, LOW)
            zero, one = jnp.zeros_like(query), jnp.ones_like(query)
            grad = jnp.where(own, grad, zero)
            wide_grad = grad.astype(WIDE)
            inner = jnp.sum(wide_grad * held.astype(WIDE), axis=-1, keepdims=True)
            parts = three_parts(-inner)
            shifted = wide_grad
            for place in range(3):
                shifted = jnp.where(lane == spare + place, parts[place], shifted)
            masked_query = jnp.where(own, query, jnp.where(lane == spare, one, zero))
            masked_keys = jnp.where(own, keys, jnp.where(lane == spare, mask, zero))
            spread_values = jnp.where(own, values, jnp.where((lane >= spare) & (lane < spare + 3), one, zero))
            probs = jnp.exp(product(masked_keys, masked_query, NT) - log_ref[seq, head : head + 1, :])
            centred = product(spread_values, shifted.astype(LOW), NT)
            grad_scores = (probs * centred).astype(LOW)
            parts = (
                (product(jnp.where(own, keys, zero), grad_scores, TN) * SCALE).astype(LOW).T,
                product(grad_scores, jnp.where(own, query, zero)).astype(LOW),
                product(probs.astype(LOW), grad).astype(LOW),
            )
            totals.append(parts)
        pair = [a + b for a, b in zip(totals[0], totals[1])]
        gq, gk, gv = totals[2]
        packed = jnp.concatenate(pair + [gq + turn_halves(gk), gv], axis=1)
        held_v[rows, 0:640] = packed
        copies.save(held_v.at[rows, 0:640], packed_ref.at[rows, :])
        part = jnp.sum(packed.astype(WIDE), axis=0, keepdims=True)
        sums = part if sums is None else sums + part
    sums_ref[...] = sums
    wait_all(h_loads)
    grads = product(h_v[...], held_v[:, 0:640], TN)
    outs = product(branch_v[...], held_v[:, 640:896], TN)
    full = jnp.concatenate([grads[:, :512], grads[:, 512:] + outs[:, :128], outs[:, 128:]], axis=1).astype(LOW)
    if relative:
        store_turned(place_ref, full, turned_v, slice(0, 768))
        copies.save(turned_v.at[384:768, :], send_ref)
        copies.save(turned_v.at[0:384, :], keep_ref)
    else:
        turned_v[...] = full
        copies.save(turned_v, keep_ref)
    copies.finish()


def store_turned(place_ref, values, target, columns):
    part = values.shape[0] // 8
    for block in range(8):
        other = place_ref[0] ^ block
        start = ((other & 1) * 4 + (other >> 1)) * part
        target[pl.ds(pl.multiple_of(start, part), part), columns] = values[block * part : (block + 1) * part]


def attend_back(relative, place, lengths, weights, proj, mixed, logs_in, branch, h):
    count, depth = branch.shape
    half = 384 if relative else 768
    outs = [kept((count, 640))] + [kept((half, 768))] * (2 if relative else 1) + [kept((1, 640), WIDE)]
    return call(
        functools.partial(attend_back_kernel, relative),
        "attend_back",
        outs,
        (1,),
        [FAR] * 3 + [whole(logs_in.shape)] + [FAR] * 2,
        [FAR] * (len(outs) - 1) + [whole((1, 640))],
        [
            pltpu.VMEM((768, depth), LOW),
            pltpu.VMEM((count, 640), LOW),
            pltpu.VMEM((count, depth), LOW),
            pltpu.VMEM((count, depth), LOW),
            pltpu.VMEM((count, 896), LOW),
            pltpu.VMEM((768, 768), LOW),
            pltpu.SemaphoreType.DMA((16,)),
        ],
        scalars=2,
        vmem=52,
    )(place, lengths, weights, proj, mixed, logs_in, branch, h)


def feed_kernel(tree, loaded, relative, first, last, place_ref, *refs):
    r = SimpleNamespace(**jax.tree.unflatten(tree, refs))
    count, depth = r.h_v.shape
    tiles = [slice(a, a + SEQ_LEN) for a in range(0, count, SEQ_LEN)]
    sems = r.sems
    used = [0]

    def copy(source, target):
        used[0] += 1
        return pltpu.make_async_copy(source, target, sems.at[used[0] - 1])

    shards = range(len(loaded))
    loads, ends = [], []
    for j, pieces in enumerate(loaded):
        both = r.both_v.at[j]
        mine = [copy(r.rows[j], r.rows_v.at[j])]
        if not pieces:
            mine += [copy(r.up[j], both.at[:, 0:768]), copy(r.down[j], both.at[:, 768:1536])]
        else:
            for base, ref in ((0, r.near[j]), (1, r.far[j])):
                for number in range(4):
                    start = pl.multiple_of((place_ref[0] ^ (2 * number + base)) * 96, 96)
                    mine.append(copy(ref.at[pl.ds(number * 96, 96), :], both.at[pl.ds(start, 96), :]))
        loads.append(mine)
    g_load = copy(r.g, r.g_v)

    def begin_save(*copies):
        for c in copies:
            c.start()
        ends.extend(copies)

    late = []
    if first:
        begin = [copy(r.x, r.x_v)]
        for k in range(4):
            begin.append(copy(r.mixed[k], r.mixed_v.at[k]))
            begin.append(copy(r.packed[k].at[512:768, :], r.out_v.at[k]))
    else:
        begin = [copy(r.h, r.h_v)]
        late = [copy(r.out_in, r.out_v), copy(r.e_in, r.e_v)]
    if last and not first:
        late.append(copy(r.middle, r.middle_v))
    for c in begin + loads[0] + [g_load] + late + [c for mine in loads[1:] for c in mine]:
        c.start()
    for c in begin:
        c.wait()
    if first:
        for rows in tiles:
            middle = r.x_v[rows].astype(WIDE) + r.out_bias[...][None]
            for k in range(4):
                middle = middle + product(r.mixed_v[k, rows, :], r.out_v[k])
            r.middle_v[rows] = middle
            normed, _ = norm_parts(middle)
            r.h_v[rows] = (normed * r.gain[...][None] + r.shift[...][None]).astype(LOW)
        begin_save(copy(r.middle_v, r.middle_out), copy(r.h_v, r.h_out))
    g_load.wait()
    h, g = r.h_v, r.g_v
    for j in shards:
        both, hidden_v, preact_v = r.both_v.at[j], r.hidden_v.at[j], r.preact_v.at[j]
        for c in loads[j]:
            c.wait()
        bias = bias_of(r.rows_v[j], 3)
        for a in range(0, 768, 768):
            b = a + 768
            sums = None
            for rows in tiles:
                preact = product(h[rows], both[:, a:b]) + bias[:, a:b]
                hidden, slope = gelu_both(preact)
                hidden_v[rows, a:b] = hidden.astype(LOW)
                grad = (product(g[rows], both[a:b, 768:1536], NT) * slope).astype(LOW)
                preact_v[rows, a:b] = grad
                part = jnp.sum(grad.astype(WIDE), axis=0, keepdims=True)
                sums = part if sums is None else sums + part
            r.sums[j : j + 1, a:b] = sums
    for c in late:
        c.wait()
    total_v, e_v = r.total_v, r.e_v
    for rows in tiles:
        total = r.middle_v[rows] + r.down_bias[...][None] if first else r.out_v[rows]
        e = None if first else e_v[rows]
        for j in shards:
            total = total + product(r.hidden_v[j, rows, :], r.both_v[j, :, 768:1536])
            term = product(r.preact_v[j, rows, :], r.both_v[j, :, 0:768], NT)
            e = term if e is None else e + term
        total_v[rows] = total.astype(total_v.dtype)
        e_v[rows] = e
    begin_save(copy(total_v, r.out))
    if not last:
        begin_save(copy(e_v, r.e))
    if last:
        totals = [0.0] * 3
        for rows in tiles:
            grad_h = e_v[rows]
            normed, inverse = norm_parts(r.middle_v[rows])
            grad = g[rows].astype(WIDE) + norm_back(grad_h, normed, inverse, r.gain[...][None])
            r.middle_v[rows] = grad
            r.branch_v[rows] = grad.astype(LOW)
            terms = (grad_h * normed, grad_h, grad)
            totals = [t + jnp.sum(v, axis=0, keepdims=True) for t, v in zip(totals, terms)]
        for number, total in enumerate(totals):
            r.turn_sums[number : number + 1, :] = total
        begin_save(copy(r.middle_v, r.grad_middle), copy(r.branch_v, r.branch))
    if first:
        r.g_sums[...] = jnp.sum(g[...].astype(WIDE), axis=0, keepdims=True)
    half = 384 if relative else 768
    for j in shards:
        turned = r.turned_v.at[j]
        for columns, left, right in ((slice(0, 768), h, r.preact_v), (slice(768, 1536), g, r.hidden_v)):
            grads = product(left[...], right[j], TN).astype(LOW)
            if relative:
                store_turned(place_ref, grads, turned, columns)
            else:
                turned[:, columns] = grads
        place = pl.ds(j * half, half)
        if relative:
            begin_save(copy(turned.at[384:768, :], r.send.at[place, :]))
        begin_save(copy(turned.at[0:half, :], r.keep.at[place, :]))
    for c in ends:
        c.wait()


def feed(relative, loaded, first, last, place, operands, vectors):
    count, depth = operands["g"].shape
    shards = len(loaded)
    half = 384 if relative else 768
    rows = (count, depth)
    big = dict(out=kept(rows, LOW if last else WIDE), keep=kept((shards * half, 1536)))
    if first:
        big |= dict(middle_out=kept(rows, WIDE), h_out=kept(rows))
    if last:
        big |= dict(grad_middle=kept(rows, WIDE), branch=kept(rows))
    else:
        big |= dict(e=kept(rows, WIDE))
    if relative:
        big |= dict(send=kept((shards * half, 1536)))
    small = dict(sums=kept((shards, 768), WIDE))
    if first:
        small |= dict(g_sums=kept((1, depth), WIDE))
    if last:
        small |= dict(turn_sums=kept((3, depth), WIDE))
    scratch = dict(
        h_v=pltpu.VMEM(rows, LOW),
        g_v=pltpu.VMEM(rows, LOW),
        hidden_v=pltpu.VMEM((shards, count, 768), LOW),
        preact_v=pltpu.VMEM((shards, count, 768), LOW),
        both_v=pltpu.VMEM((shards, depth, 1536), LOW),
        rows_v=pltpu.VMEM((shards, EXTRA, depth), LOW),
        turned_v=pltpu.VMEM((shards, 768, 1536), LOW),
        total_v=pltpu.VMEM(rows, LOW if last else WIDE),
        e_v=pltpu.VMEM(rows, WIDE),
        sems=pltpu.SemaphoreType.DMA((48,)),
    )
    if first:
        scratch |= dict(
            x_v=pltpu.VMEM(rows, LOW),
            mixed_v=pltpu.VMEM((4, count, 256), LOW),
            out_v=pltpu.VMEM((4, 256, depth), LOW),
        )
    else:
        scratch |= dict(out_v=pltpu.VMEM(rows, WIDE))
    if first or last:
        scratch |= dict(middle_v=pltpu.VMEM(rows, WIDE))
    if last:
        scratch |= dict(branch_v=pltpu.VMEM(rows, LOW))
    parts = [operands, vectors, big, small, scratch]
    flat = [jax.tree.flatten(part) for part in parts]
    numbers = iter(range(sum(len(leaves) for leaves, _ in flat)))
    order = {}
    for (leaves, tree) in flat:
        order |= jax.tree.unflatten(tree, [next(numbers) for _ in leaves])
    places, tree = jax.tree.flatten(order)

    def kernel(*refs):
        refs = refs[:1] + tuple(refs[1 + place] for place in places)
        feed_kernel(tree, loaded, relative, first, last, *refs)

    outs = flat[2][0] + flat[3][0]
    results = call(
        kernel,
        "feed",
        outs,
        (1,),
        [FAR] * len(flat[0][0]) + [whole(v.shape) for v in flat[1][0]],
        [FAR] * len(flat[2][0]) + [whole(o.shape) for o in flat[3][0]],
        flat[4][0],
        scalars=1,
    )(place, *flat[0][0], *flat[1][0])
    named = jax.tree.unflatten(flat[2][1], results[: len(big)]) | jax.tree.unflatten(flat[3][1], results[len(big) :])
    return SimpleNamespace(**named)


def finish_kernel(shards, joined, last, *refs):
    packed, weights = refs[:shards], refs[shards : 2 * shards]
    x_ref, grad_ref, gain_ref = refs[2 * shards : 2 * shards + 3]
    refs = refs[2 * shards + 3 :]
    if joined:
        refs = refs[1:]
    if last:
        before_ref, turn_ref, g_ref, *refs = refs
        ups, refs = refs[: shards // 2], refs[shards // 2 :]
        qkvs, refs = refs[:shards], refs[shards:]
    out_ref, sums_ref = refs
    grad_h = None
    for p, w in zip(packed, weights):
        term = product(p[...], w[...])
        grad_h = term if grad_h is None else grad_h + term
    normed, inverse = norm_parts(x_ref[...].astype(WIDE))
    out_ref[...] = (grad_ref[...] + norm_back(grad_h, normed, inverse, gain_ref[...][None])).astype(LOW)
    first = jnp.sum(grad_h * normed, axis=0, keepdims=True)
    second = jnp.sum(grad_h, axis=0, keepdims=True)
    if not last:
        sums_ref[0:1, :] = first
        sums_ref[1:2, :] = second
        return
    sums_ref[0:1, :] = first + before_ref[0:1, :]
    sums_ref[1:2, :] = second + before_ref[1:2, :]
    sums_ref[2:5, :] = turn_ref[...]
    sums_ref[5:6, :] = g_ref[...]
    for j, ref in enumerate(ups):
        sums_ref[6 + 2 * j : 8 + 2 * j, :] = ref[...]
    for j, ref in enumerate(qkvs):
        row = 6 + shards + j
        sums_ref[row : row + 1, 0:640] = ref[...]
        sums_ref[row : row + 1, 640:] = jnp.zeros_like(sums_ref[row : row + 1, 640:])
    sums_ref[6 + 2 * shards :, :] = jnp.zeros_like(sums_ref[6 + 2 * shards :, :])


def finish(tile, packed, weights, tokens, grad_middle, gain, joined=None, sums=()):
    count, depth = tokens.shape
    shards = len(packed)
    last = (tile + 1) * SEQ_LEN == count
    rows = lambda width: pl.BlockSpec((SEQ_LEN, width), lambda i: (tile, 0))
    operands = [*packed, *weights, tokens, grad_middle, gain]
    in_specs = [rows(640)] * shards + [pl.BlockSpec((640, depth), lambda i: (0, 0))] * shards
    in_specs += [rows(depth)] * 2 + [whole((depth,))]
    aliases = None
    if joined is not None:
        aliases = {len(operands): 0}
        operands.append(joined)
        in_specs.append(FAR)
    if last:
        operands += sums
        in_specs += [whole(v.shape) for v in sums]
    return call(
        functools.partial(finish_kernel, shards, joined is not None, last),
        "finish",
        (kept((count, depth)), kept((16 if last else 2, depth), WIDE)),
        (1,),
        in_specs,
        [rows(depth), whole((16 if last else 2, depth))],
        aliases=aliases,
    )(*operands)


def fold_kernel(pairs, plan, *refs):
    keeps, gots, refs = refs[:pairs], refs[pairs : 2 * pairs], refs[2 * pairs :]
    out_refs, refs = refs[: len(plan)], refs[len(plan) :]
    keep_vs, got_vs, sems = refs[:pairs], refs[pairs : 2 * pairs], refs[2 * pairs]
    work = []
    for out_ref, (pair, blocks) in zip(out_refs, plan):
        part = keep_vs[pair].shape[1]
        for place, block in enumerate(blocks):
            rows = pl.ds(block * part, part)
            keep_v, got_v = keep_vs[pair].at[block], got_vs[pair].at[block]
            sem = 3 * len(work)
            loads = [
                pltpu.make_async_copy(keeps[pair].at[rows, :], keep_v, sems.at[sem]),
                pltpu.make_async_copy(gots[pair].at[rows, :], got_v, sems.at[sem + 1]),
            ]
            end = pltpu.make_async_copy(keep_v, out_ref.at[pl.ds(place * part, part), :], sems.at[sem + 2])
            for copy in loads:
                copy.start()
            work.append((keep_v, got_v, loads, end))
    for keep_v, got_v, loads, end in work:
        for copy in loads:
            copy.wait()
        keep_v[...] = (keep_v[...].astype(WIDE) + got_v[...].astype(WIDE)).astype(LOW)
        end.start()
    for *_, end in work:
        end.wait()


def fold(pairs, plan, part=96):
    shapes = [(keep.shape[0] // part, part, keep.shape[1]) for keep, _ in pairs]
    count = sum(len(blocks) for _, blocks in plan)
    return call(
        functools.partial(fold_kernel, len(pairs), plan),
        "fold",
        [kept((len(blocks) * part, pairs[pair][0].shape[1])) for pair, blocks in plan],
        (1,),
        [FAR] * len(pairs) + [ANYWHERE] * len(pairs),
        [FAR] * len(plan),
        [pltpu.VMEM(shape, LOW) for shape in shapes] * 2 + [pltpu.SemaphoreType.DMA((3 * count,))],
        flops=1,
        vmem=24 if len(pairs) < 4 and sum(keep.size for keep, _ in pairs) > 1_000_000 else 60,
    )(*[keep for keep, _ in pairs], *[got for _, got in pairs])


def hop(value, mask, size=8):
    return lax.ppermute(value, "dp", [(i, i ^ mask) for i in range(size)])


def ring(value, shift, size=4):
    return lax.ppermute(value, "tensor", [(i, (i + shift) % size) for i in range(size)])


def together(*values):
    return lax.optimization_barrier(values)


def add_up(*parts):
    total = parts[0].astype(WIDE)
    for part in parts[1:]:
        total = total + part.astype(WIDE)
    return total


def bias_rows(qkv_sums, up_sums, parts):
    sums = qkv_sums[0]
    query = jnp.concatenate([sums[:128], sums[384:448]])
    value = jnp.concatenate([sums[256:384], sums[512:576]])
    return [v.reshape(parts, -1) for v in (query, value, up_sums)]


def closed(first):
    return [first, hop(first, 2), hop(first, 4), hop(first, 6)]


def joined_rows(parts):
    return jnp.concatenate(parts, axis=0)


MASK = {"x": 2, "y": 4}
SHIFTS = (0, 1, 3, 2)
OTHER = {"x": "y", "y": "x"}
FIRST = {"x": ((0, 2), (1, 3)), "y": ((0, 1), (2, 3))}


class Leaving:
    def __init__(self):
        self.live = []
        self.done = {}
        self.rings = []
        self.late = []

    def add(self, shards, keep, send):
        self.live.append((shards, 0, keep, hop(send, 1)))

    def step(self, *tied):
        arrays = [v for item in self.live for v in item[2:]]
        results = together(*tied, *arrays, *[self.done[name] for name in self.rings])
        tied, results = results[: len(tied)], results[len(tied) :]
        arrays, ended = results[: len(arrays)], results[len(arrays) :]
        self.done |= dict(zip(self.rings, ended))
        self.rings = []
        pairs = list(zip(arrays[0::2], arrays[1::2]))
        plan, follow = [], []
        for number, (shards, stage, *_) in enumerate(self.live):
            for place, shard in enumerate(shards):
                lists = [(0,), (1,)] if stage == 1 else [(0,)]
                if stage == 0:
                    lists = [tuple(4 * place + b for b in blocks) for blocks in FIRST[shard[1]]]
                follow.append((shard, stage, len(plan)))
                plan += [(number, blocks) for blocks in lists]
        held = [self.late.pop(0)] if self.late else []
        results = together(*tied, *[v for _, _, v in held], *fold(pairs, plan))
        tied, results = results[: len(tied)], results[len(tied) :]
        for (name, shift, _), value in zip(held, results):
            self.done[name] = ring(value, -shift)
            self.rings.append(name)
        results = results[len(held) :]
        self.live = []
        for shard, stage, place in follow:
            name, axis, shift = shard
            if stage < 2:
                mask = MASK[axis if stage == 0 else OTHER[axis]]
                self.live.append(((shard,), stage + 1, results[place], hop(results[place + 1], mask)))
            elif not shift:
                self.done[name] = results[place]
            elif name in (2, 7):
                self.late.append((name, shift, results[place]))
            else:
                self.done[name] = ring(results[place], -shift)
                self.rings.append(name)
        return tied


def direct_plan(args):
    (tokens, lengths, cotangent, ln1_gain, ln1_bias, w_qkv, b_qv, b_up, w_out, b_out, ln2_gain, ln2_bias, w_up, w_down, b_down) = args
    index = lax.axis_index("dp")
    place = index[None]
    own, rows_own, piece, feed_piece = pack_attention(True, place, w_qkv, w_out, b_qv, b_up, w_up, w_down)
    attn_at = {j: ring(piece, SHIFTS[j]) for j in (1, 2)}
    feed_at = {}

    packed, saved, rows = {0: own}, {}, {0: rows_own}
    *saved[0], h1 = attend(place, lengths, tokens, (rows_own, own), (ln1_gain, ln1_bias))
    h1, attn_at[1], attn_at[2], piece, feed_piece = together(h1, attn_at[1], attn_at[2], piece, feed_piece)
    near1 = joined_rows(closed(attn_at[1]))
    attn_at[3] = ring(piece, SHIFTS[3])
    feed_at[3] = ring(feed_piece, SHIFTS[3])
    near1, attn_at[2], attn_at[3], feed_piece = together(near1, attn_at[2], attn_at[3], feed_piece)
    far1 = hop(near1, 1)
    near2 = joined_rows(closed(attn_at[2]))
    near1, near2, attn_at[3], far1, feed_at[3], feed_piece, h1 = together(
        near1, near2, attn_at[3], far1, feed_at[3], feed_piece, h1
    )
    far2 = hop(near2, 1)
    close3 = closed(attn_at[3])
    feed_at[1] = ring(feed_piece, SHIFTS[1])
    *saved[1], packed[1], rows[1] = attend(place, lengths, h1, (near1, far1), None, PIECE, 0)
    h1, saved[1][0], far2, feed_at[1], feed_piece, *close3 = together(
        h1, saved[1][0], far2, feed_at[1], feed_piece, *close3
    )
    feed_at[2] = ring(feed_piece, SHIFTS[2])
    near3 = joined_rows(close3)
    near3, h1, feed_at[1] = together(near3, h1, feed_at[1])
    far3 = hop(near3, 1)
    feed1 = closed(feed_at[1])
    *saved[2], packed[2], rows[2] = attend(place, lengths, h1, (near2, far2), None, PIECE, 0)
    h1, saved[2][0], far3, feed_at[2], *feed1 = together(h1, saved[2][0], far3, feed_at[2], *feed1)
    feed_near1 = joined_rows(feed1)
    feed_near1, h1, feed_at[2] = together(feed_near1, h1, feed_at[2])
    feed_far1 = hop(feed_near1, 1)
    feed2 = closed(feed_at[2])
    *saved[3], packed[3], rows[3] = attend(place, lengths, h1, (near3, far3), None, PIECE, 0)
    saved[3][1], feed_far1, *feed2 = together(saved[3][1], feed_far1, *feed2)
    feed_near2 = joined_rows(feed2)
    feed_near2, feed_at[3], saved[3][1] = together(feed_near2, feed_at[3], saved[3][1])
    feed_far2 = hop(feed_near2, 1)
    feed3 = closed(feed_at[3])

    operands = dict(x=tokens, g=cotangent, up=[w_up], down=[w_down], rows=[rows[0], rows[1]])
    operands |= dict(near=[None, feed_near1], far=[None, feed_far1])
    operands |= dict(mixed=[saved[k][1] for k in range(4)], packed=[packed[k] for k in range(4)])
    vectors = dict(out_bias=b_out, gain=ln2_gain, shift=ln2_bias, down_bias=b_down)
    r = feed(True, (False, True), True, False, place, operands, vectors)
    middle, h2, g_sums, up_sums = r.middle_out, r.h_out, r.g_sums, [r.sums]
    h2, feed_far2, *feed3 = together(h2, feed_far2, *feed3)
    feed_near3 = joined_rows(feed3)
    feed_far3 = hop(feed_near3, 1)
    leaving = Leaving()
    leaving.add(((0, "x", 0), (1, "y", SHIFTS[1])), r.keep, r.send)
    operands = dict(h=h2, g=cotangent, out_in=r.out, e_in=r.e, middle=middle, rows=[rows[2], rows[3]])
    operands |= dict(near=[feed_near2, feed_near3], far=[feed_far2, feed_far3])
    r = feed(True, (True, True), False, True, place, operands, dict(gain=ln2_gain))
    block_output, grad_middle, branch, turn_sums = r.out, r.grad_middle, r.branch, r.turn_sums
    up_sums.append(r.sums)

    pieces, qkv_sums = {}, {}

    (branch,) = leaving.step(branch)
    leaving.add(((2, "x", SHIFTS[2]), (3, "y", SHIFTS[3])), r.keep, r.send)
    for k in (3, 2, 1, 0):
        pieces[k], keep, send, qkv_sums[k] = attend_back(
            True, place, lengths, packed[k], *saved[k], branch, h1
        )
        branch, pieces[k] = leaving.step(branch, pieces[k])
        leaving.add(((4 + k, "y" if k % 2 else "x", SHIFTS[k]),), keep, send)
    given = [[v[k] for k in range(4)] for v in (pieces, packed)] + [tokens, grad_middle]
    half_grad, half_sums = finish(0, *given, ln1_gain)
    half_grad, half_sums = leaving.step(half_grad, half_sums)
    grad_feed = add_up(*[leaving.done[k] for k in range(4)])
    line = [half_sums, turn_sums, g_sums] + up_sums + [qkv_sums[k] for k in range(4)]
    input_grad, small = finish(1, *given, ln1_gain, half_grad, line)
    input_grad, small = leaving.step(input_grad, small)
    small = small + hop(small, 1)
    leaving.step()
    small = add_up(small, hop(small, 2), hop(small, 4), hop(small, 6))
    others = [ring(small, -SHIFTS[k]) for k in (1, 2, 3)]
    grad_attn = add_up(*[leaving.done[4 + k] for k in range(4)])
    small = jnp.concatenate(
        [
            add_up(small[:6], *[o[:6] for o in others]),
            add_up(small[6:7], *[o[6 + k : 7 + k] for k, o in zip((1, 2, 3), others)]),
            add_up(small[10:11], *[o[10 + k : 11 + k] for k, o in zip((1, 2, 3), others)]),
        ]
    )
    share = tokens.shape[1] // 32
    by_depth = lax.dynamic_slice_in_dim(small[:6], (index * 4 + lax.axis_index("tensor")) * share, share, 1)
    rest = [lax.dynamic_index_in_dim(v, index, 0, keepdims=False) for v in bias_rows(small[7:8], small[6:7], 8)]
    return block_output, input_grad, grad_feed, grad_attn, jnp.concatenate([by_depth.reshape(-1)] + rest)


def per_device(dp_size, tensor_size, tokens, lengths, cotangent, ln1_gain, ln1_bias, w_qkv, b_qv, w_out, b_out, ln2_gain, ln2_bias, w_up, b_up, w_down, b_down):
    count, depth = tokens.shape
    seqs = count // SEQ_LEN
    lengths = lax.dynamic_slice_in_dim(lengths, lax.axis_index("tensor") * seqs, seqs, 0)
    args = (tokens, lengths, cotangent, ln1_gain, ln1_bias, w_qkv, b_qv, b_up, w_out, b_out, ln2_gain, ln2_bias, w_up, w_down, b_down)
    if (dp_size, tensor_size) == (8, 4):
        results = direct_plan(args)
    else:
        results = general_plan(args, dp_size, tensor_size)
    block_output, input_grad, grad_feed, grad_attn, small = results
    order = (0, 1, 4, 2, 3, 5)
    width = w_up.shape[1]
    grad_qkv, grad_out = unpack_attention(grad_attn)
    share = depth // (dp_size * tensor_size)
    vectors = small[: 6 * share].reshape(6, share)
    rest = small[6 * share :]
    own = w_qkv.shape[2] // dp_size
    return (
        block_output,
        input_grad,
        vectors[order[0]],
        vectors[order[1]],
        grad_qkv,
        rest[: 2 * own].reshape(2, own),
        grad_out,
        vectors[order[2]],
        vectors[order[3]],
        vectors[order[4]],
        grad_feed[:, :width],
        rest[2 * own :],
        grad_feed[:, width:].T,
        vectors[order[5]],
    )


def gather_shards(shard, dp_size):
    rows, columns = shard.shape
    part = rows // dp_size
    own = lax.dynamic_slice_in_dim(shard, lax.axis_index("dp") * part, part, 0)
    parts = lax.all_gather(own, ("dp", "tensor"), axis=0)
    parts = parts.reshape(dp_size, -1, part, columns).transpose(1, 0, 2, 3)
    return parts.reshape(-1, rows, columns)


def reduce_shards(partials, dp_size):
    rows, columns = partials[0].shape
    parts = jnp.stack([p.reshape(dp_size, rows // dp_size, columns) for p in partials], axis=1)
    parts = lax.psum_scatter(parts, "dp", scatter_dimension=0, tiled=True)[0]
    return lax.psum_scatter(parts, "tensor", scatter_dimension=0, tiled=True)[0].astype(WIDE)


def general_plan(args, dp_size, tensor_size):
    (tokens, lengths, cotangent, ln1_gain, ln1_bias, w_qkv, b_qv, b_up, w_out, b_out, ln2_gain, ln2_bias, w_up, w_down, b_down) = args
    place = jnp.zeros((1,), jnp.int32)
    own, rows_own = pack_attention(False, place, w_qkv, w_out, b_qv, b_up, w_up, w_down)
    attn = gather_shards(own, dp_size)
    both = gather_shards(jnp.concatenate([w_up, w_down], axis=1), dp_size)
    rows = lax.all_gather(rows_own, "tensor", axis=0)
    shards = range(tensor_size)
    saved = []
    for k in shards:
        *kept_here, h1 = attend(place, lengths, tokens, (rows[k], attn[k]), (ln1_gain, ln1_bias))
        saved.append(kept_here)
    grads, up_sums, r = [], [], None
    for k in range(0, tensor_size, 2):
        first, last = k == 0, k + 2 == tensor_size
        ours = both[k : k + 2]
        operands = dict(g=cotangent, up=list(ours[:, :, : w_up.shape[1]]), down=list(ours[:, :, w_up.shape[1] :]))
        operands |= dict(rows=list(rows[k : k + 2]))
        vectors = {}
        if first:
            operands |= dict(x=tokens, mixed=[v[1] for v in saved], packed=list(attn))
            vectors = dict(out_bias=b_out, gain=ln2_gain, shift=ln2_bias, down_bias=b_down)
        else:
            operands |= dict(h=h2, out_in=r.out, e_in=r.e)
        if last:
            operands |= dict(middle=middle)
            vectors |= dict(gain=ln2_gain)
        r = feed(False, (False, False), first, last, place, operands, vectors)
        if first:
            middle, h2, g_sums = r.middle_out, r.h_out, r.g_sums
        grads += [r.keep[:768], r.keep[768:]]
        up_sums.append(r.sums)
    grad_feed = reduce_shards(grads, dp_size)
    grad_middle, branch, turn_sums = r.grad_middle, r.branch, r.turn_sums
    pieces, grads, qkv_sums = [], [], []
    for k in shards:
        piece, grad, sums = attend_back(False, place, lengths, attn[k], *saved[k], branch, h1)
        pieces.append(piece)
        grads.append(grad)
        qkv_sums.append(sums)
    grad_attn = reduce_shards(grads, dp_size)
    given = [pieces, [attn[k] for k in shards], tokens, grad_middle]
    half_grad, half_sums = finish(0, *given, ln1_gain)
    input_grad, small = finish(1, *given, ln1_gain, half_grad, [half_sums, turn_sums, g_sums] + up_sums + qkv_sums)
    by_depth = small[:6].reshape(6, dp_size, tensor_size, -1).transpose(1, 2, 0, 3).reshape(dp_size, tensor_size, -1)
    lines = []
    for k in shards:
        up, qkv = small[6 + k : 7 + k], small[10 + k : 11 + k]
        lines.append(jnp.concatenate([by_depth[:, k]] + bias_rows(qkv, up, dp_size), axis=1))
    small = jnp.stack(lines, axis=1).reshape(dp_size * tensor_size, -1)
    small = lax.psum_scatter(small, ("dp", "tensor"), scatter_dimension=0, tiled=True)[0]
    return r.out, input_grad, grad_feed, grad_attn, small


def solution(mesh):
    in_specs = (
        P(("dp", "tensor"), None),
        P("dp"),
        P(("dp", "tensor"), None),
        P(),
        P(),
        P(None, None, "tensor"),
        P(None, "tensor"),
        P("tensor", None),
        P(),
        P(),
        P(),
        P(None, "tensor"),
        P("tensor"),
        P("tensor", None),
        P(),
    )
    out_specs = (
        P(("dp", "tensor"), None),
        P(("dp", "tensor"), None),
        P(("dp", "tensor")),
        P(("dp", "tensor")),
        P(None, "dp", "tensor"),
        P(None, ("tensor", "dp")),
        P("tensor", "dp"),
        P(("dp", "tensor")),
        P(("dp", "tensor")),
        P(("dp", "tensor")),
        P("dp", "tensor"),
        P(("tensor", "dp")),
        P("tensor", "dp"),
        P(("dp", "tensor")),
    )
    return jax.shard_map(
        functools.partial(per_device, mesh.shape["dp"], mesh.shape["tensor"]), mesh=mesh, in_specs=in_specs, out_specs=out_specs, check_vma=False
    )
```
